32 devices in a mesh: dp: 4 (over z), rows: 8 (over y, x, core).
Axes of the slice: x: 2, y: 2, z: 4, core: 2. Of those that a mesh axis runs over, the one named last changes fastest.
Arguments:
- inputs: bfloat16 [2, 8192, 9216], P(None, 'dp', 'rows'), may hold values from -21 to 21
- weights: bfloat16 [2, 9216, 4096], P(None, 'rows'), may hold values from -0.0625 to 0.0625
- bias: float32 [2, 4096], P(None, 'rows'), may hold values from -3 to 3
- stitch: float32 [2, 2, 4096], P(None, None, 'rows'), may hold values from 0.2 to 1
- cotangent: bfloat16 [2, 4096, 8192], P(None, 'rows', 'dp'), may hold values from -6 to 6
- valid: int32 [8192], P('dp'), may hold values from 0 to 1, as said below
- size_class: int32 [8192], P('dp'), may hold values from 195 to 227, as said below
Outputs:
- stitched: bfloat16 [2, 4096, 8192], P(None, 'rows', 'dp')
- grad_inputs: bfloat16 [2, 8192, 9216], P(None, 'dp', 'rows')
- grad_weights: float32 [2, 9216, 4096], P(None, 'rows', 'dp')
- grad_bias: float32 [2, 4096], P(None, 'rows')
- grad_stitch: float32 [2, 2, 4096], P(None, None, 'rows')
- rms_values: float32 [3], replicated
The draws below stay inside these ranges and needn't reach their ends.
Inputs may be any that keep to these rules, and one draw needn't show every extreme that they name: The first image of every aligned block of 2048 images is valid. `size_class`: each entry is 227 or 195.
All inputs are finite; a program needn't handle non-finite values.
Results may differ from the reference program's by a relative error of at most 0.006.
Values may be sent and summed in bfloat16 or wider, within the bound.
A program may use at most 256 MiB of HBM per device.

```python
import jax
import jax.numpy as jnp
from jax import lax

F = 9216
C = 4096
B_DEV = 2048
IMAGES = 8192


def draw_inputs(key, part):
    first = jax.random.fold_in(jax.random.fold_in(key, 11), 0)
    feature = jnp.arange(F, dtype=jnp.float32) / F
    image = jnp.arange(IMAGES, dtype=jnp.float32) / IMAGES
    ramp = jnp.sqrt((1.0 + 2.0 * feature)[None, None, :] * (1.0 + 2.0 * image)[None, :, None])
    base = jnp.clip(jax.random.normal(first, (2, IMAGES, F), jnp.float32), -6.0, 6.0)
    return (base * ramp).astype(jnp.bfloat16)


def draw_valid(key, part):
    picks = jax.random.randint(jax.random.fold_in(key, 23), (IMAGES,), 0, 4)
    leading = jnp.arange(IMAGES, dtype=jnp.int32) % B_DEV == 0
    return jnp.where(leading | (picks > 0), 1, 0).astype(jnp.int32)


def draw_size_class(key, part):
    picks = jax.random.randint(jax.random.fold_in(key, 37), (IMAGES,), 0, 8)
    return jnp.where(picks < 5, 227, 195).astype(jnp.int32)


def block_scale(key, extent, cuts, low, high):
    def one(position, parts):
        steps = jax.random.uniform(jax.random.fold_in(jax.random.fold_in(key, 6), position), (parts,), jnp.float32, low / len(cuts), high / len(cuts))
        return jnp.repeat(jnp.exp(steps), extent[position] // parts).reshape((-1,) + (1,) * (len(extent) - position - 1))

    loudness = one(*cuts[0])
    for cut in cuts[1:]:
        loudness = loudness * one(*cut)
    return loudness


def scatter_about(key, dims, scale, reach, pieces=(), kind=jnp.bfloat16):
    drawn = jax.random.normal(key, dims, jnp.float32) * scale
    if len(pieces) > 0:
        drawn = block_scale(key, dims, pieces, -0.22, 0.18) * drawn
    return jnp.clip(drawn, min=-reach, max=reach).astype(kind)


def setup_inputs(seed: int = 0) -> dict:
    key_list = jax.random.split(jax.random.key(seed), 8)
    return {
        "inputs": draw_inputs(jax.random.fold_in(key_list[7], 71), 0),
        "weights": scatter_about(key_list[1], (2, F, C), F ** -0.5, 0.0625, ((1, 8),)),
        "bias": scatter_about(key_list[2], (2, C), 0.5, 3.0, ((1, 8),), jnp.float32),
        "stitch": jnp.clip(0.2 + 0.8 * jax.random.uniform(key_list[3], (2, 2, C), jnp.float32) ** block_scale(key_list[3], (2, 2, C), ((2, 8),), -0.2, 0.2), 0.2, 1.0),
        "cotangent": scatter_about(key_list[4], (2, C, IMAGES), 1.0, 6.0, ((1, 8), (2, 4))),
        "valid": draw_valid(jax.random.fold_in(key_list[7], 71), 0),
        "size_class": draw_size_class(jax.random.fold_in(key_list[7], 71), 0),
    }


@jax.custom_vjp
def low(v):
    return lax.optimization_barrier(v.astype(jnp.bfloat16)).astype(jnp.float32)

@jax.custom_vjp
def low_back(v):
    return v

def low_keep(v):
    return (low(v), None)

def low_pass(kept, grad):
    return (grad,)

def back_keep(v):
    return (v, None)

def back_low(kept, grad):
    return (low(grad),)
low.defvjp(low_keep, low_pass)
low_back.defvjp(back_keep, back_low)

def keep_mask(size_class):
    place = jnp.arange(F, dtype=jnp.int32) % 36
    padded = (place // 6 == 5) | (place % 6 == 5)
    small = size_class == 195
    return jnp.where(small[:, None] & padded[None, :], 0.0, 1.0).astype(jnp.float32)

def forward(inputs, weights, bias, stitch, keep):
    used = low(inputs * keep[None])
    linear = jnp.einsum('tbf,tfc->tbc', used, low(weights), precision=lax.Precision.HIGHEST)
    pre = low_back(linear + bias[:, None, :])
    act = jax.nn.relu(pre)
    out = jnp.einsum('ijc,jbc->ibc', stitch, act, precision=lax.Precision.HIGHEST)
    return (out, (used, pre))

def reference(inputs, weights, bias, stitch, cotangent, valid, size_class):
    keep = keep_mask(size_class)
    source = inputs.astype(jnp.float32)
    matrix = weights.astype(jnp.float32)

    def layer(xx, ww, bb, aa):
        return forward(xx, ww, bb, aa, keep)
    out, pull, aux = jax.vjp(layer, source, matrix, bias, stitch, has_aux=True)
    used, pre = aux
    weight_valid = valid.astype(jnp.float32)
    upstream = jnp.transpose(cotangent.astype(jnp.float32), (0, 2, 1)) * weight_valid[None, :, None]
    grad_x, grad_w, grad_b, grad_a = pull(upstream)
    count = jnp.sum(weight_valid)
    mask_rows = weight_valid[None, :, None]
    square_x = jnp.sum(mask_rows * used * used)
    square_z = jnp.sum(mask_rows * pre * pre)
    square_y = jnp.sum(mask_rows * out * out)
    rms_values = jnp.sqrt(jnp.stack([square_x / (count * 2 * F), square_z / (count * 2 * C), square_y / (count * 2 * C)]))
    stitched = jnp.transpose(out, (0, 2, 1)).astype(jnp.bfloat16)
    return (stitched, grad_x.astype(jnp.bfloat16), grad_w, grad_b, grad_a, rms_values)
```

```python
import jax
import jax.numpy as jnp
from jax import lax
from jax.sharding import PartitionSpec as P

F = 9216
C = 4096
BLOCK = 128


def chain(own, up):
    size = lax.axis_size("dp")
    here = lax.axis_index("dp")
    got = None
    for step in range(size - 1):
        dest = size - 1 - step + here if up else step - (size - 1) + here
        dest = jnp.clip(dest, 0, size - 1)
        term = lax.dynamic_index_in_dim(own, dest, 0, keepdims=False)
        if got is not None:
            term = (term.astype(jnp.float32) + got.astype(jnp.float32)).astype(jnp.bfloat16)
        pairs = [(z, z + 1) for z in range(step + 1)]
        if not up:
            pairs = [(size - 1 - a, size - 1 - b) for a, b in pairs]
        got = lax.ppermute(term, "dp", pairs)
    return got


def per_device(inputs, weights, bias, stitch, cotangent, valid, size_class):
    rows = lax.axis_size("rows")
    size = lax.axis_size("dp")
    here = lax.axis_index("dp")
    width = inputs.shape[2]
    mine = bias.shape[1]
    step = min(BLOCK, mine)
    blocks = mine // step
    place = lax.iota(jnp.int32, width) % 36
    padded = (place // 6 == 5) | (place % 6 == 5)
    dropped = (size_class == 195)[:, None] & padded[None, :]
    used = jnp.where(dropped[None], jnp.zeros((), jnp.bfloat16), inputs)
    split = weights.reshape(2, width, rows, mine)
    weight_valid = valid.astype(jnp.float32)
    pieces, stitched, grad_bias, grad_stitch, square_pre, square_out = [], [], [], [], [], []
    grad_weights = []
    mats = [split[:, :, :, k * step : (k + 1) * step] for k in range(blocks)]
    sums = []
    for k in range(blocks):
        part = jnp.einsum("tfrc,tbf->rctb", mats[k], used, preferred_element_type=jnp.float32)
        sums.append(
            lax.psum_scatter(part.reshape(rows * step, 2, -1), "rows", scatter_dimension=0, tiled=True)
        )
    for k in range(blocks):
        cut = slice(k * step, (k + 1) * step)
        pre = jnp.transpose(sums[k], (1, 0, 2)) + bias[:, cut, None]
        act = jax.nn.relu(pre)
        mix = stitch[:, :, cut, None]
        out = jnp.sum(mix * act[None], axis=1)
        stitched.append(out.astype(jnp.bfloat16))
        upstream = cotangent[:, cut].astype(jnp.float32) * weight_valid[None, None, :]
        grad_act = jnp.sum(mix * upstream[:, None], axis=0)
        grad_pre = jnp.where(pre > 0, grad_act, 0.0).astype(jnp.bfloat16)
        grad_bias.append(jnp.sum(grad_pre.astype(jnp.float32), axis=2))
        grad_stitch.append(jnp.sum(upstream[:, None] * act[None], axis=3))
        square_pre.append(jnp.sum(weight_valid[None, None, :] * pre * pre))
        square_out.append(jnp.sum(weight_valid[None, None, :] * out * out))
        piece = lax.all_gather(grad_pre, "rows", axis=0)
        pieces.append(piece)
        block = jnp.einsum("tbf,rtcb->rtfc", used, piece, preferred_element_type=jnp.float32)
        block = block.reshape(size, rows // size, 2, width, step)
        own = block.astype(jnp.bfloat16)
        total = lax.dynamic_index_in_dim(block, here, 0, keepdims=False)
        total = total + chain(own, True).astype(jnp.float32) + chain(own, False).astype(jnp.float32)
        grad_weights.append(total)
    total_x = sum(
        jnp.einsum("rtcb,tfrc->tbf", pieces[k], mats[k], preferred_element_type=jnp.float32)
        for k in range(blocks)
    )
    grad_inputs = jnp.where(dropped[None], 0.0, total_x).astype(jnp.bfloat16)
    grad_weights = jnp.stack(grad_weights, axis=0)
    grad_weights = jnp.transpose(grad_weights, (2, 3, 1, 0, 4)).reshape(2, width, -1)
    stitched = jnp.concatenate(stitched, axis=1)
    grad_bias = jnp.concatenate(grad_bias, axis=1)
    grad_stitch = jnp.concatenate(grad_stitch, axis=2)
    used_wide = used.astype(jnp.float32)
    partial_value = jnp.stack(
        [
            jnp.sum(weight_valid[None, :, None] * used_wide * used_wide),
            sum(square_pre),
            sum(square_out),
            jnp.sum(weight_valid),
        ]
    )
    grad_bias, grad_stitch = lax.psum((grad_bias, grad_stitch), "dp")
    totals = lax.psum(partial_value, ("dp", "rows"))
    count = totals[3] / rows
    rms_values = jnp.sqrt(
        jnp.stack(
            [totals[0] / (count * 2 * F), totals[1] / (count * 2 * C), totals[2] / (count * 2 * C)]
        )
    )
    return (stitched, grad_inputs, grad_weights, grad_bias, grad_stitch, rms_values)


def solution(mesh):
    in_specs = (
        P(None, "dp", "rows"),
        P(None, "rows", None),
        P(None, "rows"),
        P(None, None, "rows"),
        P(None, "rows", "dp"),
        P("dp"),
        P("dp"),
    )
    out_specs = (
        P(None, "rows", "dp"),
        P(None, "dp", "rows"),
        P(None, "rows", "dp"),
        P(None, "rows"),
        P(None, None, "rows"),
        P(),
    )
    return jax.shard_map(
        per_device, mesh=mesh, in_specs=in_specs, out_specs=out_specs, check_vma=False
    )
```

```python
import functools

import jax
import jax.numpy as jnp
from jax import lax
from jax.experimental import pallas as pl
from jax.experimental.pallas import tpu as pltpu
from jax.sharding import PartitionSpec as P

F = 9216
C = 4096
BLOCK = 128
STEP = 64
IMAGES = 256
SLOTS = 4
F32 = jnp.float32
BF16 = jnp.bfloat16
MESH = pl.DeviceIdType.MESH


def fold(value):
    return sum(value[:, i : i + 128] for i in range(0, value.shape[1], 128))


def kernel(
    planes,
    x_hbm,
    wt_hbm,
    cot_hbm,
    small_ref,
    pad_ref,
    valid_ref,
    bias_ref,
    stitch_ref,
    st_hbm,
    g_hbm,
    gw_hbm,
    gb_ref,
    gs_ref,
    sq_ref,
    xb,
    wo,
    wp,
    part,
    r1,
    r2,
    gfull,
    cbuf,
    stbuf,
    zo,
    zsend,
    zrecv,
    zfin,
    x_sem,
    xs_sem,
    xr_sem,
    wo_sem,
    ws_sem,
    wr_sem,
    rs1_s,
    rs1_r,
    rs2_s,
    rs2_r,
    ag1_s,
    ag1_r,
    ag2_s,
    ag2_r,
    cx_s,
    cx_r,
    c_sem,
    st_sem,
    g_sem,
    z_s,
    z_r,
    zf_sem,
):
    towers, images, width = x_hbm.shape
    chunks = cot_hbm.shape[1]
    per_chunk = images // IMAGES
    total = chunks * per_chunk
    last = planes - 1

    z = lax.axis_index("dp")
    row = lax.axis_index("rows")
    y = row // 4
    x = (row // 2) % 2
    core = row % 2
    oy, ox, oc = 1 - y, 1 - x, 1 - core
    to_x = (z, y * 4 + ox * 2 + core)
    to_y = (z, oy * 4 + x * 2 + core)
    to_core = (z, y * 4 + x * 2 + oc)

    barrier = pltpu.get_barrier_semaphore()
    for there in (to_x, to_y, to_core):
        pl.semaphore_signal(barrier, inc=1, device_id=there, device_id_type=MESH)

    @pl.when(z > 0)
    def _():
        pl.semaphore_signal(barrier, inc=1, device_id=(z - 1, row), device_id_type=MESH)

    @pl.when(z < last)
    def _():
        pl.semaphore_signal(barrier, inc=1, device_id=(z + 1, row), device_id_type=MESH)

    def remote(src, dst, send, recv, there):
        return pltpu.make_async_remote_copy(
            src_ref=src, dst_ref=dst, send_sem=send, recv_sem=recv, device_id=there, device_id_type=MESH
        )

    def lanes(q):
        return pl.ds(pl.multiple_of((q % per_chunk) * IMAGES, IMAGES), IMAGES)

    def x_local(i):
        cut = pl.ds(i * IMAGES, IMAGES)
        return pltpu.make_async_copy(x_hbm.at[:, cut], xb.at[0, :, cut], x_sem.at[i])

    def x_remote(i):
        cut = pl.ds(i * IMAGES, IMAGES)
        return remote(x_hbm.at[:, cut], xb.at[1, :, cut], xs_sem.at[i], xr_sem.at[i], to_core)

    def w_local(k):
        return pltpu.make_async_copy(wt_hbm.at[:, :, core, k], wo.at[k % 2], wo_sem.at[k % 2])

    def w_remote(k):
        return remote(wt_hbm.at[:, :, oc, k], wp.at[k], ws_sem.at[k], wr_sem.at[k], to_core)

    def rs1(q):
        s = q % SLOTS
        return (
            remote(part.at[s, :, ox, 0], r1.at[s, 0], rs1_s.at[s, 0], rs1_r.at[s, 0], to_x),
            remote(part.at[s, oy, :, 1], r1.at[s, 1], rs1_s.at[s, 1], rs1_r.at[s, 1], to_y),
        )

    def rs2(q):
        s = q % SLOTS
        return (
            remote(part.at[s, oy, x, 0], r2.at[s, 0], rs2_s.at[s, 0], rs2_r.at[s, 0], to_y),
            remote(part.at[s, y, ox, 1], r2.at[s, 1], rs2_s.at[s, 1], rs2_r.at[s, 1], to_x),
        )

    def ag1(q):
        s, c, cut = q % SLOTS, (q // per_chunk) % 2, lanes(q)
        a = gfull.at[c, 0, y, x, core, :, cut]
        b = gfull.at[c, 1, y, x, core, :, cut]
        return (
            remote(a, a, ag1_s.at[s, 0], ag1_r.at[s, 0], to_x),
            remote(b, b, ag1_s.at[s, 1], ag1_r.at[s, 1], to_y),
        )

    def ag2(q):
        s, c, cut = q % SLOTS, (q // per_chunk) % 2, lanes(q)
        a = gfull.at[c, 0, y, :, core, :, cut]
        b = gfull.at[c, 1, :, x, core, :, cut]
        return (
            remote(a, a, ag2_s.at[s, 0], ag2_r.at[s, 0], to_y),
            remote(b, b, ag2_s.at[s, 1], ag2_r.at[s, 1], to_x),
        )

    def cx(q):
        s, c, cut = q % SLOTS, (q // per_chunk) % 2, lanes(q)
        a = gfull.at[c, :, :, :, core, :, cut]
        return (remote(a, a, cx_s.at[s], cx_r.at[s], to_core),)

    def cot_copy(q):
        s = q % SLOTS
        return pltpu.make_async_copy(cot_hbm.at[:, q // per_chunk, :, lanes(q)], cbuf.at[s], c_sem.at[s])

    def st_copy(q):
        s = q % SLOTS
        return pltpu.make_async_copy(stbuf.at[s], st_hbm.at[:, q // per_chunk, :, lanes(q)], st_sem.at[s])

    def g_copy(k):
        return pltpu.make_async_copy(gfull.at[k % 2], g_hbm.at[:, :, :, :, k], g_sem.at[k % 2])

    def gw_copy(k):
        return pltpu.make_async_copy(zfin, gw_hbm.at[:, :, k], zf_sem)

    def z_slot(k, j):
        return j if j < planes - 2 else j + k % 2

    def z_copy(k, j, way):
        n = z_slot(k, j)
        there = (z + 1, row) if way == 0 else (z - 1, row)
        return remote(zsend.at[way, j], zrecv.at[way, n], z_s.at[way, j], z_r.at[way, n], there)

    def start(copies):
        for c in copies:
            c.start()

    def wait_send(copies):
        for c in copies:
            c.wait_send()

    def wait_recv(copies):
        for c in copies:
            c.wait_recv()

    def stage(q, work, sends, *sent):
        @pl.when((q >= SLOTS) & (q < total + SLOTS))
        def _():
            for copies in sent:
                wait_send(copies(q - SLOTS))

        @pl.when((q >= 0) & (q < total))
        def _():
            work(q)
            start(sends(q))

    def forward(q):
        k, i, s = q // per_chunk, q % per_chunk, q % SLOTS

        cot_copy(q).start()

        @pl.when(i == 0)
        def _():
            w_local(k).wait()
            w_remote(k).wait_recv()

            @pl.when(k + 1 < chunks)
            def _():
                w_local(k + 1).start()

        cut = pl.ds(pl.multiple_of(i * IMAGES, IMAGES), IMAGES)

        @pl.when(k == 0)
        def _():
            x_local(i).wait()
            x_remote(i).wait_recv()
            keep = (1.0 - small_ref[cut, :] * pad_ref[...]).astype(BF16)
            for side in range(2):
                for t in range(towers):
                    xb[side, t, cut] = xb[side, t, cut] * keep

        for t in range(towers):
            out = lax.dot_general(
                wo[k % 2, t].reshape(4 * STEP, width),
                xb[0, t, cut],
                (((1,), (1,)), ((), ())),
                preferred_element_type=F32,
            ) + lax.dot_general(
                wp[k, t].reshape(4 * STEP, width),
                xb[1, t, cut],
                (((1,), (1,)), ((), ())),
                preferred_element_type=F32,
            )
            out = out.reshape(2, 2, STEP, IMAGES)
            for a in range(2):
                for b in range(2):
                    part[s, a, b, t] = out[a, b]

    def reduce(q):
        s = q % SLOTS
        wait_recv(rs1(q))
        part[s, oy, x, 0] = part[s, oy, x, 0] + r1[s, 0, oy]
        part[s, y, ox, 1] = part[s, y, ox, 1] + r1[s, 1, ox]
        part[s, y, x, 0] = part[s, y, x, 0] + r1[s, 0, y]
        part[s, y, x, 1] = part[s, y, x, 1] + r1[s, 1, x]

    def pointwise(q):
        k, i, s = q // per_chunk, q % per_chunk, q % SLOTS
        wait_recv(rs2(q))
        cot_copy(q).wait()

        @pl.when(q >= SLOTS)
        def _():
            st_copy(q - SLOTS).wait()

        valid = valid_ref[i]
        pre = [part[s, y, x, t] + r2[s, t] + bias_ref[t, k] for t in range(2)]
        act = [jnp.maximum(p, 0.0) for p in pre]
        up = [cbuf[s, t].astype(F32) * valid for t in range(2)]
        cut = lanes(q)
        for a in range(2):
            out = stitch_ref[a, 0, k] * act[0] + stitch_ref[a, 1, k] * act[1]
            stbuf[s, a] = out.astype(BF16)
            sq_ref[1] = sq_ref[1] + fold(out * out * valid)
            for b in range(2):
                gs_ref[k, a, b] = gs_ref[k, a, b] + fold(up[a] * act[b])
        for t in range(2):
            sq_ref[0] = sq_ref[0] + fold(pre[t] * pre[t] * valid)
            grad = stitch_ref[0, t, k] * up[0] + stitch_ref[1, t, k] * up[1]
            grad = jnp.where(pre[t] > 0, grad, 0.0).astype(BF16)
            gfull[k % 2, t, y, x, core, :, cut] = grad
            gb_ref[k, t] = gb_ref[k, t] + fold(grad.astype(F32))
        st_copy(q).start()

    def spread(q):
        wait_recv(ag1(q))

    def across(q):
        wait_recv(ag2(q))

    def terms(k, n):
        third = width // 3
        for t in range(towers):
            value = jnp.dot(
                gfull[k % 2, t].reshape(8 * STEP, images),
                xb[0, t, :, n * third : (n + 1) * third],
                preferred_element_type=F32,
            )
            value = value.astype(BF16).reshape(planes, 8 // planes, STEP, third)
            for d in range(planes):
                for e in range(8 // planes):
                    zo[t, d, e, :, n * third : (n + 1) * third] = value[d, e]

    halves = 8 // planes

    def chain(k, j):
        for way in range(2):
            near = z if way == 0 else last - z
            got = z_copy(k, j - 1, way) if j > 0 else None
            if j > 0:

                @pl.when((near >= 1) & (near <= j))
                def _():
                    got.wait_recv()

            if j <= planes - 2:

                @pl.when(near <= j)
                def _():
                    dest = last - j + z if way == 0 else j - last + z

                    @pl.when(k > 0)
                    def _():
                        z_copy(k - 1, j, way).wait_send()

                    if j > 0:
                        n = z_slot(k, j - 1)

                        @pl.when(near >= 1)
                        def _():
                            def add(i, carry):
                                t, e = i // halves, i % halves
                                value = zo[t, dest, e].astype(F32) + zrecv[way, n, t, e].astype(F32)
                                zsend[way, j, t, e] = value.astype(BF16)
                                return carry

                            lax.fori_loop(0, towers * halves, add, 0)

                        @pl.when(near == 0)
                        def _():
                            zsend[way, j] = zo[:, dest]

                    else:
                        zsend[way, j] = zo[:, dest]

        for way in range(2):
            near = z if way == 0 else last - z
            if j <= planes - 2:

                @pl.when(near <= j)
                def _():
                    z_copy(k, j, way).start()

        if j == planes - 2:

            @pl.when(k > 0)
            def _():
                gw_copy(k - 1).wait()

            def begin(i, carry):
                t, e = i // halves, i % halves
                zfin[t, e] = zo[t, z, e].astype(F32)
                return carry

            lax.fori_loop(0, towers * halves, begin, 0)
        if j == planes - 1:
            n = z_slot(k, j - 1)
            for way in range(2):
                near = z if way == 0 else last - z

                @pl.when(near >= 1)
                def _():
                    def more(i, carry):
                        t, e = i // halves, i % halves
                        zfin[t, e] = zfin[t, e] + zrecv[way, n, t, e].astype(F32)
                        return carry

                    lax.fori_loop(0, towers * halves, more, 0)

            gw_copy(k).start()

    x_local(0).start()
    w_local(0).start()
    for i in range(1, per_chunk):
        x_local(i).start()
    pl.semaphore_wait(barrier, 3 + jnp.minimum(z, 1) + jnp.minimum(last - z, 1))
    w_remote(0).start()

    def send_x(i, carry):
        x_remote(i).start()
        return carry

    lax.fori_loop(0, per_chunk, send_x, 0)

    def send_w(k, carry):
        w_remote(k).start()
        return carry

    lax.fori_loop(1, chunks, send_w, 0)
    gb_ref[...] = jnp.zeros_like(gb_ref)
    gs_ref[...] = jnp.zeros_like(gs_ref)
    sq_ref[...] = jnp.zeros_like(sq_ref)

    ready = per_chunk - 1 + 5
    space = per_chunk // 4
    offsets = [2 + j * space for j in range(planes)]

    def body(s, carry):
        stage(s, forward, rs1, rs1, rs2)
        stage(s - 1, reduce, rs2)
        stage(s - 2, pointwise, ag1, ag1)
        stage(s - 3, spread, ag2, ag2)
        stage(s - 4, across, cx, cx)

        @pl.when((s >= 5) & (s < total + 5))
        def _():
            wait_recv(cx(s - 5))

        @pl.when(s >= ready)
        def _():
            done = s - ready
            k = done // per_chunk
            at = done % per_chunk

            for n in range(3):

                @pl.when((at == n) & (k < chunks))
                def _():
                    if n == 0:
                        g_copy(k).start()
                    terms(k, n)
                    if n == 2:
                        g_copy(k).wait()

            for j, off in enumerate(offsets):

                @pl.when((done >= off) & ((done - off) % per_chunk == 0) & ((done - off) // per_chunk < chunks))
                def _():
                    chain((done - off) // per_chunk, j)

        return carry

    lax.fori_loop(0, total + ready - per_chunk + 1 + offsets[-1] + 1, body, 0)

    def drain(q, carry):
        st_copy(q).wait()
        return carry

    lax.fori_loop(total - SLOTS, total, drain, 0)

    def drain_x(i, carry):
        x_remote(i).wait_send()
        return carry

    lax.fori_loop(0, per_chunk, drain_x, 0)

    def drain_w(k, carry):
        w_remote(k).wait_send()
        return carry

    lax.fori_loop(0, chunks, drain_w, 0)
    gw_copy(chunks - 1).wait()
    for way in range(2):
        near = z if way == 0 else last - z
        for j in range(planes - 1):

            @pl.when(near <= j)
            def _():
                z_copy(chunks - 1, j, way).wait_send()


def fused(inputs, weights, bias, stitch, cotangent, valid, size_class):
    planes = lax.axis_size("dp")
    towers, images, width = inputs.shape
    mine = bias.shape[1]
    chunks = mine // STEP
    per_chunk = images // IMAGES
    halves = 8 // planes
    small = (size_class == 195).astype(F32)[:, None]
    place = lax.iota(jnp.int32, width) % 36
    padded = ((place // 6 == 5) | (place % 6 == 5)).astype(F32)[None, :]
    weight_valid = valid.astype(F32)
    turned = jnp.transpose(weights, (0, 2, 1)).reshape(towers, 4, 2, chunks, STEP, width)
    vmem = pl.BlockSpec(memory_space=pltpu.VMEM)
    hbm = pl.BlockSpec(memory_space=pl.ANY)
    dma = pltpu.SemaphoreType.DMA
    zslots = planes
    outs = pl.pallas_call(
        functools.partial(kernel, planes),
        out_shape=(
            jax.ShapeDtypeStruct((2, chunks, STEP, images), BF16),
            jax.ShapeDtypeStruct((2, 2, 2, 2, chunks, STEP, images), BF16),
            jax.ShapeDtypeStruct((2, halves, chunks, STEP, width), F32),
            jax.ShapeDtypeStruct((chunks, 2, STEP, 128), F32),
            jax.ShapeDtypeStruct((chunks, 2, 2, STEP, 128), F32),
            jax.ShapeDtypeStruct((2, STEP, 128), F32),
        ),
        in_specs=[hbm] * 3 + [vmem] * 5,
        out_specs=(hbm, hbm, hbm, vmem, vmem, vmem),
        scratch_shapes=[
            pltpu.VMEM((2, towers, images, width), BF16),
            pltpu.VMEM((2, towers, 4, STEP, width), BF16),
            pltpu.VMEM((chunks, towers, 4, STEP, width), BF16),
            pltpu.VMEM((SLOTS, 2, 2, towers, STEP, IMAGES), F32),
            pltpu.VMEM((SLOTS, 2, 2, STEP, IMAGES), F32),
            pltpu.VMEM((SLOTS, 2, STEP, IMAGES), F32),
            pltpu.VMEM((2, towers, 2, 2, 2, STEP, images), BF16),
            pltpu.VMEM((SLOTS, 2, STEP, IMAGES), BF16),
            pltpu.VMEM((SLOTS, 2, STEP, IMAGES), BF16),
            pltpu.VMEM((towers, planes, halves, STEP, width), BF16),
            pltpu.VMEM((2, planes - 1, towers, halves, STEP, width), BF16),
            pltpu.VMEM((2, zslots, towers, halves, STEP, width), BF16),
            pltpu.VMEM((towers, halves, STEP, width), F32),
            dma((per_chunk,)),
            dma((per_chunk,)),
            dma((per_chunk,)),
            dma((2,)),
            dma((chunks,)),
            dma((chunks,)),
            dma((SLOTS, 2)),
            dma((SLOTS, 2)),
            dma((SLOTS, 2)),
            dma((SLOTS, 2)),
            dma((SLOTS, 2)),
            dma((SLOTS, 2)),
            dma((SLOTS, 2)),
            dma((SLOTS, 2)),
            dma((SLOTS,)),
            dma((SLOTS,)),
            dma((SLOTS,)),
            dma((SLOTS,)),
            dma((2,)),
            dma((2, planes - 1)),
            dma((2, zslots)),
            dma,
        ],
        compiler_params=pltpu.CompilerParams(
            collective_id=0, has_side_effects=True, vmem_limit_bytes=67043328
        ),
        name="towers",
    )(
        inputs,
        turned,
        cotangent.reshape(2, chunks, STEP, images),
        small,
        padded,
        weight_valid.reshape(per_chunk, 1, IMAGES),
        bias.reshape(2, chunks, STEP, 1),
        stitch.reshape(2, 2, chunks, STEP, 1),
    )
    stitched, gathered, grad_weights, grad_bias, grad_stitch, squares = outs
    keep = 1.0 - small * padded
    gathered = gathered.reshape(towers, -1, images)
    total_x = jnp.einsum("tcb,tfc->tbf", gathered, weights, preferred_element_type=F32)
    grad_inputs = (total_x * keep[None]).astype(BF16)
    grad_weights = jnp.transpose(grad_weights.reshape(towers, -1, width), (0, 2, 1))
    used_wide = inputs.astype(F32) * keep[None]
    partial_value = jnp.stack(
        [
            jnp.sum(weight_valid[None, :, None] * used_wide * used_wide),
            jnp.sum(squares[0]),
            jnp.sum(squares[1]),
            jnp.sum(weight_valid),
        ]
    )
    grad_bias = jnp.transpose(jnp.sum(grad_bias, axis=3), (1, 0, 2)).reshape(2, mine)
    grad_stitch = jnp.transpose(jnp.sum(grad_stitch, axis=4), (1, 2, 0, 3)).reshape(2, 2, mine)
    grad_bias, grad_stitch = lax.psum((grad_bias, grad_stitch), "dp")
    totals = lax.psum(partial_value, ("dp", "rows"))
    return (
        stitched.reshape(2, mine, images),
        grad_inputs,
        grad_weights,
        grad_bias,
        grad_stitch,
        rms(totals),
    )


def rms(totals):
    count = totals[3] / lax.axis_size("rows")
    return jnp.sqrt(
        jnp.stack(
            [totals[0] / (count * 2 * F), totals[1] / (count * 2 * C), totals[2] / (count * 2 * C)]
        )
    )


def line_sum(own, up):
    size = lax.axis_size("dp")
    here = lax.axis_index("dp")
    got = None
    for step in range(size - 1):
        dest = size - 1 - step + here if up else step - (size - 1) + here
        dest = jnp.clip(dest, 0, size - 1)
        term = lax.dynamic_index_in_dim(own, dest, 0, keepdims=False)
        if got is not None:
            term = (term.astype(jnp.float32) + got.astype(jnp.float32)).astype(jnp.bfloat16)
        pairs = [(z, z + 1) for z in range(step + 1)]
        if not up:
            pairs = [(size - 1 - a, size - 1 - b) for a, b in pairs]
        got = lax.ppermute(term, "dp", pairs)
    return got


def plain(inputs, weights, bias, stitch, cotangent, valid, size_class):
    rows = lax.axis_size("rows")
    size = lax.axis_size("dp")
    here = lax.axis_index("dp")
    width = inputs.shape[2]
    mine = bias.shape[1]
    step = min(BLOCK, mine)
    blocks = mine // step
    place = lax.iota(jnp.int32, width) % 36
    padded = (place // 6 == 5) | (place % 6 == 5)
    dropped = (size_class == 195)[:, None] & padded[None, :]
    used = jnp.where(dropped[None], jnp.zeros((), jnp.bfloat16), inputs)
    split = weights.reshape(2, width, rows, mine)
    weight_valid = valid.astype(jnp.float32)
    pieces, stitched, grad_bias, grad_stitch, square_pre, square_out = [], [], [], [], [], []
    grad_weights = []
    mats = [split[:, :, :, k * step : (k + 1) * step] for k in range(blocks)]
    sums = []
    for k in range(blocks):
        part = jnp.einsum("tfrc,tbf->rctb", mats[k], used, preferred_element_type=jnp.float32)
        sums.append(
            lax.psum_scatter(part.reshape(rows * step, 2, -1), "rows", scatter_dimension=0, tiled=True)
        )
    for k in range(blocks):
        cut = slice(k * step, (k + 1) * step)
        pre = jnp.transpose(sums[k], (1, 0, 2)) + bias[:, cut, None]
        act = jax.nn.relu(pre)
        mix = stitch[:, :, cut, None]
        out = jnp.sum(mix * act[None], axis=1)
        stitched.append(out.astype(jnp.bfloat16))
        upstream = cotangent[:, cut].astype(jnp.float32) * weight_valid[None, None, :]
        grad_act = jnp.sum(mix * upstream[:, None], axis=0)
        grad_pre = jnp.where(pre > 0, grad_act, 0.0).astype(jnp.bfloat16)
        grad_bias.append(jnp.sum(grad_pre.astype(jnp.float32), axis=2))
        grad_stitch.append(jnp.sum(upstream[:, None] * act[None], axis=3))
        square_pre.append(jnp.sum(weight_valid[None, None, :] * pre * pre))
        square_out.append(jnp.sum(weight_valid[None, None, :] * out * out))
        piece = lax.all_gather(grad_pre, "rows", axis=0)
        pieces.append(piece)
        block = jnp.einsum("tbf,rtcb->rtfc", used, piece, preferred_element_type=jnp.float32)
        block = block.reshape(size, rows // size, 2, width, step)
        own = block.astype(jnp.bfloat16)
        total = lax.dynamic_index_in_dim(block, here, 0, keepdims=False)
        total = total + line_sum(own, True).astype(jnp.float32) + line_sum(own, False).astype(jnp.float32)
        grad_weights.append(total)
    total_x = sum(
        jnp.einsum("rtcb,tfrc->tbf", pieces[k], mats[k], preferred_element_type=jnp.float32)
        for k in range(blocks)
    )
    grad_inputs = jnp.where(dropped[None], 0.0, total_x).astype(jnp.bfloat16)
    grad_weights = jnp.stack(grad_weights, axis=0)
    grad_weights = jnp.transpose(grad_weights, (2, 3, 1, 0, 4)).reshape(2, width, -1)
    stitched = jnp.concatenate(stitched, axis=1)
    grad_bias = jnp.concatenate(grad_bias, axis=1)
    grad_stitch = jnp.concatenate(grad_stitch, axis=2)
    used_wide = used.astype(jnp.float32)
    partial_value = jnp.stack(
        [
            jnp.sum(weight_valid[None, :, None] * used_wide * used_wide),
            sum(square_pre),
            sum(square_out),
            jnp.sum(weight_valid),
        ]
    )
    grad_bias, grad_stitch = lax.psum((grad_bias, grad_stitch), "dp")
    totals = lax.psum(partial_value, ("dp", "rows"))
    return (stitched, grad_inputs, grad_weights, grad_bias, grad_stitch, rms(totals))


def small_plane(mesh):
    return mesh.shape["rows"] == 8 and mesh.shape["dp"] in (2, 4, 8)


def solution(mesh):
    in_specs = (
        P(None, "dp", "rows"),
        P(None, "rows", None),
        P(None, "rows"),
        P(None, None, "rows"),
        P(None, "rows", "dp"),
        P("dp"),
        P("dp"),
    )
    out_specs = (
        P(None, "rows", "dp"),
        P(None, "dp", "rows"),
        P(None, "rows", "dp"),
        P(None, "rows"),
        P(None, None, "rows"),
        P(),
    )
    return jax.shard_map(
        fused if small_plane(mesh) else plain, mesh=mesh, in_specs=in_specs, out_specs=out_specs, check_vma=False
    )
```

```python
import functools

import jax
import jax.numpy as jnp
from jax import lax
from jax.experimental import pallas as pl
from jax.experimental.pallas import tpu as pltpu
from jax.sharding import PartitionSpec as P

F = 9216
C = 4096
BLOCK = 128
STEP = 64
IMAGES = 256
SLOTS = 4
F32 = jnp.float32
BF16 = jnp.bfloat16
MESH = pl.DeviceIdType.MESH


def fold(value):
    return sum(value[:, i : i + 128] for i in range(0, value.shape[1], 128))


def lane_sums(value):
    ones = jnp.ones((8, 128), F32)
    return lax.dot_general(
        ones, value, (((1,), (1,)), ((), ())), precision=lax.Precision.HIGHEST, preferred_element_type=F32
    )


def kernel(
    planes,
    x_hbm,
    w_hbm,
    cot_hbm,
    image_ref,
    pad_row_ref,
    pad_col_ref,
    valid_ref,
    small_ref,
    mix_ref,
    st_hbm,
    gx_hbm,
    gw_hbm,
    stats_ref,
    g_hbm,
    acc_hbm,
    xb,
    raw,
    wt,
    part,
    r1,
    r2,
    gfull,
    cbuf,
    stbuf,
    zo,
    zsend,
    zrecv,
    zfin,
    gb_ref,
    gs_ref,
    sq_ref,
    usq_ref,
    wgx,
    gtile,
    acc,
    gout,
    scur,
    srecv,
    stats,
    x_sem,
    xs_sem,
    xr_sem,
    wo_sem,
    ws_sem,
    wr_sem,
    rs1_s,
    rs1_r,
    rs2_s,
    rs2_r,
    ag1_s,
    ag1_r,
    ag2_s,
    ag2_r,
    cx_s,
    cx_r,
    c_sem,
    st_sem,
    g_sem,
    z_s,
    z_r,
    zf_sem,
    z_free,
    wg_sem,
    gt_sem,
    ai_sem,
    ao_sem,
    go_sem,
    sc_s,
    sc_r,
    zs_s,
    zs_r,
):
    towers, images, width = x_hbm.shape
    chunks = cot_hbm.shape[1]
    pairs = chunks // 2
    mine = chunks * STEP
    per_chunk = images // IMAGES
    total = chunks * per_chunk
    tiles = towers * per_chunk
    last = planes - 1
    halves = 8 // planes

    z = lax.axis_index("dp")
    row = lax.axis_index("rows")
    y = row // 4
    x = (row // 2) % 2
    core = row % 2
    oy, ox, oc = 1 - y, 1 - x, 1 - core
    to_x = (z, y * 4 + ox * 2 + core)
    to_y = (z, oy * 4 + x * 2 + core)
    to_core = (z, y * 4 + x * 2 + oc)

    barrier = pltpu.get_barrier_semaphore()
    for there in (to_x, to_y, to_core):
        pl.semaphore_signal(barrier, inc=1, device_id=there, device_id_type=MESH)
    for off in range(1, planes):
        pl.semaphore_signal(barrier, inc=1, device_id=((z + off) % planes, row), device_id_type=MESH)

    def remote(src, dst, send, recv, there):
        return pltpu.make_async_remote_copy(
            src_ref=src, dst_ref=dst, send_sem=send, recv_sem=recv, device_id=there, device_id_type=MESH
        )

    def lanes(q):
        return pl.ds(pl.multiple_of((q % per_chunk) * IMAGES, IMAGES), IMAGES)

    def x_local(i):
        cut = pl.ds(i * IMAGES, IMAGES)
        return pltpu.make_async_copy(x_hbm.at[:, cut], xb.at[0, :, cut], x_sem.at[i])

    def x_remote(i):
        cut = pl.ds(i * IMAGES, IMAGES)
        return remote(x_hbm.at[:, cut], xb.at[1, :, cut], xs_sem.at[i], xr_sem.at[i], to_core)

    def w_lanes(owner, p):
        return pl.ds(pl.multiple_of(owner * mine + p * 2 * STEP, 2 * STEP), 2 * STEP)

    def w_local(p):
        return [
            pltpu.make_async_copy(w_hbm.at[:, :, w_lanes(c * 2 + core, p)], raw.at[0, :, c], wo_sem.at[c])
            for c in range(4)
        ]

    def w_remote(p):
        return [
            remote(
                w_hbm.at[:, :, w_lanes(c * 2 + oc, p)], raw.at[1, :, c], ws_sem.at[c], wr_sem.at[c], to_core
            )
            for c in range(4)
        ]

    def rs1(q):
        s = q % SLOTS
        return (
            remote(part.at[s, :, ox, 0], r1.at[s, 0], rs1_s.at[s, 0], rs1_r.at[s, 0], to_x),
            remote(part.at[s, oy, :, 1], r1.at[s, 1], rs1_s.at[s, 1], rs1_r.at[s, 1], to_y),
        )

    def rs2(q):
        s = q % SLOTS
        return (
            remote(part.at[s, oy, x, 0], r2.at[s, 0], rs2_s.at[s, 0], rs2_r.at[s, 0], to_y),
            remote(part.at[s, y, ox, 1], r2.at[s, 1], rs2_s.at[s, 1], rs2_r.at[s, 1], to_x),
        )

    def ag1(q):
        s, c, cut = q % SLOTS, (q // per_chunk) % 2, lanes(q)
        a = gfull.at[c, 0, y, x, core, :, cut]
        b = gfull.at[c, 1, y, x, core, :, cut]
        return (
            remote(a, a, ag1_s.at[s, 0], ag1_r.at[s, 0], to_x),
            remote(b, b, ag1_s.at[s, 1], ag1_r.at[s, 1], to_y),
        )

    def ag2(q):
        s, c, cut = q % SLOTS, (q // per_chunk) % 2, lanes(q)
        a = gfull.at[c, 0, y, :, core, :, cut]
        b = gfull.at[c, 1, :, x, core, :, cut]
        return (
            remote(a, a, ag2_s.at[s, 0], ag2_r.at[s, 0], to_y),
            remote(b, b, ag2_s.at[s, 1], ag2_r.at[s, 1], to_x),
        )

    def cx(q):
        s, c, cut = q % SLOTS, (q // per_chunk) % 2, lanes(q)
        a = gfull.at[c, :, :, :, core, :, cut]
        return (remote(a, a, cx_s.at[s], cx_r.at[s], to_core),)

    def cot_copy(q):
        s = q % SLOTS
        return pltpu.make_async_copy(cot_hbm.at[:, q // per_chunk, :, lanes(q)], cbuf.at[s], c_sem.at[s])

    def st_copy(q):
        s = q % SLOTS
        return pltpu.make_async_copy(stbuf.at[s], st_hbm.at[:, q // per_chunk, :, lanes(q)], st_sem.at[s])

    def g_copy(k):
        return pltpu.make_async_copy(gfull.at[k % 2], g_hbm.at[:, :, :, :, k], g_sem.at[k % 2])

    def gw_copy(k):
        return pltpu.make_async_copy(zfin, gw_hbm.at[:, :, k], zf_sem)

    def z_copy(k, j, way):
        there = (z + 1, row) if way == 0 else (z - 1, row)
        return remote(zsend.at[way, j], zrecv.at[way, j], z_s.at[way, j], z_r.at[way, j], there)

    def wg_load(g):
        p, t = g // tiles, (g % tiles) // per_chunk
        return [
            pltpu.make_async_copy(w_hbm.at[t, :, w_lanes(r, p)], wgx.at[:, pl.ds(r * 128, 128)], wg_sem.at[r])
            for r in range(8)
        ]

    def g_load(g):
        p, t, i = g // tiles, (g % tiles) // per_chunk, g % per_chunk
        return pltpu.make_async_copy(
            g_hbm.at[t, :, :, :, pl.ds(p * 2, 2), :, lanes(i)], gtile.at[g % 2], gt_sem.at[g % 2]
        )

    def acc_in(g):
        return pltpu.make_async_copy(acc_hbm.at[g % tiles], acc.at[g % 2], ai_sem.at[g % 2])

    def acc_out(g):
        return pltpu.make_async_copy(acc.at[g % 2], acc_hbm.at[g % tiles], ao_sem.at[g % 2])

    def gx_out(g):
        t = (g % tiles) // per_chunk
        return pltpu.make_async_copy(gout.at[g % 2], gx_hbm.at[t, :, lanes(g)], go_sem.at[g % 2])

    def in_plane(n):
        there = (to_x, to_y, to_core)[n]
        return remote(scur.at[n], srecv.at[n], sc_s.at[n], sc_r.at[n], there)

    def to_plane(off):
        there = ((z + off) % planes, row)
        return remote(stats.at[z], stats.at[z], zs_s.at[off - 1], zs_r.at[off - 1], there)

    def from_plane(off):
        there = ((z + off) % planes, row)
        held = stats.at[(z + planes - off) % planes]
        return remote(held, held, zs_s.at[off - 1], zs_r.at[off - 1], there)

    def start(copies):
        for c in copies:
            c.start()

    def wait_send(copies):
        for c in copies:
            c.wait_send()

    def wait_recv(copies):
        for c in copies:
            c.wait_recv()

    def stage(q, work, sends, *sent):
        @pl.when((q >= SLOTS) & (q < total + SLOTS))
        def _():
            for copies in sent:
                wait_send(copies(q - SLOTS))

        @pl.when((q >= 0) & (q < total))
        def _():
            work(q)
            start(sends(q))

    def turn(p):
        for c in w_local(p):
            c.wait()
        wait_recv(w_remote(p))

        def one(n, carry):
            side, t, c = n // 8, (n // 4) % 2, n % 4
            turned = jnp.transpose(raw[side, t, c])
            wt[side, t, 0, c] = turned[:STEP]
            wt[side, t, 1, c] = turned[STEP:]
            return carry

        lax.fori_loop(0, 16, one, 0)

        @pl.when(p + 1 < pairs)
        def _():
            start(w_local(p + 1))

    def forward(q):
        k, i, s = q // per_chunk, q % per_chunk, q % SLOTS
        p, h = k // 2, k % 2

        cot_copy(q).start()

        @pl.when((i == 0) & (h == 0))
        def _():
            turn(p)

        @pl.when((i == 0) & (h == 1))
        def _():
            wait_send(w_remote(p))

            @pl.when(p + 1 < pairs)
            def _():
                start(w_remote(p + 1))

        cut = pl.ds(pl.multiple_of(i * IMAGES, IMAGES), IMAGES)

        @pl.when(k == 0)
        def _():
            x_local(i).wait()
            x_remote(i).wait_recv()
            keep = (1.0 - image_ref[cut, 0:1] * pad_row_ref[...]).astype(BF16)
            valid = image_ref[cut, 1:2]
            for t in range(towers):
                used = xb[0, t, cut] * keep
                xb[0, t, cut] = used
                used = used.astype(F32)
                usq_ref[...] = usq_ref[...] + jnp.sum(used * used * valid, axis=0, keepdims=True)
                xb[1, t, cut] = xb[1, t, cut] * keep

        for t in range(towers):
            out = lax.dot_general(
                wt[0, t, h].reshape(4 * STEP, width),
                xb[0, t, cut],
                (((1,), (1,)), ((), ())),
                preferred_element_type=F32,
            ) + lax.dot_general(
                wt[1, t, h].reshape(4 * STEP, width),
                xb[1, t, cut],
                (((1,), (1,)), ((), ())),
                preferred_element_type=F32,
            )
            out = out.reshape(2, 2, STEP, IMAGES)
            for a in range(2):
                for b in range(2):
                    part[s, a, b, t] = out[a, b]

    def reduce(q):
        s = q % SLOTS
        wait_recv(rs1(q))
        part[s, oy, x, 0] = part[s, oy, x, 0] + r1[s, 0, oy]
        part[s, y, ox, 1] = part[s, y, ox, 1] + r1[s, 1, ox]
        part[s, y, x, 0] = part[s, y, x, 0] + r1[s, 0, y]
        part[s, y, x, 1] = part[s, y, x, 1] + r1[s, 1, x]

    def pointwise(q):
        k, i, s = q // per_chunk, q % per_chunk, q % SLOTS
        wait_recv(rs2(q))
        cot_copy(q).wait()

        @pl.when(q >= SLOTS)
        def _():
            st_copy(q - SLOTS).wait()

        valid = valid_ref[i]
        mix = mix_ref[k]
        bias = [mix[:, t : t + 1] for t in range(2)]
        stitch = [[mix[:, 2 + 2 * a + b : 3 + 2 * a + b] for b in range(2)] for a in range(2)]
        pre = [part[s, y, x, t] + r2[s, t] + bias[t] for t in range(2)]
        act = [jnp.maximum(p, 0.0) for p in pre]
        up = [cbuf[s, t].astype(F32) * valid for t in range(2)]
        cut = lanes(q)
        for a in range(2):
            out = stitch[a][0] * act[0] + stitch[a][1] * act[1]
            stbuf[s, a] = out.astype(BF16)
            sq_ref[1] = sq_ref[1] + fold(out * out * valid)
            for b in range(2):
                gs_ref[k, a, b] = gs_ref[k, a, b] + fold(up[a] * act[b])
        for t in range(2):
            sq_ref[0] = sq_ref[0] + fold(pre[t] * pre[t] * valid)
            grad = stitch[0][t] * up[0] + stitch[1][t] * up[1]
            grad = jnp.where(pre[t] > 0, grad, 0.0).astype(BF16)
            gfull[k % 2, t, y, x, core, :, cut] = grad
            gb_ref[k, t] = gb_ref[k, t] + fold(grad.astype(F32))
        st_copy(q).start()

    def spread(q):
        wait_recv(ag1(q))

    def across(q):
        wait_recv(ag2(q))

    def terms(k, n):
        third = width // 3
        for t in range(towers):
            value = jnp.dot(
                gfull[k % 2, t].reshape(8 * STEP, images),
                xb[0, t, :, n * third : (n + 1) * third],
                preferred_element_type=F32,
            )
            value = value.astype(BF16).reshape(planes, halves, STEP, third)
            for d in range(planes):
                for e in range(halves):
                    zo[t, d, e, :, n * third : (n + 1) * third] = value[d, e]

    def chain(k, j):
        if j == planes - 2:

            @pl.when(k > 0)
            def _():
                gw_copy(k - 1).wait()

            def begin(i, carry):
                t, e = i // halves, i % halves
                zfin[t, e] = zo[t, z, e].astype(F32)
                return carry

            lax.fori_loop(0, towers * halves, begin, 0)
        for way in range(2):
            near = z if way == 0 else last - z
            source = (z - 1, row) if way == 0 else (z + 1, row)

            def freed():
                @pl.when(k + 1 < chunks)
                def _():
                    pl.semaphore_signal(
                        z_free.at[way, j - 1], inc=1, device_id=source, device_id_type=MESH
                    )

            if j <= planes - 2:

                @pl.when(near <= j)
                def _():
                    dest = last - j + z if way == 0 else j - last + z

                    @pl.when(k > 0)
                    def _():
                        z_copy(k - 1, j, way).wait_send()

                    if j > 0:

                        @pl.when(near >= 1)
                        def _():
                            z_copy(k, j - 1, way).wait_recv()

                            def add(i, carry):
                                t, e = i // halves, i % halves
                                value = zo[t, dest, e].astype(F32) + zrecv[way, j - 1, t, e].astype(F32)
                                zsend[way, j, t, e] = value.astype(BF16)
                                return carry

                            lax.fori_loop(0, towers * halves, add, 0)
                            freed()

                        @pl.when(near == 0)
                        def _():
                            zsend[way, j] = zo[:, dest]

                    else:
                        zsend[way, j] = zo[:, dest]

                    @pl.when(k > 0)
                    def _():
                        pl.semaphore_wait(z_free.at[way, j], 1)

                    z_copy(k, j, way).start()

            else:

                @pl.when(near >= 1)
                def _():
                    z_copy(k, j - 1, way).wait_recv()

                    def more(i, carry):
                        t, e = i // halves, i % halves
                        zfin[t, e] = zfin[t, e] + zrecv[way, j - 1, t, e].astype(F32)
                        return carry

                    lax.fori_loop(0, towers * halves, more, 0)
                    freed()

        if j == planes - 1:
            gw_copy(k).start()

    def prepare(g):
        g_load(g).start()

        @pl.when(g % per_chunk == 0)
        def _():
            start(wg_load(g))

        @pl.when((g >= 2) & (g - 2 < (pairs - 1) * tiles))
        def _():
            acc_out(g - 2).wait()

        @pl.when(g >= tiles)
        def _():
            acc_in(g).start()

    def tile(g):
        g_load(g).wait()

        @pl.when(g % per_chunk == 0)
        def _():
            for c in wg_load(g):
                c.wait()

        value = jnp.dot(
            wgx[...], gtile[g % 2].reshape(16 * STEP, IMAGES), preferred_element_type=F32
        )

        @pl.when(g < tiles)
        def _():
            acc[g % 2] = value

        @pl.when(g >= tiles)
        def _():
            acc_in(g).wait()
            acc[g % 2] = acc[g % 2] + value

        @pl.when(g < (pairs - 1) * tiles)
        def _():
            acc_out(g).start()

        @pl.when(g >= (pairs - 1) * tiles)
        def _():
            @pl.when(g >= (pairs - 1) * tiles + 2)
            def _():
                gx_out(g - 2).wait()

            keep = 1.0 - pad_col_ref[...] * small_ref[g % per_chunk]
            gout[g % 2] = (acc[g % 2] * keep).astype(BF16)
            gx_out(g).start()

    def sums(n):
        if n == 0:
            scur[0] = jnp.zeros_like(scur[0])
            scur[0, 0:1] = fold(usq_ref[...])
            scur[0, 1:2] = jnp.sum(sq_ref[0], axis=0, keepdims=True)
            scur[0, 2:3] = jnp.sum(sq_ref[1], axis=0, keepdims=True)
            scur[0, 3:4] = fold(sum(valid_ref[i] for i in range(per_chunk)))
            for k in range(chunks):
                at = k * 6 * STEP
                stats[z, :, at : at + 2 * STEP] = lane_sums(gb_ref[k].reshape(2 * STEP, 128))
                stats[z, :, at + 2 * STEP : at + 6 * STEP] = lane_sums(gs_ref[k].reshape(4 * STEP, 128))
        else:
            in_plane(n - 1).wait()
            value = scur[n - 1] + srecv[n - 1]
            if n < 3:
                scur[n] = value
            else:
                stats[z, :, chunks * 6 * STEP :] = value
        if n < 3:
            in_plane(n).start()
        else:
            for off in range(1, planes):
                to_plane(off).start()

    start(w_local(0))
    for i in range(per_chunk):
        x_local(i).start()
    pl.semaphore_wait(barrier, 2 + planes)
    start(w_remote(0))

    def send_x(i, carry):
        x_remote(i).start()
        return carry

    lax.fori_loop(0, per_chunk, send_x, 0)
    gb_ref[...] = jnp.zeros_like(gb_ref)
    gs_ref[...] = jnp.zeros_like(gs_ref)
    sq_ref[...] = jnp.zeros_like(sq_ref)
    usq_ref[...] = jnp.zeros_like(usq_ref)

    ready = per_chunk - 1 + 5
    offsets = [2 + 3 * j for j in range(planes)]
    ends = [2 + 5 * j for j in range(planes)]
    first = per_chunk + 3

    def body(s, carry):
        stage(s, forward, rs1, rs1, rs2)
        stage(s - 1, reduce, rs2)
        stage(s - 2, pointwise, ag1, ag1)
        stage(s - 3, spread, ag2, ag2)
        stage(s - 4, across, cx, cx)

        @pl.when((s >= 5) & (s < total + 5))
        def _():
            wait_recv(cx(s - 5))

        for n in range(4):

            @pl.when(s == total + 2 + n)
            def _():
                sums(n)

        @pl.when(s >= ready)
        def _():
            done = s - ready
            k = done // per_chunk
            at = done % per_chunk

            def step(j):
                since = done - offsets[j]
                usual = (since >= 0) & (since % per_chunk == 0) & (since // per_chunk < chunks - 1)
                final = done == (chunks - 1) * per_chunk + ends[j]

                @pl.when(usual | final)
                def _():
                    chain(jnp.where(final, chunks - 1, since // per_chunk), j)

            for j in range(1, planes):
                step(j)
            for n in range(3):

                @pl.when((at == n) & (k < chunks))
                def _():
                    if n == 0:
                        g_copy(k).start()
                    terms(k, n)
                    if n == 2:
                        g_copy(k).wait()

            step(0)
            g = done - first

            @pl.when((g >= 0) & (g < pairs * tiles))
            def _():
                tile(g)

            @pl.when((g >= -1) & (g < pairs * tiles - 1))
            def _():
                prepare(g + 1)

        return carry

    lax.fori_loop(0, ready + max((chunks - 1) * per_chunk + ends[-1], first + pairs * tiles - 1) + 1, body, 0)

    def drain(q, carry):
        st_copy(q).wait()
        return carry

    lax.fori_loop(total - SLOTS, total, drain, 0)

    def drain_x(i, carry):
        x_remote(i).wait_send()
        return carry

    lax.fori_loop(0, per_chunk, drain_x, 0)
    for g in (pairs * tiles - 2, pairs * tiles - 1):
        gx_out(g).wait()
    gw_copy(chunks - 1).wait()
    for way in range(2):
        near = z if way == 0 else last - z
        for j in range(planes - 1):

            @pl.when(near <= j)
            def _():
                z_copy(chunks - 1, j, way).wait_send()

    for off in range(1, planes):
        to_plane(off).wait_send()
        from_plane(off).wait_recv()
    stats_ref[...] = sum(stats[d] for d in range(planes))


def fused(inputs, weights, bias, stitch, cotangent, valid, size_class):
    planes = lax.axis_size("dp")
    towers, images, width = inputs.shape
    mine = bias.shape[1]
    chunks = mine // STEP
    per_chunk = images // IMAGES
    halves = 8 // planes
    tiles = towers * per_chunk
    small = (size_class == 195).astype(F32)
    place = lax.iota(jnp.int32, width) % 36
    padded = ((place // 6 == 5) | (place % 6 == 5)).astype(F32)
    weight_valid = valid.astype(F32)
    mix = jnp.concatenate([bias, stitch.reshape(4, mine)], axis=0).reshape(6, chunks, STEP)
    many = chunks * 6 * STEP + 128
    vmem = pl.BlockSpec(memory_space=pltpu.VMEM)
    hbm = pl.BlockSpec(memory_space=pl.ANY)
    dma = pltpu.SemaphoreType.DMA
    stitched, grad_inputs, grad_weights, stats, _, _ = pl.pallas_call(
        functools.partial(kernel, planes),
        out_shape=(
            jax.ShapeDtypeStruct((2, chunks, STEP, images), BF16),
            jax.ShapeDtypeStruct((towers, width, images), BF16),
            jax.ShapeDtypeStruct((2, halves, chunks, STEP, width), F32),
            jax.ShapeDtypeStruct((8, many), F32),
            jax.ShapeDtypeStruct((2, 2, 2, 2, chunks, STEP, images), BF16),
            jax.ShapeDtypeStruct((tiles, width, IMAGES), F32),
        ),
        in_specs=[hbm] * 3 + [vmem] * 6,
        out_specs=(hbm, hbm, hbm, vmem, hbm, hbm),
        scratch_shapes=[
            pltpu.VMEM((2, towers, images, width), BF16),
            pltpu.VMEM((2, towers, 4, width, 2 * STEP), BF16),
            pltpu.VMEM((2, towers, 2, 4, STEP, width), BF16),
            pltpu.VMEM((SLOTS, 2, 2, towers, STEP, IMAGES), F32),
            pltpu.VMEM((SLOTS, 2, 2, STEP, IMAGES), F32),
            pltpu.VMEM((SLOTS, 2, STEP, IMAGES), F32),
            pltpu.VMEM((2, towers, 2, 2, 2, STEP, images), BF16),
            pltpu.VMEM((SLOTS, 2, STEP, IMAGES), BF16),
            pltpu.VMEM((SLOTS, 2, STEP, IMAGES), BF16),
            pltpu.VMEM((towers, planes, halves, STEP, width), BF16),
            pltpu.VMEM((2, planes - 1, towers, halves, STEP, width), BF16),
            pltpu.VMEM((2, planes - 1, towers, halves, STEP, width), BF16),
            pltpu.VMEM((towers, halves, STEP, width), F32),
            pltpu.VMEM((chunks, 2, STEP, 128), F32),
            pltpu.VMEM((chunks, 2, 2, STEP, 128), F32),
            pltpu.VMEM((2, STEP, 128), F32),
            pltpu.VMEM((1, width), F32),
            pltpu.VMEM((width, 16 * STEP), BF16),
            pltpu.VMEM((2, 2, 2, 2, 2, STEP, IMAGES), BF16),
            pltpu.VMEM((2, width, IMAGES), F32),
            pltpu.VMEM((2, width, IMAGES), BF16),
            pltpu.VMEM((3, 8, 128), F32),
            pltpu.VMEM((3, 8, 128), F32),
            pltpu.VMEM((planes, 8, many), F32),
            dma((per_chunk,)),
            dma((per_chunk,)),
            dma((per_chunk,)),
            dma((4,)),
            dma((4,)),
            dma((4,)),
            dma((SLOTS, 2)),
            dma((SLOTS, 2)),
            dma((SLOTS, 2)),
            dma((SLOTS, 2)),
            dma((SLOTS, 2)),
            dma((SLOTS, 2)),
            dma((SLOTS, 2)),
            dma((SLOTS, 2)),
            dma((SLOTS,)),
            dma((SLOTS,)),
            dma((SLOTS,)),
            dma((SLOTS,)),
            dma((2,)),
            dma((2, planes - 1)),
            dma((2, planes - 1)),
            dma,
            pltpu.SemaphoreType.REGULAR((2, planes - 1)),
            dma((8,)),
            dma((2,)),
            dma((2,)),
            dma((2,)),
            dma((2,)),
            dma((3,)),
            dma((3,)),
            dma((planes - 1,)),
            dma((planes - 1,)),
        ],
        compiler_params=pltpu.CompilerParams(
            collective_id=0, has_side_effects=True, vmem_limit_bytes=67043328
        ),
        name="towers",
    )(
        inputs,
        weights,
        cotangent.reshape(2, chunks, STEP, images),
        jnp.stack([small, weight_valid], axis=1),
        padded[None, :],
        padded[:, None],
        weight_valid.reshape(per_chunk, 1, IMAGES),
        small.reshape(per_chunk, 1, IMAGES),
        jnp.transpose(mix, (1, 2, 0)),
    )
    grad_weights = jnp.transpose(grad_weights.reshape(towers, -1, width), (0, 2, 1))
    grads = jnp.transpose(stats[0, :-128].reshape(chunks, 6, STEP), (1, 0, 2)).reshape(6, mine)
    return (
        stitched.reshape(2, mine, images),
        jnp.transpose(grad_inputs, (0, 2, 1)),
        grad_weights,
        grads[:2],
        grads[2:].reshape(2, 2, mine),
        rms(jnp.sum(stats[:4, -128:], axis=1)),
    )


def rms(totals):
    count = totals[3] / lax.axis_size("rows")
    return jnp.sqrt(
        jnp.stack(
            [totals[0] / (count * 2 * F), totals[1] / (count * 2 * C), totals[2] / (count * 2 * C)]
        )
    )


def line_sum(own, up):
    size = lax.axis_size("dp")
    here = lax.axis_index("dp")
    got = None
    for step in range(size - 1):
        dest = size - 1 - step + here if up else step - (size - 1) + here
        dest = jnp.clip(dest, 0, size - 1)
        term = lax.dynamic_index_in_dim(own, dest, 0, keepdims=False)
        if got is not None:
            term = (term.astype(jnp.float32) + got.astype(jnp.float32)).astype(jnp.bfloat16)
        pairs = [(z, z + 1) for z in range(step + 1)]
        if not up:
            pairs = [(size - 1 - a, size - 1 - b) for a, b in pairs]
        got = lax.ppermute(term, "dp", pairs)
    return got


def plain(inputs, weights, bias, stitch, cotangent, valid, size_class):
    rows = lax.axis_size("rows")
    size = lax.axis_size("dp")
    here = lax.axis_index("dp")
    width = inputs.shape[2]
    mine = bias.shape[1]
    step = min(BLOCK, mine)
    blocks = mine // step
    place = lax.iota(jnp.int32, width) % 36
    padded = (place // 6 == 5) | (place % 6 == 5)
    dropped = (size_class == 195)[:, None] & padded[None, :]
    used = jnp.where(dropped[None], jnp.zeros((), jnp.bfloat16), inputs)
    split = weights.reshape(2, width, rows, mine)
    weight_valid = valid.astype(jnp.float32)
    pieces, stitched, grad_bias, grad_stitch, square_pre, square_out = [], [], [], [], [], []
    grad_weights = []
    mats = [split[:, :, :, k * step : (k + 1) * step] for k in range(blocks)]
    sums = []
    for k in range(blocks):
        part = jnp.einsum("tfrc,tbf->rctb", mats[k], used, preferred_element_type=jnp.float32)
        sums.append(
            lax.psum_scatter(part.reshape(rows * step, 2, -1), "rows", scatter_dimension=0, tiled=True)
        )
    for k in range(blocks):
        cut = slice(k * step, (k + 1) * step)
        pre = jnp.transpose(sums[k], (1, 0, 2)) + bias[:, cut, None]
        act = jax.nn.relu(pre)
        mix = stitch[:, :, cut, None]
        out = jnp.sum(mix * act[None], axis=1)
        stitched.append(out.astype(jnp.bfloat16))
        upstream = cotangent[:, cut].astype(jnp.float32) * weight_valid[None, None, :]
        grad_act = jnp.sum(mix * upstream[:, None], axis=0)
        grad_pre = jnp.where(pre > 0, grad_act, 0.0).astype(jnp.bfloat16)
        grad_bias.append(jnp.sum(grad_pre.astype(jnp.float32), axis=2))
        grad_stitch.append(jnp.sum(upstream[:, None] * act[None], axis=3))
        square_pre.append(jnp.sum(weight_valid[None, None, :] * pre * pre))
        square_out.append(jnp.sum(weight_valid[None, None, :] * out * out))
        piece = lax.all_gather(grad_pre, "rows", axis=0)
        pieces.append(piece)
        block = jnp.einsum("tbf,rtcb->rtfc", used, piece, preferred_element_type=jnp.float32)
        block = block.reshape(size, rows // size, 2, width, step)
        own = block.astype(jnp.bfloat16)
        total = lax.dynamic_index_in_dim(block, here, 0, keepdims=False)
        total = total + line_sum(own, True).astype(jnp.float32) + line_sum(own, False).astype(jnp.float32)
        grad_weights.append(total)
    total_x = sum(
        jnp.einsum("rtcb,tfrc->tbf", pieces[k], mats[k], preferred_element_type=jnp.float32)
        for k in range(blocks)
    )
    grad_inputs = jnp.where(dropped[None], 0.0, total_x).astype(jnp.bfloat16)
    grad_weights = jnp.stack(grad_weights, axis=0)
    grad_weights = jnp.transpose(grad_weights, (2, 3, 1, 0, 4)).reshape(2, width, -1)
    stitched = jnp.concatenate(stitched, axis=1)
    grad_bias = jnp.concatenate(grad_bias, axis=1)
    grad_stitch = jnp.concatenate(grad_stitch, axis=2)
    used_wide = used.astype(jnp.float32)
    partial_value = jnp.stack(
        [
            jnp.sum(weight_valid[None, :, None] * used_wide * used_wide),
            sum(square_pre),
            sum(square_out),
            jnp.sum(weight_valid),
        ]
    )
    grad_bias, grad_stitch = lax.psum((grad_bias, grad_stitch), "dp")
    totals = lax.psum(partial_value, ("dp", "rows"))
    return (stitched, grad_inputs, grad_weights, grad_bias, grad_stitch, rms(totals))


def small_plane(mesh):
    return mesh.shape["rows"] == 8 and mesh.shape["dp"] in (2, 4, 8)


def solution(mesh):
    in_specs = (
        P(None, "dp", "rows"),
        P(None, "rows", None),
        P(None, "rows"),
        P(None, None, "rows"),
        P(None, "rows", "dp"),
        P("dp"),
        P("dp"),
    )
    out_specs = (
        P(None, "rows", "dp"),
        P(None, "dp", "rows"),
        P(None, "rows", "dp"),
        P(None, "rows"),
        P(None, None, "rows"),
        P(),
    )
    return jax.shard_map(
        fused if small_plane(mesh) else plain, mesh=mesh, in_specs=in_specs, out_specs=out_specs, check_vma=False
    )
```

```python
import functools

import jax
import jax.numpy as jnp
from jax import lax
from jax.experimental import pallas as pl
from jax.experimental.pallas import tpu as pltpu
from jax.sharding import PartitionSpec as P

F = 9216
C = 4096
BLOCK = 128
STEP = 64
IMAGES = 256
SLOTS = 4
WORDS = 40
TOP = 2.0**18 - 2.0
F32 = jnp.float32
BF16 = jnp.bfloat16
MESH = pl.DeviceIdType.MESH


def fold(value):
    return sum(value[:, i : i + 128] for i in range(0, value.shape[1], 128))


def lane_sums(value):
    ones = jnp.ones((8, 128), F32)
    return lax.dot_general(
        ones, value, (((1,), (1,)), ((), ())), precision=lax.Precision.HIGHEST, preferred_element_type=F32
    )


def pack(value):
    tiles = [value[8 * i : 8 * i + 8] for i in range(8)]
    top = jnp.abs(tiles[0])
    for v in tiles[1:]:
        top = jnp.maximum(top, jnp.abs(v))
    exponent = jnp.floor(jnp.log2(jnp.maximum(top, 2.0**-60))) + 1.0
    scale = jnp.exp2(-exponent) * TOP
    q = [jnp.round(v * scale).astype(jnp.int32) for v in tiles]
    low = [v & 0x1FFF for v in q[5:]]
    high = [(v >> 13) & 0x3F for v in q[5:]]
    words = [
        (q[0] << 13) | low[0],
        (q[1] << 13) | low[1],
        (q[2] << 13) | low[2],
        (q[3] << 13) | high[0] | (high[1] << 6),
        (q[4] << 13) | high[2] | ((exponent.astype(jnp.int32) & 0x7F) << 6),
    ]
    return jnp.concatenate(words, axis=0)


def unpack(words):
    w = [words[8 * i : 8 * i + 8] for i in range(5)]
    exponent = (w[4] << 19) >> 25
    scale = jnp.exp2(exponent.astype(F32)) * (1.0 / TOP)
    q = [v >> 13 for v in w]
    q.append(((w[3] << 26) >> 26 << 13) | (w[0] & 0x1FFF))
    q.append(((w[3] << 20) >> 26 << 13) | (w[1] & 0x1FFF))
    q.append(((w[4] << 26) >> 26 << 13) | (w[2] & 0x1FFF))
    return jnp.concatenate([v.astype(F32) * scale for v in q], axis=0)


def kernel(
    planes,
    x_hbm,
    w_hbm,
    cot_hbm,
    image_ref,
    pad_row_ref,
    valid_ref,
    mix_ref,
    st_hbm,
    gx_hbm,
    gw_hbm,
    stats_ref,
    g_hbm,
    acc_hbm,
    xb,
    raw,
    wt,
    part,
    p1,
    p2,
    r1,
    r2,
    gfull,
    cbuf,
    stbuf,
    zo,
    zsend,
    zrecv,
    zfin,
    gb_ref,
    gs_ref,
    sq_ref,
    usq_ref,
    wgx,
    gtile,
    acc,
    gout,
    scur,
    srecv,
    stats,
    x_sem,
    xs_sem,
    xr_sem,
    wo_sem,
    ws_sem,
    wr_sem,
    rs1_s,
    rs1_r,
    rs2_s,
    rs2_r,
    ag1_s,
    ag1_r,
    ag2_s,
    ag2_r,
    cx_s,
    cx_r,
    c_sem,
    st_sem,
    g_sem,
    z_s,
    z_r,
    zf_sem,
    z_free,
    wg_sem,
    gt_sem,
    ai_sem,
    ao_sem,
    go_sem,
    sc_s,
    sc_r,
    zs_s,
    zs_r,
):
    towers, images, width = x_hbm.shape
    chunks = cot_hbm.shape[1]
    pairs = chunks // 2
    mine = chunks * STEP
    per_chunk = images // IMAGES
    total = chunks * per_chunk
    tiles = towers * per_chunk
    last = planes - 1
    halves = 8 // planes

    z = lax.axis_index("dp")
    row = lax.axis_index("rows")
    y = row // 4
    x = (row // 2) % 2
    core = row % 2
    oy, ox, oc = 1 - y, 1 - x, 1 - core
    to_x = (z, y * 4 + ox * 2 + core)
    to_y = (z, oy * 4 + x * 2 + core)
    to_core = (z, y * 4 + x * 2 + oc)

    barrier = pltpu.get_barrier_semaphore()
    for there in (to_x, to_y, to_core):
        pl.semaphore_signal(barrier, inc=1, device_id=there, device_id_type=MESH)
    for off in range(1, planes):
        pl.semaphore_signal(barrier, inc=1, device_id=((z + off) % planes, row), device_id_type=MESH)

    def remote(src, dst, send, recv, there):
        return pltpu.make_async_remote_copy(
            src_ref=src, dst_ref=dst, send_sem=send, recv_sem=recv, device_id=there, device_id_type=MESH
        )

    def lanes(q):
        return pl.ds(pl.multiple_of((q % per_chunk) * IMAGES, IMAGES), IMAGES)

    def x_local(i):
        cut = pl.ds(i * IMAGES, IMAGES)
        return pltpu.make_async_copy(x_hbm.at[:, cut], xb.at[0, :, cut], x_sem.at[i])

    def x_remote(i):
        cut = pl.ds(i * IMAGES, IMAGES)
        return remote(x_hbm.at[:, cut], xb.at[1, :, cut], xs_sem.at[i], xr_sem.at[i], to_core)

    def w_lanes(owner, p):
        return pl.ds(pl.multiple_of(owner * mine + p * 2 * STEP, 2 * STEP), 2 * STEP)

    def w_local(p):
        return [
            pltpu.make_async_copy(w_hbm.at[:, :, w_lanes(c * 2 + core, p)], raw.at[0, :, c], wo_sem.at[c])
            for c in range(4)
        ]

    def w_remote(p):
        return [
            remote(
                w_hbm.at[:, :, w_lanes(c * 2 + oc, p)], raw.at[1, :, c], ws_sem.at[c], wr_sem.at[c], to_core
            )
            for c in range(4)
        ]

    def rs1(q):
        s = q % SLOTS
        return (
            remote(p1.at[s, 0], r1.at[s, 0], rs1_s.at[s, 0], rs1_r.at[s, 0], to_x),
            remote(p1.at[s, 1], r1.at[s, 1], rs1_s.at[s, 1], rs1_r.at[s, 1], to_y),
        )

    def rs2(q):
        s = q % SLOTS
        return (
            remote(p2.at[s, 0], r2.at[s, 0], rs2_s.at[s, 0], rs2_r.at[s, 0], to_y),
            remote(p2.at[s, 1], r2.at[s, 1], rs2_s.at[s, 1], rs2_r.at[s, 1], to_x),
        )

    def ag1(q):
        s, c, cut = q % SLOTS, (q // per_chunk) % 2, lanes(q)
        a = gfull.at[c, 0, y, x, core, :, cut]
        b = gfull.at[c, 1, y, x, core, :, cut]
        return (
            remote(a, a, ag1_s.at[s, 0], ag1_r.at[s, 0], to_x),
            remote(b, b, ag1_s.at[s, 1], ag1_r.at[s, 1], to_y),
        )

    def ag2(q):
        s, c, cut = q % SLOTS, (q // per_chunk) % 2, lanes(q)
        a = gfull.at[c, 0, y, :, core, :, cut]
        b = gfull.at[c, 1, :, x, core, :, cut]
        return (
            remote(a, a, ag2_s.at[s, 0], ag2_r.at[s, 0], to_y),
            remote(b, b, ag2_s.at[s, 1], ag2_r.at[s, 1], to_x),
        )

    def cx(q):
        s, c, cut = q % SLOTS, (q // per_chunk) % 2, lanes(q)
        a = gfull.at[c, :, :, :, core, :, cut]
        return (remote(a, a, cx_s.at[s], cx_r.at[s], to_core),)

    def cot_copy(q):
        s = q % SLOTS
        return pltpu.make_async_copy(cot_hbm.at[:, q // per_chunk, :, lanes(q)], cbuf.at[s], c_sem.at[s])

    def st_copy(q):
        s = q % SLOTS
        return pltpu.make_async_copy(stbuf.at[s], st_hbm.at[:, q // per_chunk, :, lanes(q)], st_sem.at[s])

    def g_copy(k):
        return pltpu.make_async_copy(gfull.at[k % 2], g_hbm.at[:, :, :, :, k], g_sem.at[k % 2])

    def gw_copy(k):
        return pltpu.make_async_copy(zfin, gw_hbm.at[:, :, k], zf_sem)

    def z_copy(k, j, way):
        there = (z + 1, row) if way == 0 else (z - 1, row)
        return remote(zsend.at[way, j], zrecv.at[way, j], z_s.at[way, j], z_r.at[way, j], there)

    def wg_load(g):
        p, t = g // tiles, (g % tiles) // per_chunk
        return [
            pltpu.make_async_copy(w_hbm.at[t, :, w_lanes(r, p)], wgx.at[:, pl.ds(r * 128, 128)], wg_sem.at[r])
            for r in range(8)
        ]

    def g_load(g):
        p, t, i = g // tiles, (g % tiles) // per_chunk, g % per_chunk
        return pltpu.make_async_copy(
            g_hbm.at[t, :, :, :, pl.ds(p * 2, 2), :, lanes(i)], gtile.at[g % 2], gt_sem.at[g % 2]
        )

    def acc_in(g):
        return pltpu.make_async_copy(acc_hbm.at[g % tiles], acc.at[g % 2], ai_sem.at[g % 2])

    def acc_out(g):
        return pltpu.make_async_copy(acc.at[g % 2], acc_hbm.at[g % tiles], ao_sem.at[g % 2])

    def gx_out(g):
        t = (g % tiles) // per_chunk
        return pltpu.make_async_copy(gout.at[g % 2], gx_hbm.at[t, lanes(g)], go_sem.at[g % 2])

    def in_plane(n):
        there = (to_x, to_y, to_core)[n]
        return remote(scur.at[n], srecv.at[n], sc_s.at[n], sc_r.at[n], there)

    def to_plane(off):
        there = ((z + off) % planes, row)
        return remote(stats.at[z], stats.at[z], zs_s.at[off - 1], zs_r.at[off - 1], there)

    def from_plane(off):
        there = ((z + off) % planes, row)
        held = stats.at[(z + planes - off) % planes]
        return remote(held, held, zs_s.at[off - 1], zs_r.at[off - 1], there)

    def start(copies):
        for c in copies:
            c.start()

    def wait_send(copies):
        for c in copies:
            c.wait_send()

    def wait_recv(copies):
        for c in copies:
            c.wait_recv()

    def stage(q, work, sends, *sent):
        @pl.when((q >= SLOTS) & (q < total + SLOTS))
        def _():
            for copies in sent:
                wait_send(copies(q - SLOTS))

        @pl.when((q >= 0) & (q < total))
        def _():
            work(q)
            start(sends(q))

    def turn(p):
        for c in w_local(p):
            c.wait()
        wait_recv(w_remote(p))

        def one(n, carry):
            side, t, c = n // 8, (n // 4) % 2, n % 4
            turned = jnp.transpose(raw[side, t, c])
            wt[side, t, 0, c] = turned[:STEP]
            wt[side, t, 1, c] = turned[STEP:]
            return carry

        lax.fori_loop(0, 16, one, 0)

        @pl.when(p + 1 < pairs)
        def _():
            start(w_local(p + 1))

    def forward(q):
        k, i, s = q // per_chunk, q % per_chunk, q % SLOTS
        p, h = k // 2, k % 2

        cot_copy(q).start()

        @pl.when((i == 0) & (h == 0))
        def _():
            turn(p)

        @pl.when((i == 0) & (h == 1))
        def _():
            wait_send(w_remote(p))

            @pl.when(p + 1 < pairs)
            def _():
                start(w_remote(p + 1))

        cut = pl.ds(pl.multiple_of(i * IMAGES, IMAGES), IMAGES)

        @pl.when(k == 0)
        def _():
            x_local(i).wait()
            x_remote(i).wait_recv()
            keep = (1.0 - image_ref[cut, 0:1] * pad_row_ref[...]).astype(BF16)
            valid = image_ref[cut, 1:2]
            for t in range(towers):
                used = xb[0, t, cut] * keep
                xb[0, t, cut] = used
                used = used.astype(F32)
                usq_ref[...] = usq_ref[...] + jnp.sum(used * used * valid, axis=0, keepdims=True)
                xb[1, t, cut] = xb[1, t, cut] * keep

        for t in range(towers):
            out = lax.dot_general(
                wt[0, t, h].reshape(4 * STEP, width),
                xb[0, t, cut],
                (((1,), (1,)), ((), ())),
                preferred_element_type=F32,
            ) + lax.dot_general(
                wt[1, t, h].reshape(4 * STEP, width),
                xb[1, t, cut],
                (((1,), (1,)), ((), ())),
                preferred_element_type=F32,
            )
            out = out.reshape(2, 2, STEP, IMAGES)
            for a in range(2):
                for b in range(2):
                    part[s, a, b, t] = out[a, b]
        for a in range(2):
            p1[s, 0, a] = pack(part[s, a, ox, 0])
            p1[s, 1, a] = pack(part[s, oy, a, 1])

    def reduce(q):
        s = q % SLOTS
        wait_recv(rs1(q))
        p2[s, 0] = pack(part[s, oy, x, 0] + unpack(r1[s, 0, oy]))
        p2[s, 1] = pack(part[s, y, ox, 1] + unpack(r1[s, 1, ox]))
        part[s, y, x, 0] = part[s, y, x, 0] + unpack(r1[s, 0, y])
        part[s, y, x, 1] = part[s, y, x, 1] + unpack(r1[s, 1, x])

    def pointwise(q):
        k, i, s = q // per_chunk, q % per_chunk, q % SLOTS
        wait_recv(rs2(q))
        cot_copy(q).wait()

        @pl.when(q >= SLOTS)
        def _():
            st_copy(q - SLOTS).wait()

        valid = valid_ref[i]
        mix = mix_ref[k]
        bias = [mix[:, t : t + 1] for t in range(2)]
        stitch = [[mix[:, 2 + 2 * a + b : 3 + 2 * a + b] for b in range(2)] for a in range(2)]
        pre = [part[s, y, x, t] + unpack(r2[s, t]) + bias[t] for t in range(2)]
        act = [jnp.maximum(p, 0.0) for p in pre]
        up = [cbuf[s, t].astype(F32) * valid for t in range(2)]
        cut = lanes(q)
        for a in range(2):
            out = stitch[a][0] * act[0] + stitch[a][1] * act[1]
            stbuf[s, a] = out.astype(BF16)
            sq_ref[1] = sq_ref[1] + fold(out * out * valid)
            for b in range(2):
                gs_ref[k, a, b] = gs_ref[k, a, b] + fold(up[a] * act[b])
        for t in range(2):
            sq_ref[0] = sq_ref[0] + fold(pre[t] * pre[t] * valid)
            grad = stitch[0][t] * up[0] + stitch[1][t] * up[1]
            grad = jnp.where(pre[t] > 0, grad, 0.0).astype(BF16)
            gfull[k % 2, t, y, x, core, :, cut] = grad
            gb_ref[k, t] = gb_ref[k, t] + fold(grad.astype(F32))
        st_copy(q).start()

    def spread(q):
        wait_recv(ag1(q))

    def across(q):
        wait_recv(ag2(q))

    def terms(k, n):
        third = width // 3
        for t in range(towers):
            value = jnp.dot(
                gfull[k % 2, t].reshape(8 * STEP, images),
                xb[0, t, :, n * third : (n + 1) * third],
                preferred_element_type=F32,
            )
            value = value.astype(BF16).reshape(planes, halves, STEP, third)
            for d in range(planes):
                for e in range(halves):
                    zo[t, d, e, :, n * third : (n + 1) * third] = value[d, e]

    def chain(k, j):
        if j == planes - 2:

            @pl.when(k > 0)
            def _():
                gw_copy(k - 1).wait()

            def begin(i, carry):
                t, e = i // halves, i % halves
                zfin[t, e] = zo[t, z, e].astype(F32)
                return carry

            lax.fori_loop(0, towers * halves, begin, 0)
        for way in range(2):
            near = z if way == 0 else last - z
            source = (z - 1, row) if way == 0 else (z + 1, row)

            def freed():
                @pl.when(k + 1 < chunks)
                def _():
                    pl.semaphore_signal(
                        z_free.at[way, j - 1], inc=1, device_id=source, device_id_type=MESH
                    )

            if j <= planes - 2:

                @pl.when(near <= j)
                def _():
                    dest = last - j + z if way == 0 else j - last + z

                    @pl.when(k > 0)
                    def _():
                        z_copy(k - 1, j, way).wait_send()

                    if j > 0:

                        @pl.when(near >= 1)
                        def _():
                            z_copy(k, j - 1, way).wait_recv()

                            def add(i, carry):
                                t, e = i // halves, i % halves
                                value = zo[t, dest, e].astype(F32) + zrecv[way, j - 1, t, e].astype(F32)
                                zsend[way, j, t, e] = value.astype(BF16)
                                return carry

                            lax.fori_loop(0, towers * halves, add, 0)
                            freed()

                        @pl.when(near == 0)
                        def _():
                            zsend[way, j] = zo[:, dest]

                    else:
                        zsend[way, j] = zo[:, dest]

                    @pl.when(k > 0)
                    def _():
                        pl.semaphore_wait(z_free.at[way, j], 1)

                    z_copy(k, j, way).start()

            else:

                @pl.when(near >= 1)
                def _():
                    z_copy(k, j - 1, way).wait_recv()

                    def more(i, carry):
                        t, e = i // halves, i % halves
                        zfin[t, e] = zfin[t, e] + zrecv[way, j - 1, t, e].astype(F32)
                        return carry

                    lax.fori_loop(0, towers * halves, more, 0)
                    freed()

        if j == planes - 1:
            gw_copy(k).start()

    def prepare(g):
        g_load(g).start()

        @pl.when(g % per_chunk == 0)
        def _():
            start(wg_load(g))

        @pl.when((g >= 2) & (g - 2 < (pairs - 1) * tiles))
        def _():
            acc_out(g - 2).wait()

        @pl.when(g >= tiles)
        def _():
            acc_in(g).start()

    def tile(g):
        g_load(g).wait()

        @pl.when(g % per_chunk == 0)
        def _():
            for c in wg_load(g):
                c.wait()

        value = jnp.dot(
            wgx[...], gtile[g % 2].reshape(16 * STEP, IMAGES), preferred_element_type=F32
        )

        @pl.when(g < tiles)
        def _():
            acc[g % 2] = value

        @pl.when(g >= tiles)
        def _():
            acc_in(g).wait()
            acc[g % 2] = acc[g % 2] + value

        @pl.when(g < (pairs - 1) * tiles)
        def _():
            acc_out(g).start()

        @pl.when(g >= (pairs - 1) * tiles)
        def _():
            @pl.when(g >= (pairs - 1) * tiles + 2)
            def _():
                gx_out(g - 2).wait()

            keep = (1.0 - image_ref[lanes(g), 0:1] * pad_row_ref[...]).astype(BF16)
            gout[g % 2] = jnp.transpose(acc[g % 2].astype(BF16)) * keep
            gx_out(g).start()

    def sums(n):
        if n == 0:
            scur[0] = jnp.zeros_like(scur[0])
            scur[0, 0:1] = fold(usq_ref[...])
            scur[0, 1:2] = jnp.sum(sq_ref[0], axis=0, keepdims=True)
            scur[0, 2:3] = jnp.sum(sq_ref[1], axis=0, keepdims=True)
            scur[0, 3:4] = fold(sum(valid_ref[i] for i in range(per_chunk)))
            for k in range(chunks):
                at = k * 6 * STEP
                stats[z, :, at : at + 2 * STEP] = lane_sums(gb_ref[k].reshape(2 * STEP, 128))
                stats[z, :, at + 2 * STEP : at + 6 * STEP] = lane_sums(gs_ref[k].reshape(4 * STEP, 128))
        else:
            in_plane(n - 1).wait()
            value = scur[n - 1] + srecv[n - 1]
            if n < 3:
                scur[n] = value
            else:
                stats[z, :, chunks * 6 * STEP :] = value
        if n < 3:
            in_plane(n).start()
        else:
            for off in range(1, planes):
                to_plane(off).start()

    start(w_local(0))
    for i in range(per_chunk):
        x_local(i).start()
    pl.semaphore_wait(barrier, 2 + planes)
    start(w_remote(0))

    def send_x(i, carry):
        x_remote(i).start()
        return carry

    lax.fori_loop(0, per_chunk, send_x, 0)
    gb_ref[...] = jnp.zeros_like(gb_ref)
    gs_ref[...] = jnp.zeros_like(gs_ref)
    sq_ref[...] = jnp.zeros_like(sq_ref)
    usq_ref[...] = jnp.zeros_like(usq_ref)

    ready = per_chunk - 1 + 5
    offsets = [2 + 3 * j for j in range(planes)]
    ends = [2 + 5 * j for j in range(planes)]
    first = per_chunk + 3

    def body(s, carry):
        stage(s, forward, rs1, rs1)
        stage(s - 1, reduce, rs2, rs2)
        stage(s - 2, pointwise, ag1, ag1)
        stage(s - 3, spread, ag2, ag2)
        stage(s - 4, across, cx, cx)

        @pl.when((s >= 5) & (s < total + 5))
        def _():
            wait_recv(cx(s - 5))

        for n in range(4):

            @pl.when(s == total + 2 + n)
            def _():
                sums(n)

        @pl.when(s >= ready)
        def _():
            done = s - ready
            k = done // per_chunk
            at = done % per_chunk

            def step(j):
                since = done - offsets[j]
                usual = (since >= 0) & (since % per_chunk == 0) & (since // per_chunk < chunks - 1)
                final = done == (chunks - 1) * per_chunk + ends[j]

                @pl.when(usual | final)
                def _():
                    chain(jnp.where(final, chunks - 1, since // per_chunk), j)

            for j in range(1, planes):
                step(j)
            for n in range(3):

                @pl.when((at == n) & (k < chunks))
                def _():
                    if n == 0:
                        g_copy(k).start()
                    terms(k, n)
                    if n == 2:
                        g_copy(k).wait()

            step(0)
            g = done - first

            @pl.when((g >= 0) & (g < pairs * tiles))
            def _():
                tile(g)

            @pl.when((g >= -1) & (g < pairs * tiles - 1))
            def _():
                prepare(g + 1)

        return carry

    lax.fori_loop(0, ready + max((chunks - 1) * per_chunk + ends[-1], first + pairs * tiles - 1) + 1, body, 0)

    def drain(q, carry):
        st_copy(q).wait()
        return carry

    lax.fori_loop(total - SLOTS, total, drain, 0)

    def drain_x(i, carry):
        x_remote(i).wait_send()
        return carry

    lax.fori_loop(0, per_chunk, drain_x, 0)
    for g in (pairs * tiles - 2, pairs * tiles - 1):
        gx_out(g).wait()
    gw_copy(chunks - 1).wait()
    for way in range(2):
        near = z if way == 0 else last - z
        for j in range(planes - 1):

            @pl.when(near <= j)
            def _():
                z_copy(chunks - 1, j, way).wait_send()

    for off in range(1, planes):
        to_plane(off).wait_send()
        from_plane(off).wait_recv()
    stats_ref[...] = sum(stats[d] for d in range(planes))


def fused(inputs, weights, bias, stitch, cotangent, valid, size_class):
    planes = lax.axis_size("dp")
    towers, images, width = inputs.shape
    mine = bias.shape[1]
    chunks = mine // STEP
    per_chunk = images // IMAGES
    halves = 8 // planes
    tiles = towers * per_chunk
    small = (size_class == 195).astype(F32)
    place = lax.iota(jnp.int32, width) % 36
    padded = ((place // 6 == 5) | (place % 6 == 5)).astype(F32)
    weight_valid = valid.astype(F32)
    mix = jnp.concatenate([bias, stitch.reshape(4, mine)], axis=0).reshape(6, chunks, STEP)
    many = chunks * 6 * STEP + 128
    vmem = pl.BlockSpec(memory_space=pltpu.VMEM)
    hbm = pl.BlockSpec(memory_space=pl.ANY)
    dma = pltpu.SemaphoreType.DMA
    stitched, grad_inputs, grad_weights, stats, _, _ = pl.pallas_call(
        functools.partial(kernel, planes),
        out_shape=(
            jax.ShapeDtypeStruct((2, chunks, STEP, images), BF16),
            jax.ShapeDtypeStruct((towers, images, width), BF16),
            jax.ShapeDtypeStruct((2, halves, chunks, STEP, width), F32),
            jax.ShapeDtypeStruct((8, many), F32),
            jax.ShapeDtypeStruct((2, 2, 2, 2, chunks, STEP, images), BF16),
            jax.ShapeDtypeStruct((tiles, width, IMAGES), F32),
        ),
        in_specs=[hbm] * 3 + [vmem] * 4,
        out_specs=(hbm, hbm, hbm, vmem, hbm, hbm),
        scratch_shapes=[
            pltpu.VMEM((2, towers, images, width), BF16),
            pltpu.VMEM((2, towers, 4, width, 2 * STEP), BF16),
            pltpu.VMEM((2, towers, 2, 4, STEP, width), BF16),
            pltpu.VMEM((SLOTS, 2, 2, towers, STEP, IMAGES), F32),
            pltpu.VMEM((SLOTS, 2, 2, WORDS, IMAGES), jnp.int32),
            pltpu.VMEM((SLOTS, 2, WORDS, IMAGES), jnp.int32),
            pltpu.VMEM((SLOTS, 2, 2, WORDS, IMAGES), jnp.int32),
            pltpu.VMEM((SLOTS, 2, WORDS, IMAGES), jnp.int32),
            pltpu.VMEM((2, towers, 2, 2, 2, STEP, images), BF16),
            pltpu.VMEM((SLOTS, 2, STEP, IMAGES), BF16),
            pltpu.VMEM((SLOTS, 2, STEP, IMAGES), BF16),
            pltpu.VMEM((towers, planes, halves, STEP, width), BF16),
            pltpu.VMEM((2, planes - 1, towers, halves, STEP, width), BF16),
            pltpu.VMEM((2, planes - 1, towers, halves, STEP, width), BF16),
            pltpu.VMEM((towers, halves, STEP, width), F32),
            pltpu.VMEM((chunks, 2, STEP, 128), F32),
            pltpu.VMEM((chunks, 2, 2, STEP, 128), F32),
            pltpu.VMEM((2, STEP, 128), F32),
            pltpu.VMEM((1, width), F32),
            pltpu.VMEM((width, 16 * STEP), BF16),
            pltpu.VMEM((2, 2, 2, 2, 2, STEP, IMAGES), BF16),
            pltpu.VMEM((2, width, IMAGES), F32),
            pltpu.VMEM((2, IMAGES, width), BF16),
            pltpu.VMEM((3, 8, 128), F32),
            pltpu.VMEM((3, 8, 128), F32),
            pltpu.VMEM((planes, 8, many), F32),
            dma((per_chunk,)),
            dma((per_chunk,)),
            dma((per_chunk,)),
            dma((4,)),
            dma((4,)),
            dma((4,)),
            dma((SLOTS, 2)),
            dma((SLOTS, 2)),
            dma((SLOTS, 2)),
            dma((SLOTS, 2)),
            dma((SLOTS, 2)),
            dma((SLOTS, 2)),
            dma((SLOTS, 2)),
            dma((SLOTS, 2)),
            dma((SLOTS,)),
            dma((SLOTS,)),
            dma((SLOTS,)),
            dma((SLOTS,)),
            dma((2,)),
            dma((2, planes - 1)),
            dma((2, planes - 1)),
            dma,
            pltpu.SemaphoreType.REGULAR((2, planes - 1)),
            dma((8,)),
            dma((2,)),
            dma((2,)),
            dma((2,)),
            dma((2,)),
            dma((3,)),
            dma((3,)),
            dma((planes - 1,)),
            dma((planes - 1,)),
        ],
        compiler_params=pltpu.CompilerParams(
            collective_id=0, has_side_effects=True, vmem_limit_bytes=67043328
        ),
        name="towers",
    )(
        inputs,
        weights,
        cotangent.reshape(2, chunks, STEP, images),
        jnp.stack([small, weight_valid], axis=1),
        padded[None, :],
        weight_valid.reshape(per_chunk, 1, IMAGES),
        jnp.transpose(mix, (1, 2, 0)),
    )
    grad_weights = jnp.transpose(grad_weights.reshape(towers, -1, width), (0, 2, 1))
    grads = jnp.transpose(stats[0, :-128].reshape(chunks, 6, STEP), (1, 0, 2)).reshape(6, mine)
    return (
        stitched.reshape(2, mine, images),
        grad_inputs,
        grad_weights,
        grads[:2],
        grads[2:].reshape(2, 2, mine),
        rms(jnp.sum(stats[:4, -128:], axis=1)),
    )


def rms(totals):
    count = totals[3] / lax.axis_size("rows")
    return jnp.sqrt(
        jnp.stack(
            [totals[0] / (count * 2 * F), totals[1] / (count * 2 * C), totals[2] / (count * 2 * C)]
        )
    )


def line_sum(own, up):
    size = lax.axis_size("dp")
    here = lax.axis_index("dp")
    got = None
    for step in range(size - 1):
        dest = size - 1 - step + here if up else step - (size - 1) + here
        dest = jnp.clip(dest, 0, size - 1)
        term = lax.dynamic_index_in_dim(own, dest, 0, keepdims=False)
        if got is not None:
            term = (term.astype(jnp.float32) + got.astype(jnp.float32)).astype(jnp.bfloat16)
        pairs = [(z, z + 1) for z in range(step + 1)]
        if not up:
            pairs = [(size - 1 - a, size - 1 - b) for a, b in pairs]
        got = lax.ppermute(term, "dp", pairs)
    return got


def plain(inputs, weights, bias, stitch, cotangent, valid, size_class):
    rows = lax.axis_size("rows")
    size = lax.axis_size("dp")
    here = lax.axis_index("dp")
    width = inputs.shape[2]
    mine = bias.shape[1]
    step = min(BLOCK, mine)
    blocks = mine // step
    place = lax.iota(jnp.int32, width) % 36
    padded = (place // 6 == 5) | (place % 6 == 5)
    dropped = (size_class == 195)[:, None] & padded[None, :]
    used = jnp.where(dropped[None], jnp.zeros((), jnp.bfloat16), inputs)
    split = weights.reshape(2, width, rows, mine)
    weight_valid = valid.astype(jnp.float32)
    pieces, stitched, grad_bias, grad_stitch, square_pre, square_out = [], [], [], [], [], []
    grad_weights = []
    mats = [split[:, :, :, k * step : (k + 1) * step] for k in range(blocks)]
    sums = []
    for k in range(blocks):
        part = jnp.einsum("tfrc,tbf->rctb", mats[k], used, preferred_element_type=jnp.float32)
        sums.append(
            lax.psum_scatter(part.reshape(rows * step, 2, -1), "rows", scatter_dimension=0, tiled=True)
        )
    for k in range(blocks):
        cut = slice(k * step, (k + 1) * step)
        pre = jnp.transpose(sums[k], (1, 0, 2)) + bias[:, cut, None]
        act = jax.nn.relu(pre)
        mix = stitch[:, :, cut, None]
        out = jnp.sum(mix * act[None], axis=1)
        stitched.append(out.astype(jnp.bfloat16))
        upstream = cotangent[:, cut].astype(jnp.float32) * weight_valid[None, None, :]
        grad_act = jnp.sum(mix * upstream[:, None], axis=0)
        grad_pre = jnp.where(pre > 0, grad_act, 0.0).astype(jnp.bfloat16)
        grad_bias.append(jnp.sum(grad_pre.astype(jnp.float32), axis=2))
        grad_stitch.append(jnp.sum(upstream[:, None] * act[None], axis=3))
        square_pre.append(jnp.sum(weight_valid[None, None, :] * pre * pre))
        square_out.append(jnp.sum(weight_valid[None, None, :] * out * out))
        piece = lax.all_gather(grad_pre, "rows", axis=0)
        pieces.append(piece)
        block = jnp.einsum("tbf,rtcb->rtfc", used, piece, preferred_element_type=jnp.float32)
        block = block.reshape(size, rows // size, 2, width, step)
        own = block.astype(jnp.bfloat16)
        total = lax.dynamic_index_in_dim(block, here, 0, keepdims=False)
        total = total + line_sum(own, True).astype(jnp.float32) + line_sum(own, False).astype(jnp.float32)
        grad_weights.append(total)
    total_x = sum(
        jnp.einsum("rtcb,tfrc->tbf", pieces[k], mats[k], preferred_element_type=jnp.float32)
        for k in range(blocks)
    )
    grad_inputs = jnp.where(dropped[None], 0.0, total_x).astype(jnp.bfloat16)
    grad_weights = jnp.stack(grad_weights, axis=0)
    grad_weights = jnp.transpose(grad_weights, (2, 3, 1, 0, 4)).reshape(2, width, -1)
    stitched = jnp.concatenate(stitched, axis=1)
    grad_bias = jnp.concatenate(grad_bias, axis=1)
    grad_stitch = jnp.concatenate(grad_stitch, axis=2)
    used_wide = used.astype(jnp.float32)
    partial_value = jnp.stack(
        [
            jnp.sum(weight_valid[None, :, None] * used_wide * used_wide),
            sum(square_pre),
            sum(square_out),
            jnp.sum(weight_valid),
        ]
    )
    grad_bias, grad_stitch = lax.psum((grad_bias, grad_stitch), "dp")
    totals = lax.psum(partial_value, ("dp", "rows"))
    return (stitched, grad_inputs, grad_weights, grad_bias, grad_stitch, rms(totals))


def small_plane(mesh):
    return mesh.shape["rows"] == 8 and mesh.shape["dp"] in (2, 4, 8)


def solution(mesh):
    in_specs = (
        P(None, "dp", "rows"),
        P(None, "rows", None),
        P(None, "rows"),
        P(None, None, "rows"),
        P(None, "rows", "dp"),
        P("dp"),
        P("dp"),
    )
    out_specs = (
        P(None, "rows", "dp"),
        P(None, "dp", "rows"),
        P(None, "rows", "dp"),
        P(None, "rows"),
        P(None, None, "rows"),
        P(),
    )
    return jax.shard_map(
        fused if small_plane(mesh) else plain, mesh=mesh, in_specs=in_specs, out_specs=out_specs, check_vma=False
    )
```

```python
import functools

import jax
import jax.numpy as jnp
import numpy as np
from jax import lax
from jax.experimental import pallas as pl
from jax.experimental.pallas import tpu as pltpu
from jax.sharding import PartitionSpec as P

F = 9216
C = 4096
BLOCK = 128
STEP = 64
IMAGES = 256
SLOTS = 4
WORDS = 40
TOP = 2.0**18 - 2.0
F32 = jnp.float32
BF16 = jnp.bfloat16
MESH = pl.DeviceIdType.MESH


def fold(value):
    return sum(value[:, i : i + 128] for i in range(0, value.shape[1], 128))


def lane_sums(value):
    ones = jnp.ones((8, 128), F32)
    return lax.dot_general(
        ones, value, (((1,), (1,)), ((), ())), precision=lax.Precision.HIGHEST, preferred_element_type=F32
    )


def pack(value):
    tiles = [value[8 * i : 8 * i + 8] for i in range(8)]
    top = jnp.abs(tiles[0])
    for v in tiles[1:]:
        top = jnp.maximum(top, jnp.abs(v))
    exponent = jnp.floor(jnp.log2(jnp.maximum(top, 2.0**-60))) + 1.0
    scale = jnp.exp2(-exponent) * TOP
    q = [jnp.round(v * scale).astype(jnp.int32) for v in tiles]
    low = [v & 0x1FFF for v in q[5:]]
    high = [(v >> 13) & 0x3F for v in q[5:]]
    words = [
        (q[0] << 13) | low[0],
        (q[1] << 13) | low[1],
        (q[2] << 13) | low[2],
        (q[3] << 13) | high[0] | (high[1] << 6),
        (q[4] << 13) | high[2] | ((exponent.astype(jnp.int32) & 0x7F) << 6),
    ]
    return jnp.concatenate(words, axis=0)


def unpack(words):
    w = [words[8 * i : 8 * i + 8] for i in range(5)]
    exponent = (w[4] << 19) >> 25
    scale = jnp.exp2(exponent.astype(F32)) * (1.0 / TOP)
    q = [v >> 13 for v in w]
    q.append(((w[3] << 26) >> 26 << 13) | (w[0] & 0x1FFF))
    q.append(((w[3] << 20) >> 26 << 13) | (w[1] & 0x1FFF))
    q.append(((w[4] << 26) >> 26 << 13) | (w[2] & 0x1FFF))
    return jnp.concatenate([v.astype(F32) * scale for v in q], axis=0)


def kernel(
    planes,
    x_hbm,
    w_hbm,
    cot_hbm,
    valid_in,
    class_in,
    pad_row_ref,
    bias_in,
    stitch_in,
    st_hbm,
    gx_hbm,
    gw_hbm,
    bias_out,
    stitch_out,
    rms_out,
    g_hbm,
    acc_hbm,
    image_ref,
    valid_ref,
    mix_ref,
    xb,
    raw,
    wt,
    part,
    p1,
    p2,
    r1,
    r2,
    gfull,
    cbuf,
    stbuf,
    zo,
    zsend,
    zrecv,
    zfin,
    gb_ref,
    gs_ref,
    sq_ref,
    usq_ref,
    wgx,
    gtile,
    acc,
    gout,
    scur,
    srecv,
    stats,
    x_sem,
    xs_sem,
    xr_sem,
    wo_sem,
    ws_sem,
    wr_sem,
    rs1_s,
    rs1_r,
    rs2_s,
    rs2_r,
    ag1_s,
    ag1_r,
    ag2_s,
    ag2_r,
    cx_s,
    cx_r,
    c_sem,
    st_sem,
    g_sem,
    z_s,
    z_r,
    zf_sem,
    z_free,
    wg_sem,
    gt_sem,
    ai_sem,
    ao_sem,
    go_sem,
    sc_s,
    sc_r,
    zs_s,
    zs_r,
):
    towers, images, width = x_hbm.shape
    chunks = cot_hbm.shape[1]
    pairs = chunks // 2
    mine = chunks * STEP
    per_chunk = images // IMAGES
    total = chunks * per_chunk
    tiles = towers * per_chunk
    last = planes - 1
    halves = 8 // planes

    z = lax.axis_index("dp")
    row = lax.axis_index("rows")
    y = row // 4
    x = (row // 2) % 2
    core = row % 2
    oy, ox, oc = 1 - y, 1 - x, 1 - core
    to_x = (z, y * 4 + ox * 2 + core)
    to_y = (z, oy * 4 + x * 2 + core)
    to_core = (z, y * 4 + x * 2 + oc)

    barrier = pltpu.get_barrier_semaphore()
    for there in (to_x, to_y, to_core):
        pl.semaphore_signal(barrier, inc=1, device_id=there, device_id_type=MESH)
    for off in range(1, planes):
        pl.semaphore_signal(barrier, inc=1, device_id=((z + off) % planes, row), device_id_type=MESH)

    def remote(src, dst, send, recv, there):
        return pltpu.make_async_remote_copy(
            src_ref=src, dst_ref=dst, send_sem=send, recv_sem=recv, device_id=there, device_id_type=MESH
        )

    def lanes(q):
        return pl.ds(pl.multiple_of((q % per_chunk) * IMAGES, IMAGES), IMAGES)

    def x_local(i):
        cut = pl.ds(i * IMAGES, IMAGES)
        return pltpu.make_async_copy(x_hbm.at[:, cut], xb.at[0, :, cut], x_sem.at[i])

    def x_remote(i):
        cut = pl.ds(i * IMAGES, IMAGES)
        return remote(x_hbm.at[:, cut], xb.at[1, :, cut], xs_sem.at[i], xr_sem.at[i], to_core)

    def w_lanes(owner, p):
        return pl.ds(pl.multiple_of(owner * mine + p * 2 * STEP, 2 * STEP), 2 * STEP)

    def w_local(p):
        return [
            pltpu.make_async_copy(w_hbm.at[:, :, w_lanes(c * 2 + core, p)], raw.at[0, :, c], wo_sem.at[c])
            for c in range(4)
        ]

    def w_remote(p):
        return [
            remote(
                w_hbm.at[:, :, w_lanes(c * 2 + oc, p)], raw.at[1, :, c], ws_sem.at[c], wr_sem.at[c], to_core
            )
            for c in range(4)
        ]

    def rs1(q):
        s = q % SLOTS
        return (
            remote(p1.at[s, 0], r1.at[s, 0], rs1_s.at[s, 0], rs1_r.at[s, 0], to_x),
            remote(p1.at[s, 1], r1.at[s, 1], rs1_s.at[s, 1], rs1_r.at[s, 1], to_y),
        )

    def rs2(q):
        s = q % SLOTS
        return (
            remote(p2.at[s, 0], r2.at[s, 0], rs2_s.at[s, 0], rs2_r.at[s, 0], to_y),
            remote(p2.at[s, 1], r2.at[s, 1], rs2_s.at[s, 1], rs2_r.at[s, 1], to_x),
        )

    def ag1(q):
        s, c, cut = q % SLOTS, (q // per_chunk) % 2, lanes(q)
        a = gfull.at[c, 0, y, x, core, :, cut]
        b = gfull.at[c, 1, y, x, core, :, cut]
        return (
            remote(a, a, ag1_s.at[s, 0], ag1_r.at[s, 0], to_x),
            remote(b, b, ag1_s.at[s, 1], ag1_r.at[s, 1], to_y),
        )

    def ag2(q):
        s, c, cut = q % SLOTS, (q // per_chunk) % 2, lanes(q)
        a = gfull.at[c, 0, y, :, core, :, cut]
        b = gfull.at[c, 1, :, x, core, :, cut]
        return (
            remote(a, a, ag2_s.at[s, 0], ag2_r.at[s, 0], to_y),
            remote(b, b, ag2_s.at[s, 1], ag2_r.at[s, 1], to_x),
        )

    def cx(q):
        s, c, cut = q % SLOTS, (q // per_chunk) % 2, lanes(q)
        a = gfull.at[c, :, :, :, core, :, cut]
        return (remote(a, a, cx_s.at[s], cx_r.at[s], to_core),)

    def cot_copy(q):
        s = q % SLOTS
        return pltpu.make_async_copy(cot_hbm.at[:, q // per_chunk, :, lanes(q)], cbuf.at[s], c_sem.at[s])

    def st_copy(q):
        s = q % SLOTS
        return pltpu.make_async_copy(stbuf.at[s], st_hbm.at[:, q // per_chunk, :, lanes(q)], st_sem.at[s])

    def g_copy(k):
        return pltpu.make_async_copy(gfull.at[k % 2], g_hbm.at[:, :, :, :, k], g_sem.at[k % 2])

    def gw_copy(k):
        return pltpu.make_async_copy(zfin, gw_hbm.at[:, :, k], zf_sem)

    def z_copy(k, j, way):
        there = (z + 1, row) if way == 0 else (z - 1, row)
        return remote(zsend.at[way, j], zrecv.at[way, j], z_s.at[way, j], z_r.at[way, j], there)

    def wg_load(g):
        p, t = g // tiles, (g % tiles) // per_chunk
        return [
            pltpu.make_async_copy(w_hbm.at[t, :, w_lanes(r, p)], wgx.at[:, pl.ds(r * 128, 128)], wg_sem.at[r])
            for r in range(8)
        ]

    def g_load(g):
        p, t, i = g // tiles, (g % tiles) // per_chunk, g % per_chunk
        return pltpu.make_async_copy(
            g_hbm.at[t, :, :, :, pl.ds(p * 2, 2), :, lanes(i)], gtile.at[g % 2], gt_sem.at[g % 2]
        )

    def acc_in(g):
        return pltpu.make_async_copy(acc_hbm.at[g % tiles], acc.at[g % 2], ai_sem.at[g % 2])

    def acc_out(g):
        return pltpu.make_async_copy(acc.at[g % 2], acc_hbm.at[g % tiles], ao_sem.at[g % 2])

    def gx_out(g):
        t = (g % tiles) // per_chunk
        return pltpu.make_async_copy(gout.at[g % 2], gx_hbm.at[t, lanes(g)], go_sem.at[g % 2])

    def in_plane(n):
        there = (to_x, to_y, to_core)[n]
        return remote(scur.at[n], srecv.at[n], sc_s.at[n], sc_r.at[n], there)

    def to_plane(off):
        there = ((z + off) % planes, row)
        return remote(stats.at[z], stats.at[z], zs_s.at[off - 1], zs_r.at[off - 1], there)

    def from_plane(off):
        there = ((z + off) % planes, row)
        held = stats.at[(z + planes - off) % planes]
        return remote(held, held, zs_s.at[off - 1], zs_r.at[off - 1], there)

    def start(copies):
        for c in copies:
            c.start()

    def wait_send(copies):
        for c in copies:
            c.wait_send()

    def wait_recv(copies):
        for c in copies:
            c.wait_recv()

    def stage(q, work, sends, *sent):
        @pl.when((q >= SLOTS) & (q < total + SLOTS))
        def _():
            for copies in sent:
                wait_send(copies(q - SLOTS))

        @pl.when((q >= 0) & (q < total))
        def _():
            work(q)
            start(sends(q))

    def turn(p):
        for c in w_local(p):
            c.wait()
        wait_recv(w_remote(p))

        def one(n, carry):
            side, t, c = n // 8, (n // 4) % 2, n % 4
            turned = jnp.transpose(raw[side, t, c])
            wt[side, t, 0, c] = turned[:STEP]
            wt[side, t, 1, c] = turned[STEP:]
            return carry

        lax.fori_loop(0, 16, one, 0)

        @pl.when(p + 1 < pairs)
        def _():
            start(w_local(p + 1))

    def forward(q):
        k, i, s = q // per_chunk, q % per_chunk, q % SLOTS
        p, h = k // 2, k % 2

        cot_copy(q).start()

        @pl.when((i == 0) & (h == 0))
        def _():
            turn(p)

        @pl.when((i == 0) & (h == 1))
        def _():
            wait_send(w_remote(p))

            @pl.when(p + 1 < pairs)
            def _():
                start(w_remote(p + 1))

        cut = pl.ds(pl.multiple_of(i * IMAGES, IMAGES), IMAGES)

        @pl.when(k == 0)
        def _():
            x_local(i).wait()
            x_remote(i).wait_recv()
            keep = (1.0 - image_ref[cut, 0:1] * pad_row_ref[...]).astype(BF16)
            valid = image_ref[cut, 64:65]
            for t in range(towers):
                used = xb[0, t, cut] * keep
                xb[0, t, cut] = used
                used = used.astype(F32)
                usq_ref[...] = usq_ref[...] + jnp.sum(used * used * valid, axis=0, keepdims=True)
                xb[1, t, cut] = xb[1, t, cut] * keep

        for t in range(towers):
            out = lax.dot_general(
                wt[0, t, h].reshape(4 * STEP, width),
                xb[0, t, cut],
                (((1,), (1,)), ((), ())),
                preferred_element_type=F32,
            ) + lax.dot_general(
                wt[1, t, h].reshape(4 * STEP, width),
                xb[1, t, cut],
                (((1,), (1,)), ((), ())),
                preferred_element_type=F32,
            )
            out = out.reshape(2, 2, STEP, IMAGES)
            for a in range(2):
                for b in range(2):
                    part[s, a, b, t] = out[a, b]
        for a in range(2):
            p1[s, 0, a] = pack(part[s, a, ox, 0])
            p1[s, 1, a] = pack(part[s, oy, a, 1])

    def reduce(q):
        s = q % SLOTS
        wait_recv(rs1(q))
        p2[s, 0] = pack(part[s, oy, x, 0] + unpack(r1[s, 0, oy]))
        p2[s, 1] = pack(part[s, y, ox, 1] + unpack(r1[s, 1, ox]))
        part[s, y, x, 0] = part[s, y, x, 0] + unpack(r1[s, 0, y])
        part[s, y, x, 1] = part[s, y, x, 1] + unpack(r1[s, 1, x])

    def pointwise(q):
        k, i, s = q // per_chunk, q % per_chunk, q % SLOTS
        wait_recv(rs2(q))
        cot_copy(q).wait()

        @pl.when(q >= SLOTS)
        def _():
            st_copy(q - SLOTS).wait()

        valid = valid_ref[i]
        mix = mix_ref[k]
        bias = [mix[:, t : t + 1] for t in range(2)]
        stitch = [[mix[:, 2 + 2 * a + b : 3 + 2 * a + b] for b in range(2)] for a in range(2)]
        pre = [part[s, y, x, t] + unpack(r2[s, t]) + bias[t] for t in range(2)]
        act = [jnp.maximum(p, 0.0) for p in pre]
        up = [cbuf[s, t].astype(F32) * valid for t in range(2)]
        cut = lanes(q)
        for a in range(2):
            out = stitch[a][0] * act[0] + stitch[a][1] * act[1]
            stbuf[s, a] = out.astype(BF16)
            sq_ref[1] = sq_ref[1] + fold(out * out * valid)
            for b in range(2):
                gs_ref[k, a, b] = gs_ref[k, a, b] + fold(up[a] * act[b])
        for t in range(2):
            sq_ref[0] = sq_ref[0] + fold(pre[t] * pre[t] * valid)
            grad = stitch[0][t] * up[0] + stitch[1][t] * up[1]
            grad = jnp.where(pre[t] > 0, grad, 0.0).astype(BF16)
            gfull[k % 2, t, y, x, core, :, cut] = grad
            gb_ref[k, t] = gb_ref[k, t] + fold(grad.astype(F32))
        st_copy(q).start()

    def spread(q):
        wait_recv(ag1(q))

    def across(q):
        wait_recv(ag2(q))

    def terms(k, n):
        unit = width // 3
        for t, at, wide in (((0, 0, 2 * unit),), ((0, 2 * unit, unit), (1, 0, unit)), ((1, unit, 2 * unit),))[n]:
            value = jnp.dot(
                gfull[k % 2, t].reshape(8 * STEP, images),
                xb[0, t, :, at : at + wide],
                preferred_element_type=F32,
            )
            value = value.astype(BF16).reshape(planes, halves, STEP, wide)
            for d in range(planes):
                for e in range(halves):
                    zo[t, d, e, :, at : at + wide] = value[d, e]

    def chain(k, j):
        if j == planes - 2:

            @pl.when(k > 0)
            def _():
                gw_copy(k - 1).wait()

            def begin(i, carry):
                t, e = i // halves, i % halves
                zfin[t, e] = zo[t, z, e].astype(F32)
                return carry

            lax.fori_loop(0, towers * halves, begin, 0)
        for way in range(2):
            near = z if way == 0 else last - z
            source = (z - 1, row) if way == 0 else (z + 1, row)

            def freed():
                @pl.when(k + 1 < chunks)
                def _():
                    pl.semaphore_signal(
                        z_free.at[way, j - 1], inc=1, device_id=source, device_id_type=MESH
                    )

            if j <= planes - 2:

                @pl.when(near <= j)
                def _():
                    dest = last - j + z if way == 0 else j - last + z

                    @pl.when(k > 0)
                    def _():
                        z_copy(k - 1, j, way).wait_send()

                    if j > 0:

                        @pl.when(near >= 1)
                        def _():
                            z_copy(k, j - 1, way).wait_recv()

                            def add(i, carry):
                                t, e = i // halves, i % halves
                                value = zo[t, dest, e].astype(F32) + zrecv[way, j - 1, t, e].astype(F32)
                                zsend[way, j, t, e] = value.astype(BF16)
                                return carry

                            lax.fori_loop(0, towers * halves, add, 0)
                            freed()

                        @pl.when(near == 0)
                        def _():
                            zsend[way, j] = zo[:, dest]

                    else:
                        zsend[way, j] = zo[:, dest]

                    @pl.when(k > 0)
                    def _():
                        pl.semaphore_wait(z_free.at[way, j], 1)

                    z_copy(k, j, way).start()

            else:

                @pl.when(near >= 1)
                def _():
                    z_copy(k, j - 1, way).wait_recv()

                    def more(i, carry):
                        t, e = i // halves, i % halves
                        zfin[t, e] = zfin[t, e] + zrecv[way, j - 1, t, e].astype(F32)
                        return carry

                    lax.fori_loop(0, towers * halves, more, 0)
                    freed()

        if j == planes - 1:
            gw_copy(k).start()

    def prepare(g):
        g_load(g).start()

        @pl.when(g % per_chunk == 0)
        def _():
            start(wg_load(g))

        @pl.when((g >= 2) & (g - 2 < (pairs - 1) * tiles))
        def _():
            acc_out(g - 2).wait()

        @pl.when(g >= tiles)
        def _():
            acc_in(g).start()

    def tile(g):
        g_load(g).wait()

        @pl.when(g % per_chunk == 0)
        def _():
            for c in wg_load(g):
                c.wait()

        value = jnp.dot(
            wgx[...], gtile[g % 2].reshape(16 * STEP, IMAGES), preferred_element_type=F32
        )

        @pl.when(g < tiles)
        def _():
            acc[g % 2] = value

        @pl.when(g >= tiles)
        def _():
            acc_in(g).wait()
            acc[g % 2] = acc[g % 2] + value

        @pl.when(g < (pairs - 1) * tiles)
        def _():
            acc_out(g).start()

        @pl.when(g >= (pairs - 1) * tiles)
        def _():
            @pl.when(g >= (pairs - 1) * tiles + 2)
            def _():
                gx_out(g - 2).wait()

            keep = (1.0 - image_ref[lanes(g), 0:1] * pad_row_ref[...]).astype(BF16)
            gout[g % 2] = jnp.transpose(acc[g % 2].astype(BF16)) * keep
            gx_out(g).start()

    def sums(n):
        if n == 0:
            scur[0] = jnp.zeros_like(scur[0])
            scur[0, 0:1] = fold(usq_ref[...])
            scur[0, 1:2] = jnp.sum(sq_ref[0], axis=0, keepdims=True)
            scur[0, 2:3] = jnp.sum(sq_ref[1], axis=0, keepdims=True)
            scur[0, 3:4] = fold(sum(valid_ref[i] for i in range(per_chunk)))
            for k in range(chunks):
                at = k * 6 * STEP
                stats[z, :, at : at + 2 * STEP] = lane_sums(gb_ref[k].reshape(2 * STEP, 128))
                stats[z, :, at + 2 * STEP : at + 6 * STEP] = lane_sums(gs_ref[k].reshape(4 * STEP, 128))
        else:
            in_plane(n - 1).wait()
            value = scur[n - 1] + srecv[n - 1]
            if n < 3:
                scur[n] = value
            else:
                stats[z, :, chunks * 6 * STEP :] = value
        if n < 3:
            in_plane(n).start()
        else:
            for off in range(1, planes):
                to_plane(off).start()

    start(w_local(0))
    for i in range(per_chunk):
        x_local(i).start()
    for i in range(per_chunk):
        cut = slice(i * IMAGES, (i + 1) * IMAGES)
        valid = valid_in[:, cut].astype(F32)
        small = jnp.where(class_in[:, cut] == 195, 1.0, 0.0)
        valid_ref[i] = valid
        both = jnp.concatenate(
            [jnp.broadcast_to(small, (64, IMAGES)), jnp.broadcast_to(valid, (64, IMAGES))], axis=0
        )
        image_ref[cut] = jnp.transpose(both)
    mix = jnp.concatenate(
        [bias_in[...], stitch_in[0], stitch_in[1], jnp.zeros((122, mine), F32)], axis=0
    )
    mix_ref[...] = jnp.transpose(mix).reshape(chunks, STEP, 128)
    pl.semaphore_wait(barrier, 2 + planes)
    start(w_remote(0))

    def send_x(i, carry):
        x_remote(i).start()
        return carry

    lax.fori_loop(0, per_chunk, send_x, 0)
    gb_ref[...] = jnp.zeros_like(gb_ref)
    gs_ref[...] = jnp.zeros_like(gs_ref)
    sq_ref[...] = jnp.zeros_like(sq_ref)
    usq_ref[...] = jnp.zeros_like(usq_ref)

    ready = per_chunk - 1 + 5
    offsets = [2 + 3 * j for j in range(planes)]
    ends = [2 + 5 * j for j in range(planes)]
    first = per_chunk + 3

    def body(s, carry):
        stage(s, forward, rs1, rs1)
        stage(s - 1, reduce, rs2, rs2)
        stage(s - 2, pointwise, ag1, ag1)
        stage(s - 3, spread, ag2, ag2)
        stage(s - 4, across, cx, cx)

        @pl.when((s >= 5) & (s < total + 5))
        def _():
            wait_recv(cx(s - 5))

        for n in range(4):

            @pl.when(s == total + 2 + n)
            def _():
                sums(n)

        @pl.when(s >= ready)
        def _():
            done = s - ready
            k = done // per_chunk
            at = done % per_chunk

            def step(j):
                since = done - offsets[j]
                usual = (since >= 0) & (since % per_chunk == 0) & (since // per_chunk < chunks - 1)
                final = done == (chunks - 1) * per_chunk + ends[j]

                @pl.when(usual | final)
                def _():
                    chain(jnp.where(final, chunks - 1, since // per_chunk), j)

            for j in range(1, planes):
                step(j)
            for n in range(3):

                @pl.when((at == n) & (k < chunks))
                def _():
                    if n == 0:
                        g_copy(k).start()
                    terms(k, n)
                    if n == 2:
                        g_copy(k).wait()

            step(0)
            g = done - first

            @pl.when((g >= 0) & (g < pairs * tiles))
            def _():
                tile(g)

            @pl.when((g >= -1) & (g < pairs * tiles - 1))
            def _():
                prepare(g + 1)

        return carry

    lax.fori_loop(0, ready + max((chunks - 1) * per_chunk + ends[-1], first + pairs * tiles - 1) + 1, body, 0)

    def drain(q, carry):
        st_copy(q).wait()
        return carry

    lax.fori_loop(total - SLOTS, total, drain, 0)

    def drain_x(i, carry):
        x_remote(i).wait_send()
        return carry

    lax.fori_loop(0, per_chunk, drain_x, 0)
    for g in (pairs * tiles - 2, pairs * tiles - 1):
        gx_out(g).wait()
    gw_copy(chunks - 1).wait()
    for way in range(2):
        near = z if way == 0 else last - z
        for j in range(planes - 1):

            @pl.when(near <= j)
            def _():
                z_copy(chunks - 1, j, way).wait_send()

    for off in range(1, planes):
        to_plane(off).wait_send()
        from_plane(off).wait_recv()
    every = sum(stats[d] for d in range(planes))
    for k in range(chunks):
        for n in range(6):
            at = (k * 6 + n) * STEP
            value = every[0:1, at : at + STEP]
            if n < 2:
                bias_out[n : n + 1, k * STEP : (k + 1) * STEP] = value
            else:
                stitch_out[(n - 2) // 2, n % 2 : n % 2 + 1, k * STEP : (k + 1) * STEP] = value
    ends = jnp.sum(every[:, chunks * 6 * STEP :], axis=1, keepdims=True)
    images_in = ends[3:4] / lax.axis_size("rows")
    for n, size in enumerate((F, C, C)):
        rms_out[n : n + 1] = jnp.broadcast_to(jnp.sqrt(ends[n : n + 1] / (images_in * 2 * size)), (1, 128))


def put_out(st_ref, gx_ref, gw_ref, st_out, gx_out, gw_out):
    st_out[...] = st_ref[...]
    gx_out[...] = gx_ref[...]
    gw_out[0] = jnp.transpose(gw_ref[0])


def results(stitched, grad_inputs, grad_weights):
    towers, width = grad_weights.shape[0], grad_weights.shape[2]
    mine = grad_weights.shape[1]
    each = mine // 128
    steps = towers * each
    flat = [v.reshape(-1, v.shape[-1]) for v in (stitched, grad_inputs)]
    plain = [pl.BlockSpec((v.shape[0] // steps, v.shape[1]), lambda i: (i, 0)) for v in flat]
    out = pl.pallas_call(
        put_out,
        grid=(steps,),
        out_shape=(
            *(jax.ShapeDtypeStruct(v.shape, v.dtype) for v in flat),
            jax.ShapeDtypeStruct((towers, width, mine), F32),
        ),
        in_specs=[*plain, pl.BlockSpec((1, 128, width), lambda i: (i // each, i % each, 0))],
        out_specs=[*plain, pl.BlockSpec((1, width, 128), lambda i: (i // each, 0, i % each))],
        name="results",
    )(*flat, grad_weights)
    return out[0].reshape(stitched.shape), out[1].reshape(grad_inputs.shape), out[2]


def fused(inputs, weights, bias, stitch, cotangent, valid, size_class):
    planes = lax.axis_size("dp")
    towers, images, width = inputs.shape
    mine = bias.shape[1]
    chunks = mine // STEP
    per_chunk = images // IMAGES
    halves = 8 // planes
    tiles = towers * per_chunk
    place = np.arange(width) % 36
    padded = ((place // 6 == 5) | (place % 6 == 5)).astype(np.float32)
    many = chunks * 6 * STEP + 128
    vmem = pl.BlockSpec(memory_space=pltpu.VMEM)
    hbm = pl.BlockSpec(memory_space=pl.ANY)
    dma = pltpu.SemaphoreType.DMA
    stitched, grad_inputs, grad_weights, grad_bias, grad_stitch, means, _, _ = pl.pallas_call(
        functools.partial(kernel, planes),
        out_shape=(
            jax.ShapeDtypeStruct((2, chunks, STEP, images), BF16),
            jax.ShapeDtypeStruct((towers, images, width), BF16),
            jax.ShapeDtypeStruct((2, halves, chunks, STEP, width), F32),
            jax.ShapeDtypeStruct((2, mine), F32),
            jax.ShapeDtypeStruct((2, 2, mine), F32),
            jax.ShapeDtypeStruct((8, 128), F32),
            jax.ShapeDtypeStruct((2, 2, 2, 2, chunks, STEP, images), BF16),
            jax.ShapeDtypeStruct((tiles, width, IMAGES), F32),
        ),
        in_specs=[hbm] * 3 + [vmem] * 5,
        out_specs=(hbm, hbm, hbm, vmem, vmem, vmem, hbm, hbm),
        scratch_shapes=[
            pltpu.VMEM((images, 128), F32),
            pltpu.VMEM((per_chunk, 1, IMAGES), F32),
            pltpu.VMEM((chunks, STEP, 128), F32),
            pltpu.VMEM((2, towers, images, width), BF16),
            pltpu.VMEM((2, towers, 4, width, 2 * STEP), BF16),
            pltpu.VMEM((2, towers, 2, 4, STEP, width), BF16),
            pltpu.VMEM((SLOTS, 2, 2, towers, STEP, IMAGES), F32),
            pltpu.VMEM((SLOTS, 2, 2, WORDS, IMAGES), jnp.int32),
            pltpu.VMEM((SLOTS, 2, WORDS, IMAGES), jnp.int32),
            pltpu.VMEM((SLOTS, 2, 2, WORDS, IMAGES), jnp.int32),
            pltpu.VMEM((SLOTS, 2, WORDS, IMAGES), jnp.int32),
            pltpu.VMEM((2, towers, 2, 2, 2, STEP, images), BF16),
            pltpu.VMEM((SLOTS, 2, STEP, IMAGES), BF16),
            pltpu.VMEM((SLOTS, 2, STEP, IMAGES), BF16),
            pltpu.VMEM((towers, planes, halves, STEP, width), BF16),
            pltpu.VMEM((2, planes - 1, towers, halves, STEP, width), BF16),
            pltpu.VMEM((2, planes - 1, towers, halves, STEP, width), BF16),
            pltpu.VMEM((towers, halves, STEP, width), F32),
            pltpu.VMEM((chunks, 2, STEP, 128), F32),
            pltpu.VMEM((chunks, 2, 2, STEP, 128), F32),
            pltpu.VMEM((2, STEP, 128), F32),
            pltpu.VMEM((1, width), F32),
            pltpu.VMEM((width, 16 * STEP), BF16),
            pltpu.VMEM((2, 2, 2, 2, 2, STEP, IMAGES), BF16),
            pltpu.VMEM((2, width, IMAGES), F32),
            pltpu.VMEM((2, IMAGES, width), BF16),
            pltpu.VMEM((3, 8, 128), F32),
            pltpu.VMEM((3, 8, 128), F32),
            pltpu.VMEM((planes, 8, many), F32),
            dma((per_chunk,)),
            dma((per_chunk,)),
            dma((per_chunk,)),
            dma((4,)),
            dma((4,)),
            dma((4,)),
            dma((SLOTS, 2)),
            dma((SLOTS, 2)),
            dma((SLOTS, 2)),
            dma((SLOTS, 2)),
            dma((SLOTS, 2)),
            dma((SLOTS, 2)),
            dma((SLOTS, 2)),
            dma((SLOTS, 2)),
            dma((SLOTS,)),
            dma((SLOTS,)),
            dma((SLOTS,)),
            dma((SLOTS,)),
            dma((2,)),
            dma((2, planes - 1)),
            dma((2, planes - 1)),
            dma,
            pltpu.SemaphoreType.REGULAR((2, planes - 1)),
            dma((8,)),
            dma((2,)),
            dma((2,)),
            dma((2,)),
            dma((2,)),
            dma((3,)),
            dma((3,)),
            dma((planes - 1,)),
            dma((planes - 1,)),
        ],
        compiler_params=pltpu.CompilerParams(
            collective_id=0, has_side_effects=True, vmem_limit_bytes=67043328
        ),
        name="towers",
    )(
        inputs,
        weights,
        cotangent.reshape(2, chunks, STEP, images),
        valid[None, :],
        size_class[None, :],
        padded[None, :],
        bias,
        stitch,
    )
    stitched, grad_inputs, grad_weights = results(
        stitched.reshape(2, mine, images), grad_inputs, grad_weights.reshape(towers, -1, width)
    )
    return (stitched, grad_inputs, grad_weights, grad_bias, grad_stitch, means[:3, 0])


def rms(totals):
    count = totals[3] / lax.axis_size("rows")
    return jnp.sqrt(
        jnp.stack(
            [totals[0] / (count * 2 * F), totals[1] / (count * 2 * C), totals[2] / (count * 2 * C)]
        )
    )


def line_sum(own, up):
    size = lax.axis_size("dp")
    here = lax.axis_index("dp")
    got = None
    for step in range(size - 1):
        dest = size - 1 - step + here if up else step - (size - 1) + here
        dest = jnp.clip(dest, 0, size - 1)
        term = lax.dynamic_index_in_dim(own, dest, 0, keepdims=False)
        if got is not None:
            term = (term.astype(jnp.float32) + got.astype(jnp.float32)).astype(jnp.bfloat16)
        pairs = [(z, z + 1) for z in range(step + 1)]
        if not up:
            pairs = [(size - 1 - a, size - 1 - b) for a, b in pairs]
        got = lax.ppermute(term, "dp", pairs)
    return got


def plain(inputs, weights, bias, stitch, cotangent, valid, size_class):
    rows = lax.axis_size("rows")
    size = lax.axis_size("dp")
    here = lax.axis_index("dp")
    width = inputs.shape[2]
    mine = bias.shape[1]
    step = min(BLOCK, mine)
    blocks = mine // step
    place = lax.iota(jnp.int32, width) % 36
    padded = (place // 6 == 5) | (place % 6 == 5)
    dropped = (size_class == 195)[:, None] & padded[None, :]
    used = jnp.where(dropped[None], jnp.zeros((), jnp.bfloat16), inputs)
    split = weights.reshape(2, width, rows, mine)
    weight_valid = valid.astype(jnp.float32)
    pieces, stitched, grad_bias, grad_stitch, square_pre, square_out = [], [], [], [], [], []
    grad_weights = []
    mats = [split[:, :, :, k * step : (k + 1) * step] for k in range(blocks)]
    sums = []
    for k in range(blocks):
        part = jnp.einsum("tfrc,tbf->rctb", mats[k], used, preferred_element_type=jnp.float32)
        sums.append(
            lax.psum_scatter(part.reshape(rows * step, 2, -1), "rows", scatter_dimension=0, tiled=True)
        )
    for k in range(blocks):
        cut = slice(k * step, (k + 1) * step)
        pre = jnp.transpose(sums[k], (1, 0, 2)) + bias[:, cut, None]
        act = jax.nn.relu(pre)
        mix = stitch[:, :, cut, None]
        out = jnp.sum(mix * act[None], axis=1)
        stitched.append(out.astype(jnp.bfloat16))
        upstream = cotangent[:, cut].astype(jnp.float32) * weight_valid[None, None, :]
        grad_act = jnp.sum(mix * upstream[:, None], axis=0)
        grad_pre = jnp.where(pre > 0, grad_act, 0.0).astype(jnp.bfloat16)
        grad_bias.append(jnp.sum(grad_pre.astype(jnp.float32), axis=2))
        grad_stitch.append(jnp.sum(upstream[:, None] * act[None], axis=3))
        square_pre.append(jnp.sum(weight_valid[None, None, :] * pre * pre))
        square_out.append(jnp.sum(weight_valid[None, None, :] * out * out))
        piece = lax.all_gather(grad_pre, "rows", axis=0)
        pieces.append(piece)
        block = jnp.einsum("tbf,rtcb->rtfc", used, piece, preferred_element_type=jnp.float32)
        block = block.reshape(size, rows // size, 2, width, step)
        own = block.astype(jnp.bfloat16)
        total = lax.dynamic_index_in_dim(block, here, 0, keepdims=False)
        total = total + line_sum(own, True).astype(jnp.float32) + line_sum(own, False).astype(jnp.float32)
        grad_weights.append(total)
    total_x = sum(
        jnp.einsum("rtcb,tfrc->tbf", pieces[k], mats[k], preferred_element_type=jnp.float32)
        for k in range(blocks)
    )
    grad_inputs = jnp.where(dropped[None], 0.0, total_x).astype(jnp.bfloat16)
    grad_weights = jnp.stack(grad_weights, axis=0)
    grad_weights = jnp.transpose(grad_weights, (2, 3, 1, 0, 4)).reshape(2, width, -1)
    stitched = jnp.concatenate(stitched, axis=1)
    grad_bias = jnp.concatenate(grad_bias, axis=1)
    grad_stitch = jnp.concatenate(grad_stitch, axis=2)
    used_wide = used.astype(jnp.float32)
    partial_value = jnp.stack(
        [
            jnp.sum(weight_valid[None, :, None] * used_wide * used_wide),
            sum(square_pre),
            sum(square_out),
            jnp.sum(weight_valid),
        ]
    )
    grad_bias, grad_stitch = lax.psum((grad_bias, grad_stitch), "dp")
    totals = lax.psum(partial_value, ("dp", "rows"))
    return (stitched, grad_inputs, grad_weights, grad_bias, grad_stitch, rms(totals))


def small_plane(mesh):
    return mesh.shape["rows"] == 8 and mesh.shape["dp"] in (2, 4, 8)


def solution(mesh):
    in_specs = (
        P(None, "dp", "rows"),
        P(None, "rows", None),
        P(None, "rows"),
        P(None, None, "rows"),
        P(None, "rows", "dp"),
        P("dp"),
        P("dp"),
    )
    out_specs = (
        P(None, "rows", "dp"),
        P(None, "dp", "rows"),
        P(None, "rows", "dp"),
        P(None, "rows"),
        P(None, None, "rows"),
        P(),
    )
    return jax.shard_map(
        fused if small_plane(mesh) else plain, mesh=mesh, in_specs=in_specs, out_specs=out_specs, check_vma=False
    )
```

```python
import functools

import jax
import jax.numpy as jnp
import numpy as np
from jax import lax
from jax.experimental import pallas as pl
from jax.experimental.pallas import tpu as pltpu
from jax.sharding import PartitionSpec as P

F = 9216
C = 4096
BLOCK = 128
STEP = 64
IMAGES = 256
SLOTS = 4
HELD = 3
EACH = 6
WORDS = 40
TOP = 2.0**18 - 2.0
F32 = jnp.float32
BF16 = jnp.bfloat16
MESH = pl.DeviceIdType.MESH


def fold(value):
    return sum(value[:, i : i + 128] for i in range(0, value.shape[1], 128))


def lane_sums(value):
    ones = jnp.ones((8, 128), F32)
    return lax.dot_general(
        ones, value, (((1,), (1,)), ((), ())), precision=lax.Precision.HIGHEST, preferred_element_type=F32
    )


def pack(value):
    tiles = [value[8 * i : 8 * i + 8] for i in range(8)]
    top = jnp.abs(tiles[0])
    for v in tiles[1:]:
        top = jnp.maximum(top, jnp.abs(v))
    exponent = jnp.floor(jnp.log2(jnp.maximum(top, 2.0**-60))) + 1.0
    scale = jnp.exp2(-exponent) * TOP
    q = [jnp.round(v * scale).astype(jnp.int32) for v in tiles]
    low = [v & 0x1FFF for v in q[5:]]
    high = [(v >> 13) & 0x3F for v in q[5:]]
    words = [
        (q[0] << 13) | low[0],
        (q[1] << 13) | low[1],
        (q[2] << 13) | low[2],
        (q[3] << 13) | high[0] | (high[1] << 6),
        (q[4] << 13) | high[2] | ((exponent.astype(jnp.int32) & 0x7F) << 6),
    ]
    return jnp.concatenate(words, axis=0)


def unpack(words):
    w = [words[8 * i : 8 * i + 8] for i in range(5)]
    exponent = (w[4] << 19) >> 25
    scale = jnp.exp2(exponent.astype(F32)) * (1.0 / TOP)
    q = [v >> 13 for v in w]
    q.append(((w[3] << 26) >> 26 << 13) | (w[0] & 0x1FFF))
    q.append(((w[3] << 20) >> 26 << 13) | (w[1] & 0x1FFF))
    q.append(((w[4] << 26) >> 26 << 13) | (w[2] & 0x1FFF))
    return jnp.concatenate([v.astype(F32) * scale for v in q], axis=0)


def kernel(
    planes,
    x_hbm,
    w_hbm,
    cot_hbm,
    valid_in,
    class_in,
    pad_row_ref,
    bias_in,
    stitch_in,
    st_hbm,
    gx_hbm,
    gw_hbm,
    bias_out,
    stitch_out,
    rms_out,
    g_hbm,
    acc_hbm,
    image_ref,
    valid_ref,
    mix_ref,
    xb,
    raw,
    wt,
    part,
    p1,
    p2,
    r1,
    r2,
    gfull,
    cbuf,
    stbuf,
    zo,
    zsend,
    zrecv,
    zfin,
    gb_ref,
    gs_ref,
    sq_ref,
    usq_ref,
    wgx,
    gtile,
    acc,
    gout,
    scur,
    srecv,
    stats,
    x_sem,
    xs_sem,
    xr_sem,
    wo_sem,
    ws_sem,
    wr_sem,
    rs1_s,
    rs1_r,
    rs2_s,
    rs2_r,
    ag1_s,
    ag1_r,
    ag2_s,
    ag2_r,
    cx_s,
    cx_r,
    c_sem,
    st_sem,
    g_sem,
    z_s,
    z_r,
    zf_sem,
    z_free,
    wg_sem,
    gt_sem,
    ai_sem,
    ao_sem,
    go_sem,
    sc_s,
    sc_r,
    zs_s,
    zs_r,
):
    towers, images, width = x_hbm.shape
    chunks = cot_hbm.shape[1]
    pairs = chunks // 2
    mine = chunks * STEP
    per_chunk = images // IMAGES
    total = chunks * per_chunk
    tiles = towers * per_chunk
    last = planes - 1
    halves = 8 // planes

    z = lax.axis_index("dp")
    row = lax.axis_index("rows")
    y = row // 4
    x = (row // 2) % 2
    core = row % 2
    oy, ox, oc = 1 - y, 1 - x, 1 - core
    to_x = (z, y * 4 + ox * 2 + core)
    to_y = (z, oy * 4 + x * 2 + core)
    to_core = (z, y * 4 + x * 2 + oc)

    barrier = pltpu.get_barrier_semaphore()
    for there in (to_x, to_y, to_core):
        pl.semaphore_signal(barrier, inc=1, device_id=there, device_id_type=MESH)
    for off in range(1, planes):
        pl.semaphore_signal(barrier, inc=1, device_id=((z + off) % planes, row), device_id_type=MESH)

    def remote(src, dst, send, recv, there):
        return pltpu.make_async_remote_copy(
            src_ref=src, dst_ref=dst, send_sem=send, recv_sem=recv, device_id=there, device_id_type=MESH
        )

    def lanes(q):
        return pl.ds(pl.multiple_of((q % per_chunk) * IMAGES, IMAGES), IMAGES)

    def x_local(i):
        cut = pl.ds(i * IMAGES, IMAGES)
        return pltpu.make_async_copy(x_hbm.at[:, cut], xb.at[0, :, cut], x_sem.at[i])

    def x_remote(i):
        cut = pl.ds(i * IMAGES, IMAGES)
        return remote(x_hbm.at[:, cut], xb.at[1, :, cut], xs_sem.at[i], xr_sem.at[i], to_core)

    def w_lanes(owner, p):
        return pl.ds(pl.multiple_of(owner * mine + p * 2 * STEP, 2 * STEP), 2 * STEP)

    def w_local(p):
        return [
            pltpu.make_async_copy(w_hbm.at[:, :, w_lanes(c * 2 + core, p)], raw.at[0, :, c], wo_sem.at[c])
            for c in range(4)
        ]

    def w_remote(p):
        return [
            remote(
                w_hbm.at[:, :, w_lanes(c * 2 + oc, p)], raw.at[1, :, c], ws_sem.at[c], wr_sem.at[c], to_core
            )
            for c in range(4)
        ]

    def rs1(q):
        s = q % SLOTS
        return (
            remote(p1.at[s, 0], r1.at[s, 0], rs1_s.at[s, 0], rs1_r.at[s, 0], to_x),
            remote(p1.at[s, 1], r1.at[s, 1], rs1_s.at[s, 1], rs1_r.at[s, 1], to_y),
        )

    def rs2(q):
        s = q % SLOTS
        return (
            remote(p2.at[s, 0], r2.at[s, 0], rs2_s.at[s, 0], rs2_r.at[s, 0], to_y),
            remote(p2.at[s, 1], r2.at[s, 1], rs2_s.at[s, 1], rs2_r.at[s, 1], to_x),
        )

    def ag1(q):
        s, c, cut = q % SLOTS, (q // per_chunk) % 2, lanes(q)
        a = gfull.at[c, 0, y, x, core, :, cut]
        b = gfull.at[c, 1, y, x, core, :, cut]
        return (
            remote(a, a, ag1_s.at[s, 0], ag1_r.at[s, 0], to_x),
            remote(b, b, ag1_s.at[s, 1], ag1_r.at[s, 1], to_y),
        )

    def ag2(q):
        s, c, cut = q % SLOTS, (q // per_chunk) % 2, lanes(q)
        a = gfull.at[c, 0, y, :, core, :, cut]
        b = gfull.at[c, 1, :, x, core, :, cut]
        return (
            remote(a, a, ag2_s.at[s, 0], ag2_r.at[s, 0], to_y),
            remote(b, b, ag2_s.at[s, 1], ag2_r.at[s, 1], to_x),
        )

    def cx(q):
        s, c, cut = q % SLOTS, (q // per_chunk) % 2, lanes(q)
        a = gfull.at[c, :, :, :, core, :, cut]
        return (remote(a, a, cx_s.at[s], cx_r.at[s], to_core),)

    def cot_copy(q):
        s = q % SLOTS
        return pltpu.make_async_copy(cot_hbm.at[:, q // per_chunk, :, lanes(q)], cbuf.at[s], c_sem.at[s])

    def st_copy(q):
        s = q % SLOTS
        return pltpu.make_async_copy(stbuf.at[s], st_hbm.at[:, q // per_chunk, :, lanes(q)], st_sem.at[s])

    def g_copy(k):
        return pltpu.make_async_copy(gfull.at[k % 2], g_hbm.at[:, :, :, :, k], g_sem.at[k % 2])

    def gw_copy(k):
        return pltpu.make_async_copy(zfin, gw_hbm.at[:, :, k], zf_sem)

    def z_copy(k, j, way):
        there = (z + 1, row) if way == 0 else (z - 1, row)
        return remote(zsend.at[way, j], zrecv.at[way, j], z_s.at[way, j], z_r.at[way, j], there)

    def wg_load(g):
        p, t = g // tiles, (g % tiles) // per_chunk
        return [
            pltpu.make_async_copy(w_hbm.at[t, :, w_lanes(r, p)], wgx.at[:, pl.ds(r * 128, 128)], wg_sem.at[r])
            for r in range(8)
        ]

    def g_load(g):
        p, t, i = g // tiles, (g % tiles) // per_chunk, g % per_chunk
        return pltpu.make_async_copy(
            g_hbm.at[t, :, :, :, pl.ds(p * 2, 2), :, lanes(i)], gtile.at[g % HELD], gt_sem.at[g % HELD]
        )

    def acc_in(g):
        return pltpu.make_async_copy(acc_hbm.at[g % tiles], acc.at[g % HELD], ai_sem.at[g % HELD])

    def acc_out(g):
        return pltpu.make_async_copy(acc.at[g % HELD], acc_hbm.at[g % tiles], ao_sem.at[g % HELD])

    def gx_out(g):
        t = (g % tiles) // per_chunk
        return pltpu.make_async_copy(gout.at[g % 2], gx_hbm.at[t, lanes(g)], go_sem.at[g % 2])

    def in_plane(n):
        there = (to_x, to_y, to_core)[n]
        return remote(scur.at[n], srecv.at[n], sc_s.at[n], sc_r.at[n], there)

    def to_plane(off):
        there = ((z + off) % planes, row)
        return remote(stats.at[z], stats.at[z], zs_s.at[off - 1], zs_r.at[off - 1], there)

    def from_plane(off):
        there = ((z + off) % planes, row)
        held = stats.at[(z + planes - off) % planes]
        return remote(held, held, zs_s.at[off - 1], zs_r.at[off - 1], there)

    def start(copies):
        for c in copies:
            c.start()

    def wait_send(copies):
        for c in copies:
            c.wait_send()

    def wait_recv(copies):
        for c in copies:
            c.wait_recv()

    def stage(q, work, sends, *sent):
        @pl.when((q >= SLOTS) & (q < total + SLOTS))
        def _():
            for copies in sent:
                wait_send(copies(q - SLOTS))

        @pl.when((q >= 0) & (q < total))
        def _():
            work(q)
            start(sends(q))

    def turn(p):
        for c in w_local(p):
            c.wait()

        def one(n, carry):
            side, t, c = n // 8, (n // 4) % 2, n % 4
            turned = jnp.transpose(raw[side, t, c])
            wt[side, t, 0, c] = turned[:STEP]
            wt[side, t, 1, c] = turned[STEP:]
            return carry

        lax.fori_loop(0, 8, one, 0)
        wait_recv(w_remote(p))
        lax.fori_loop(8, 16, one, 0)

        @pl.when(p + 1 < pairs)
        def _():
            start(w_local(p + 1))

    def forward(q):
        k, i, s = q // per_chunk, q % per_chunk, q % SLOTS
        p, h = k // 2, k % 2

        cot_copy(q).start()

        @pl.when((i == 0) & (h == 0))
        def _():
            turn(p)

        @pl.when((i == 0) & (h == 1))
        def _():
            wait_send(w_remote(p))

            @pl.when(p + 1 < pairs)
            def _():
                start(w_remote(p + 1))

        cut = pl.ds(pl.multiple_of(i * IMAGES, IMAGES), IMAGES)

        @pl.when(k == 0)
        def _():
            x_local(i).wait()
            x_remote(i).wait_recv()
            keep = (1.0 - image_ref[cut, 0:1] * pad_row_ref[...]).astype(BF16)
            valid = image_ref[cut, 64:65]
            for t in range(towers):
                used = xb[0, t, cut] * keep
                xb[0, t, cut] = used
                used = used.astype(F32)
                usq_ref[...] = usq_ref[...] + jnp.sum(used * used * valid, axis=0, keepdims=True)
                xb[1, t, cut] = xb[1, t, cut] * keep

        for t in range(towers):
            out = lax.dot_general(
                wt[0, t, h].reshape(4 * STEP, width),
                xb[0, t, cut],
                (((1,), (1,)), ((), ())),
                preferred_element_type=F32,
            ) + lax.dot_general(
                wt[1, t, h].reshape(4 * STEP, width),
                xb[1, t, cut],
                (((1,), (1,)), ((), ())),
                preferred_element_type=F32,
            )
            out = out.reshape(2, 2, STEP, IMAGES)
            for a in range(2):
                for b in range(2):
                    part[s, a, b, t] = out[a, b]
        for a in range(2):
            p1[s, 0, a] = pack(part[s, a, ox, 0])
            p1[s, 1, a] = pack(part[s, oy, a, 1])

    def reduce(q):
        s = q % SLOTS
        wait_recv(rs1(q))
        p2[s, 0] = pack(part[s, oy, x, 0] + unpack(r1[s, 0, oy]))
        p2[s, 1] = pack(part[s, y, ox, 1] + unpack(r1[s, 1, ox]))
        part[s, y, x, 0] = part[s, y, x, 0] + unpack(r1[s, 0, y])
        part[s, y, x, 1] = part[s, y, x, 1] + unpack(r1[s, 1, x])

    def pointwise(q):
        k, i, s = q // per_chunk, q % per_chunk, q % SLOTS
        wait_recv(rs2(q))
        cot_copy(q).wait()

        @pl.when(q >= SLOTS)
        def _():
            st_copy(q - SLOTS).wait()

        valid = valid_ref[i]
        mix = mix_ref[k]
        bias = [mix[:, t : t + 1] for t in range(2)]
        stitch = [[mix[:, 2 + 2 * a + b : 3 + 2 * a + b] for b in range(2)] for a in range(2)]
        pre = [part[s, y, x, t] + unpack(r2[s, t]) + bias[t] for t in range(2)]
        act = [jnp.maximum(p, 0.0) for p in pre]
        up = [cbuf[s, t].astype(F32) * valid for t in range(2)]
        cut = lanes(q)
        for a in range(2):
            out = stitch[a][0] * act[0] + stitch[a][1] * act[1]
            stbuf[s, a] = out.astype(BF16)
            sq_ref[1] = sq_ref[1] + fold(out * out * valid)
            for b in range(2):
                gs_ref[k, a, b] = gs_ref[k, a, b] + fold(up[a] * act[b])
        for t in range(2):
            sq_ref[0] = sq_ref[0] + fold(pre[t] * pre[t] * valid)
            grad = stitch[0][t] * up[0] + stitch[1][t] * up[1]
            grad = jnp.where(pre[t] > 0, grad, 0.0).astype(BF16)
            gfull[k % 2, t, y, x, core, :, cut] = grad
            gb_ref[k, t] = gb_ref[k, t] + fold(grad.astype(F32))
        st_copy(q).start()

    def spread(q):
        wait_recv(ag1(q))

    def across(q):
        wait_recv(ag2(q))

    def terms(k, n):
        unit = width // 3
        for t, at, wide in (((0, 0, 2 * unit),), ((0, 2 * unit, unit), (1, 0, unit)), ((1, unit, 2 * unit),))[n]:
            value = jnp.dot(
                gfull[k % 2, t].reshape(8 * STEP, images),
                xb[0, t, :, at : at + wide],
                preferred_element_type=F32,
            )
            value = value.astype(BF16).reshape(planes, halves, STEP, wide)
            for d in range(planes):
                for e in range(halves):
                    zo[t, d, e, :, at : at + wide] = value[d, e]

    def chain(k, j):
        if j == planes - 2:

            @pl.when(k > 0)
            def _():
                gw_copy(k - 1).wait()

            def begin(i, carry):
                t, e = i // halves, i % halves
                zfin[t, e] = zo[t, z, e].astype(F32)
                return carry

            lax.fori_loop(0, towers * halves, begin, 0)
        for way in range(2):
            near = z if way == 0 else last - z
            source = (z - 1, row) if way == 0 else (z + 1, row)

            def freed():
                @pl.when(k + 1 < chunks)
                def _():
                    pl.semaphore_signal(
                        z_free.at[way, j - 1], inc=1, device_id=source, device_id_type=MESH
                    )

            if j <= planes - 2:

                @pl.when(near <= j)
                def _():
                    dest = last - j + z if way == 0 else j - last + z

                    @pl.when(k > 0)
                    def _():
                        z_copy(k - 1, j, way).wait_send()

                    if j > 0:

                        @pl.when(near >= 1)
                        def _():
                            z_copy(k, j - 1, way).wait_recv()

                            def add(i, carry):
                                t, e = i // halves, i % halves
                                value = zo[t, dest, e].astype(F32) + zrecv[way, j - 1, t, e].astype(F32)
                                zsend[way, j, t, e] = value.astype(BF16)
                                return carry

                            lax.fori_loop(0, towers * halves, add, 0)
                            freed()

                        @pl.when(near == 0)
                        def _():
                            zsend[way, j] = zo[:, dest]

                    else:
                        zsend[way, j] = zo[:, dest]

                    @pl.when(k > 0)
                    def _():
                        pl.semaphore_wait(z_free.at[way, j], 1)

                    z_copy(k, j, way).start()

            else:

                @pl.when(near >= 1)
                def _():
                    z_copy(k, j - 1, way).wait_recv()

                    def more(i, carry):
                        t, e = i // halves, i % halves
                        zfin[t, e] = zfin[t, e] + zrecv[way, j - 1, t, e].astype(F32)
                        return carry

                    lax.fori_loop(0, towers * halves, more, 0)
                    freed()

        if j == planes - 1:
            gw_copy(k).start()

    def prepare(g):
        g_load(g).start()

        @pl.when((g >= HELD) & (g - HELD < (pairs - 1) * tiles))
        def _():
            acc_out(g - HELD).wait()

        @pl.when(g >= tiles)
        def _():
            acc_in(g).start()

    def tile(g):
        g_load(g).wait()

        @pl.when(g % per_chunk == 0)
        def _():
            for c in wg_load(g):
                c.wait()

        value = jnp.dot(
            wgx[...], gtile[g % HELD].reshape(16 * STEP, IMAGES), preferred_element_type=F32
        )
        final = g >= (pairs - 1) * tiles

        @pl.when(g < tiles)
        def _():
            acc[g % HELD] = value

        @pl.when(g >= tiles)
        def _():
            acc_in(g).wait()
            acc[g % HELD] = acc[g % HELD] + value

        @pl.when(jnp.logical_not(final))
        def _():
            acc_out(g).start()

        @pl.when(final)
        def _():
            @pl.when(g >= (pairs - 1) * tiles + 2)
            def _():
                gx_out(g - 2).wait()

            keep = (1.0 - image_ref[lanes(g), 0:1] * pad_row_ref[...]).astype(BF16)
            gout[g % 2] = jnp.transpose(acc[g % HELD].astype(BF16)) * keep
            gx_out(g).start()

        @pl.when(((g + 1) % per_chunk == 0) & (g + 1 < pairs * tiles))
        def _():
            start(wg_load(g + 1))

        @pl.when(g + 2 < pairs * tiles)
        def _():
            prepare(g + 2)

    def sums(n):
        if n == 0:
            scur[0] = jnp.zeros_like(scur[0])
            scur[0, 0:1] = fold(usq_ref[...])
            scur[0, 1:2] = jnp.sum(sq_ref[0], axis=0, keepdims=True)
            scur[0, 2:3] = jnp.sum(sq_ref[1], axis=0, keepdims=True)
            scur[0, 3:4] = fold(sum(valid_ref[i] for i in range(per_chunk)))
            for k in range(chunks):
                at = k * 6 * STEP
                stats[z, :, at : at + 2 * STEP] = lane_sums(gb_ref[k].reshape(2 * STEP, 128))
                stats[z, :, at + 2 * STEP : at + 6 * STEP] = lane_sums(gs_ref[k].reshape(4 * STEP, 128))
        else:
            in_plane(n - 1).wait()
            value = scur[n - 1] + srecv[n - 1]
            if n < 3:
                scur[n] = value
            else:
                stats[z, :, chunks * 6 * STEP :] = value
        if n < 3:
            in_plane(n).start()
        else:
            for off in range(1, planes):
                to_plane(off).start()

    start(w_local(0))
    for i in range(per_chunk):
        x_local(i).start()
    for i in range(per_chunk):
        cut = slice(i * IMAGES, (i + 1) * IMAGES)
        valid = valid_in[:, cut].astype(F32)
        small = jnp.where(class_in[:, cut] == 195, 1.0, 0.0)
        valid_ref[i] = valid
        both = jnp.concatenate(
            [jnp.broadcast_to(small, (64, IMAGES)), jnp.broadcast_to(valid, (64, IMAGES))], axis=0
        )
        image_ref[cut] = jnp.transpose(both)
    mix = jnp.concatenate(
        [bias_in[...], stitch_in[0], stitch_in[1], jnp.zeros((122, mine), F32)], axis=0
    )
    mix_ref[...] = jnp.transpose(mix).reshape(chunks, STEP, 128)
    pl.semaphore_wait(barrier, 2 + planes)
    start(w_remote(0))

    def send_x(i, carry):
        x_remote(i).start()
        return carry

    lax.fori_loop(0, per_chunk, send_x, 0)
    gb_ref[...] = jnp.zeros_like(gb_ref)
    gs_ref[...] = jnp.zeros_like(gs_ref)
    sq_ref[...] = jnp.zeros_like(sq_ref)
    usq_ref[...] = jnp.zeros_like(usq_ref)

    ready = per_chunk - 1 + 5
    offsets = [2 + 3 * j for j in range(planes)]
    ends = [2 + 10 * j for j in range(planes)]
    first = per_chunk + 3
    late = (chunks - 1) * per_chunk + 3

    def body(s, carry):
        stage(s, forward, rs1, rs1)
        stage(s - 1, reduce, rs2, rs2)
        stage(s - 2, pointwise, ag1, ag1)
        stage(s - 3, spread, ag2, ag2)
        stage(s - 4, across, cx, cx)

        @pl.when((s >= 5) & (s < total + 5))
        def _():
            wait_recv(cx(s - 5))

        for n in range(4):

            @pl.when(s == total + 2 + n)
            def _():
                sums(n)

        @pl.when(s >= ready)
        def _():
            done = s - ready
            k = done // per_chunk
            at = done % per_chunk

            def step(j):
                since = done - offsets[j]
                usual = (since >= 0) & (since % per_chunk == 0) & (since // per_chunk < chunks - 1)
                final = done == (chunks - 1) * per_chunk + ends[j]

                @pl.when(usual | final)
                def _():
                    chain(jnp.where(final, chunks - 1, since // per_chunk), j)

            for j in range(1, planes):
                step(j)
            for n in range(3):

                @pl.when((at == n) & (k < chunks))
                def _():
                    if n == 0:
                        g_copy(k).start()
                    terms(k, n)
                    if n == 2:
                        g_copy(k).wait()

            step(0)
            @pl.when(done == first - 1)
            def _():
                start(wg_load(0))
                prepare(0)
                prepare(1)

            since = done - first
            usual = (since >= 0) & (since % per_chunk < 5) & (since // per_chunk < chunks - 2)
            g = jnp.where(
                done >= late,
                done - late + EACH * (chunks - 2),
                EACH * (since // per_chunk) + since % per_chunk,
            )

            @pl.when(usual | ((done >= late) & (g < pairs * tiles)))
            def _():
                tile(g)

            @pl.when(usual & (since % per_chunk == 4))
            def _():
                tile(g + 1)

        return carry

    left = pairs * tiles - EACH * (chunks - 2)
    lax.fori_loop(0, ready + max((chunks - 1) * per_chunk + ends[-1], late + left - 1) + 1, body, 0)

    def drain(q, carry):
        st_copy(q).wait()
        return carry

    lax.fori_loop(total - SLOTS, total, drain, 0)

    def drain_x(i, carry):
        x_remote(i).wait_send()
        return carry

    lax.fori_loop(0, per_chunk, drain_x, 0)
    for g in (pairs * tiles - 2, pairs * tiles - 1):
        gx_out(g).wait()
    gw_copy(chunks - 1).wait()
    for way in range(2):
        near = z if way == 0 else last - z
        for j in range(planes - 1):

            @pl.when(near <= j)
            def _():
                z_copy(chunks - 1, j, way).wait_send()

    for off in range(1, planes):
        to_plane(off).wait_send()
        from_plane(off).wait_recv()
    every = sum(stats[d] for d in range(planes))
    for k in range(chunks):
        for n in range(6):
            at = (k * 6 + n) * STEP
            value = every[0:1, at : at + STEP]
            if n < 2:
                bias_out[n : n + 1, k * STEP : (k + 1) * STEP] = value
            else:
                stitch_out[(n - 2) // 2, n % 2 : n % 2 + 1, k * STEP : (k + 1) * STEP] = value
    ends = jnp.sum(every[:, chunks * 6 * STEP :], axis=1, keepdims=True)
    images_in = ends[3:4] / lax.axis_size("rows")
    for n, size in enumerate((F, C, C)):
        rms_out[n : n + 1] = jnp.broadcast_to(jnp.sqrt(ends[n : n + 1] / (images_in * 2 * size)), (1, 128))


def put_out(st_ref, gx_ref, gw_ref, st_out, gx_out, gw_out):
    st_out[...] = st_ref[...]
    gx_out[...] = gx_ref[...]
    gw_out[0] = jnp.transpose(gw_ref[0])


def results(stitched, grad_inputs, grad_weights):
    towers, width = grad_weights.shape[0], grad_weights.shape[2]
    mine = grad_weights.shape[1]
    block = min(mine, 512)
    each = mine // block
    steps = towers * each
    flat = [v.reshape(-1, v.shape[-1]) for v in (stitched, grad_inputs)]
    plain = [pl.BlockSpec((v.shape[0] // steps, v.shape[1]), lambda i: (i, 0)) for v in flat]
    out = pl.pallas_call(
        put_out,
        grid=(steps,),
        out_shape=(
            *(jax.ShapeDtypeStruct(v.shape, v.dtype) for v in flat),
            jax.ShapeDtypeStruct((towers, width, mine), F32),
        ),
        in_specs=[*plain, pl.BlockSpec((1, block, width), lambda i: (i // each, i % each, 0))],
        out_specs=[*plain, pl.BlockSpec((1, width, block), lambda i: (i // each, 0, i % each))],
        name="results",
    )(*flat, grad_weights)
    return out[0].reshape(stitched.shape), out[1].reshape(grad_inputs.shape), out[2]


def fused(inputs, weights, bias, stitch, cotangent, valid, size_class):
    planes = lax.axis_size("dp")
    towers, images, width = inputs.shape
    mine = bias.shape[1]
    chunks = mine // STEP
    per_chunk = images // IMAGES
    halves = 8 // planes
    tiles = towers * per_chunk
    place = np.arange(width) % 36
    padded = ((place // 6 == 5) | (place % 6 == 5)).astype(np.float32)
    many = chunks * 6 * STEP + 128
    vmem = pl.BlockSpec(memory_space=pltpu.VMEM)
    hbm = pl.BlockSpec(memory_space=pl.ANY)
    dma = pltpu.SemaphoreType.DMA
    stitched, grad_inputs, grad_weights, grad_bias, grad_stitch, means, _, _ = pl.pallas_call(
        functools.partial(kernel, planes),
        out_shape=(
            jax.ShapeDtypeStruct((2, chunks, STEP, images), BF16),
            jax.ShapeDtypeStruct((towers, images, width), BF16),
            jax.ShapeDtypeStruct((2, halves, chunks, STEP, width), F32),
            jax.ShapeDtypeStruct((2, mine), F32),
            jax.ShapeDtypeStruct((2, 2, mine), F32),
            jax.ShapeDtypeStruct((8, 128), F32),
            jax.ShapeDtypeStruct((2, 2, 2, 2, chunks, STEP, images), BF16),
            jax.ShapeDtypeStruct((tiles, width, IMAGES), F32),
        ),
        in_specs=[hbm] * 3 + [vmem] * 5,
        out_specs=(hbm, hbm, hbm, vmem, vmem, vmem, hbm, hbm),
        scratch_shapes=[
            pltpu.VMEM((images, 128), F32),
            pltpu.VMEM((per_chunk, 1, IMAGES), F32),
            pltpu.VMEM((chunks, STEP, 128), F32),
            pltpu.VMEM((2, towers, images, width), BF16),
            pltpu.VMEM((2, towers, 4, width, 2 * STEP), BF16),
            pltpu.VMEM((2, towers, 2, 4, STEP, width), BF16),
            pltpu.VMEM((SLOTS, 2, 2, towers, STEP, IMAGES), F32),
            pltpu.VMEM((SLOTS, 2, 2, WORDS, IMAGES), jnp.int32),
            pltpu.VMEM((SLOTS, 2, WORDS, IMAGES), jnp.int32),
            pltpu.VMEM((SLOTS, 2, 2, WORDS, IMAGES), jnp.int32),
            pltpu.VMEM((SLOTS, 2, WORDS, IMAGES), jnp.int32),
            pltpu.VMEM((2, towers, 2, 2, 2, STEP, images), BF16),
            pltpu.VMEM((SLOTS, 2, STEP, IMAGES), BF16),
            pltpu.VMEM((SLOTS, 2, STEP, IMAGES), BF16),
            pltpu.VMEM((towers, planes, halves, STEP, width), BF16),
            pltpu.VMEM((2, planes - 1, towers, halves, STEP, width), BF16),
            pltpu.VMEM((2, planes - 1, towers, halves, STEP, width), BF16),
            pltpu.VMEM((towers, halves, STEP, width), F32),
            pltpu.VMEM((chunks, 2, STEP, 128), F32),
            pltpu.VMEM((chunks, 2, 2, STEP, 128), F32),
            pltpu.VMEM((2, STEP, 128), F32),
            pltpu.VMEM((1, width), F32),
            pltpu.VMEM((width, 16 * STEP), BF16),
            pltpu.VMEM((HELD, 2, 2, 2, 2, STEP, IMAGES), BF16),
            pltpu.VMEM((HELD, width, IMAGES), F32),
            pltpu.VMEM((2, IMAGES, width), BF16),
            pltpu.VMEM((3, 8, 128), F32),
            pltpu.VMEM((3, 8, 128), F32),
            pltpu.VMEM((planes, 8, many), F32),
            dma((per_chunk,)),
            dma((per_chunk,)),
            dma((per_chunk,)),
            dma((4,)),
            dma((4,)),
            dma((4,)),
            dma((SLOTS, 2)),
            dma((SLOTS, 2)),
            dma((SLOTS, 2)),
            dma((SLOTS, 2)),
            dma((SLOTS, 2)),
            dma((SLOTS, 2)),
            dma((SLOTS, 2)),
            dma((SLOTS, 2)),
            dma((SLOTS,)),
            dma((SLOTS,)),
            dma((SLOTS,)),
            dma((SLOTS,)),
            dma((2,)),
            dma((2, planes - 1)),
            dma((2, planes - 1)),
            dma,
            pltpu.SemaphoreType.REGULAR((2, planes - 1)),
            dma((8,)),
            dma((HELD,)),
            dma((HELD,)),
            dma((HELD,)),
            dma((2,)),
            dma((3,)),
            dma((3,)),
            dma((planes - 1,)),
            dma((planes - 1,)),
        ],
        compiler_params=pltpu.CompilerParams(
            collective_id=0, has_side_effects=True, vmem_limit_bytes=67043328
        ),
        name="towers",
    )(
        inputs,
        weights,
        cotangent.reshape(2, chunks, STEP, images),
        valid[None, :],
        size_class[None, :],
        padded[None, :],
        bias,
        stitch,
    )
    stitched, grad_inputs, grad_weights = results(
        stitched.reshape(2, mine, images), grad_inputs, grad_weights.reshape(towers, -1, width)
    )
    return (stitched, grad_inputs, grad_weights, grad_bias, grad_stitch, means[:3, 0])


def rms(totals):
    count = totals[3] / lax.axis_size("rows")
    return jnp.sqrt(
        jnp.stack(
            [totals[0] / (count * 2 * F), totals[1] / (count * 2 * C), totals[2] / (count * 2 * C)]
        )
    )


def line_sum(own, up):
    size = lax.axis_size("dp")
    here = lax.axis_index("dp")
    got = None
    for step in range(size - 1):
        dest = size - 1 - step + here if up else step - (size - 1) + here
        dest = jnp.clip(dest, 0, size - 1)
        term = lax.dynamic_index_in_dim(own, dest, 0, keepdims=False)
        if got is not None:
            term = (term.astype(jnp.float32) + got.astype(jnp.float32)).astype(jnp.bfloat16)
        pairs = [(z, z + 1) for z in range(step + 1)]
        if not up:
            pairs = [(size - 1 - a, size - 1 - b) for a, b in pairs]
        got = lax.ppermute(term, "dp", pairs)
    return got


def plain(inputs, weights, bias, stitch, cotangent, valid, size_class):
    rows = lax.axis_size("rows")
    size = lax.axis_size("dp")
    here = lax.axis_index("dp")
    width = inputs.shape[2]
    mine = bias.shape[1]
    step = min(BLOCK, mine)
    blocks = mine // step
    place = lax.iota(jnp.int32, width) % 36
    padded = (place // 6 == 5) | (place % 6 == 5)
    dropped = (size_class == 195)[:, None] & padded[None, :]
    used = jnp.where(dropped[None], jnp.zeros((), jnp.bfloat16), inputs)
    split = weights.reshape(2, width, rows, mine)
    weight_valid = valid.astype(jnp.float32)
    pieces, stitched, grad_bias, grad_stitch, square_pre, square_out = [], [], [], [], [], []
    grad_weights = []
    mats = [split[:, :, :, k * step : (k + 1) * step] for k in range(blocks)]
    sums = []
    for k in range(blocks):
        part = jnp.einsum("tfrc,tbf->rctb", mats[k], used, preferred_element_type=jnp.float32)
        sums.append(
            lax.psum_scatter(part.reshape(rows * step, 2, -1), "rows", scatter_dimension=0, tiled=True)
        )
    for k in range(blocks):
        cut = slice(k * step, (k + 1) * step)
        pre = jnp.transpose(sums[k], (1, 0, 2)) + bias[:, cut, None]
        act = jax.nn.relu(pre)
        mix = stitch[:, :, cut, None]
        out = jnp.sum(mix * act[None], axis=1)
        stitched.append(out.astype(jnp.bfloat16))
        upstream = cotangent[:, cut].astype(jnp.float32) * weight_valid[None, None, :]
        grad_act = jnp.sum(mix * upstream[:, None], axis=0)
        grad_pre = jnp.where(pre > 0, grad_act, 0.0).astype(jnp.bfloat16)
        grad_bias.append(jnp.sum(grad_pre.astype(jnp.float32), axis=2))
        grad_stitch.append(jnp.sum(upstream[:, None] * act[None], axis=3))
        square_pre.append(jnp.sum(weight_valid[None, None, :] * pre * pre))
        square_out.append(jnp.sum(weight_valid[None, None, :] * out * out))
        piece = lax.all_gather(grad_pre, "rows", axis=0)
        pieces.append(piece)
        block = jnp.einsum("tbf,rtcb->rtfc", used, piece, preferred_element_type=jnp.float32)
        block = block.reshape(size, rows // size, 2, width, step)
        own = block.astype(jnp.bfloat16)
        total = lax.dynamic_index_in_dim(block, here, 0, keepdims=False)
        total = total + line_sum(own, True).astype(jnp.float32) + line_sum(own, False).astype(jnp.float32)
        grad_weights.append(total)
    total_x = sum(
        jnp.einsum("rtcb,tfrc->tbf", pieces[k], mats[k], preferred_element_type=jnp.float32)
        for k in range(blocks)
    )
    grad_inputs = jnp.where(dropped[None], 0.0, total_x).astype(jnp.bfloat16)
    grad_weights = jnp.stack(grad_weights, axis=0)
    grad_weights = jnp.transpose(grad_weights, (2, 3, 1, 0, 4)).reshape(2, width, -1)
    stitched = jnp.concatenate(stitched, axis=1)
    grad_bias = jnp.concatenate(grad_bias, axis=1)
    grad_stitch = jnp.concatenate(grad_stitch, axis=2)
    used_wide = used.astype(jnp.float32)
    partial_value = jnp.stack(
        [
            jnp.sum(weight_valid[None, :, None] * used_wide * used_wide),
            sum(square_pre),
            sum(square_out),
            jnp.sum(weight_valid),
        ]
    )
    grad_bias, grad_stitch = lax.psum((grad_bias, grad_stitch), "dp")
    totals = lax.psum(partial_value, ("dp", "rows"))
    return (stitched, grad_inputs, grad_weights, grad_bias, grad_stitch, rms(totals))


def small_plane(mesh):
    return mesh.shape["rows"] == 8 and mesh.shape["dp"] in (2, 4, 8)


def solution(mesh):
    in_specs = (
        P(None, "dp", "rows"),
        P(None, "rows", None),
        P(None, "rows"),
        P(None, None, "rows"),
        P(None, "rows", "dp"),
        P("dp"),
        P("dp"),
    )
    out_specs = (
        P(None, "rows", "dp"),
        P(None, "dp", "rows"),
        P(None, "rows", "dp"),
        P(None, "rows"),
        P(None, None, "rows"),
        P(),
    )
    return jax.shard_map(
        fused if small_plane(mesh) else plain, mesh=mesh, in_specs=in_specs, out_specs=out_specs, check_vma=False
    )
```

```python
import functools

import jax
import jax.numpy as jnp
import numpy as np
from jax import lax
from jax.experimental import pallas as pl
from jax.experimental.pallas import tpu as pltpu
from jax.sharding import PartitionSpec as P

F = 9216
C = 4096
BLOCK = 128
STEP = 64
IMAGES = 256
SLOTS = 4
HELD = 3
EACH = 6
WORDS = 40
TOP = 2.0**18 - 2.0
F32 = jnp.float32
BF16 = jnp.bfloat16
MESH = pl.DeviceIdType.MESH


def fold(value):
    return sum(value[:, i : i + 128] for i in range(0, value.shape[1], 128))


def lane_sums(value):
    ones = jnp.ones((8, 128), F32)
    return lax.dot_general(
        ones, value, (((1,), (1,)), ((), ())), precision=lax.Precision.HIGHEST, preferred_element_type=F32
    )


def pack(value):
    tiles = [value[8 * i : 8 * i + 8] for i in range(8)]
    top = jnp.abs(tiles[0])
    for v in tiles[1:]:
        top = jnp.maximum(top, jnp.abs(v))
    exponent = jnp.floor(jnp.log2(jnp.maximum(top, 2.0**-60))) + 1.0
    scale = jnp.exp2(-exponent) * TOP
    q = [jnp.round(v * scale).astype(jnp.int32) for v in tiles]
    low = [v & 0x1FFF for v in q[5:]]
    high = [(v >> 13) & 0x3F for v in q[5:]]
    words = [
        (q[0] << 13) | low[0],
        (q[1] << 13) | low[1],
        (q[2] << 13) | low[2],
        (q[3] << 13) | high[0] | (high[1] << 6),
        (q[4] << 13) | high[2] | ((exponent.astype(jnp.int32) & 0x7F) << 6),
    ]
    return jnp.concatenate(words, axis=0)


def unpack(words):
    w = [words[8 * i : 8 * i + 8] for i in range(5)]
    exponent = (w[4] << 19) >> 25
    scale = jnp.exp2(exponent.astype(F32)) * (1.0 / TOP)
    q = [v >> 13 for v in w]
    q.append(((w[3] << 26) >> 26 << 13) | (w[0] & 0x1FFF))
    q.append(((w[3] << 20) >> 26 << 13) | (w[1] & 0x1FFF))
    q.append(((w[4] << 26) >> 26 << 13) | (w[2] & 0x1FFF))
    return jnp.concatenate([v.astype(F32) * scale for v in q], axis=0)


def kernel(
    planes,
    x_hbm,
    w_hbm,
    cot_hbm,
    valid_in,
    class_in,
    pad_row_ref,
    bias_in,
    stitch_in,
    st_hbm,
    gx_hbm,
    gw_hbm,
    bias_out,
    stitch_out,
    rms_out,
    g_hbm,
    acc_hbm,
    image_ref,
    valid_ref,
    mix_ref,
    xb,
    raw,
    wt,
    part,
    p1,
    p2,
    r1,
    r2,
    gfull,
    cbuf,
    stbuf,
    zo,
    zsend,
    zrecv,
    zfin,
    gb_ref,
    gs_ref,
    sq_ref,
    usq_ref,
    wgx,
    gtile,
    acc,
    gout,
    scur,
    srecv,
    stats,
    x_sem,
    xs_sem,
    xr_sem,
    wo_sem,
    ws_sem,
    wr_sem,
    rs1_s,
    rs1_r,
    rs2_s,
    rs2_r,
    ag1_s,
    ag1_r,
    ag2_s,
    ag2_r,
    cx_s,
    cx_r,
    c_sem,
    st_sem,
    g_sem,
    z_s,
    z_r,
    zf_sem,
    z_free,
    wg_sem,
    gt_sem,
    ai_sem,
    ao_sem,
    go_sem,
    sc_s,
    sc_r,
    zs_s,
    zs_r,
):
    towers, images, width = x_hbm.shape
    chunks = cot_hbm.shape[1]
    pairs = chunks // 2
    mine = chunks * STEP
    per_chunk = images // IMAGES
    total = chunks * per_chunk
    tiles = towers * per_chunk
    last = planes - 1
    halves = 8 // planes

    z = lax.axis_index("dp")
    row = lax.axis_index("rows")
    y = row // 4
    x = (row // 2) % 2
    core = row % 2
    oy, ox, oc = 1 - y, 1 - x, 1 - core
    to_x = (z, y * 4 + ox * 2 + core)
    to_y = (z, oy * 4 + x * 2 + core)
    to_core = (z, y * 4 + x * 2 + oc)

    barrier = pltpu.get_barrier_semaphore()
    for there in (to_x, to_y, to_core):
        pl.semaphore_signal(barrier, inc=1, device_id=there, device_id_type=MESH)
    for off in range(1, planes):
        pl.semaphore_signal(barrier, inc=1, device_id=((z + off) % planes, row), device_id_type=MESH)

    def remote(src, dst, send, recv, there):
        return pltpu.make_async_remote_copy(
            src_ref=src, dst_ref=dst, send_sem=send, recv_sem=recv, device_id=there, device_id_type=MESH
        )

    def lanes(q):
        return pl.ds(pl.multiple_of((q % per_chunk) * IMAGES, IMAGES), IMAGES)

    def x_local(i):
        cut = pl.ds(i * IMAGES, IMAGES)
        return pltpu.make_async_copy(x_hbm.at[:, cut], xb.at[0, :, cut], x_sem.at[i])

    def x_remote(i):
        cut = pl.ds(i * IMAGES, IMAGES)
        return remote(x_hbm.at[:, cut], xb.at[1, :, cut], xs_sem.at[i], xr_sem.at[i], to_core)

    def w_lanes(owner, p):
        return pl.ds(pl.multiple_of(owner * mine + p * 2 * STEP, 2 * STEP), 2 * STEP)

    def w_local(p):
        return [
            pltpu.make_async_copy(w_hbm.at[:, :, w_lanes(c * 2 + core, p)], raw.at[0, :, c], wo_sem.at[c])
            for c in range(4)
        ]

    def w_remote(p):
        return [
            remote(
                w_hbm.at[:, :, w_lanes(c * 2 + oc, p)], raw.at[1, :, c], ws_sem.at[c], wr_sem.at[c], to_core
            )
            for c in range(4)
        ]

    def rs1(q):
        s = q % SLOTS
        return (
            remote(p1.at[s, 0], r1.at[s, 0], rs1_s.at[s, 0], rs1_r.at[s, 0], to_x),
            remote(p1.at[s, 1], r1.at[s, 1], rs1_s.at[s, 1], rs1_r.at[s, 1], to_y),
        )

    def rs2(q):
        s = q % SLOTS
        return (
            remote(p2.at[s, 0], r2.at[s, 0], rs2_s.at[s, 0], rs2_r.at[s, 0], to_y),
            remote(p2.at[s, 1], r2.at[s, 1], rs2_s.at[s, 1], rs2_r.at[s, 1], to_x),
        )

    def ag1(q):
        s, c, cut = q % SLOTS, (q // per_chunk) % 2, lanes(q)
        a = gfull.at[c, 0, y, x, core, :, cut]
        b = gfull.at[c, 1, y, x, core, :, cut]
        return (
            remote(a, a, ag1_s.at[s, 0], ag1_r.at[s, 0], to_x),
            remote(b, b, ag1_s.at[s, 1], ag1_r.at[s, 1], to_y),
        )

    def ag2(q):
        s, c, cut = q % SLOTS, (q // per_chunk) % 2, lanes(q)
        a = gfull.at[c, 0, y, :, core, :, cut]
        b = gfull.at[c, 1, :, x, core, :, cut]
        return (
            remote(a, a, ag2_s.at[s, 0], ag2_r.at[s, 0], to_y),
            remote(b, b, ag2_s.at[s, 1], ag2_r.at[s, 1], to_x),
        )

    def cx(q):
        s, c, cut = q % SLOTS, (q // per_chunk) % 2, lanes(q)
        a = gfull.at[c, :, :, :, core, :, cut]
        return (remote(a, a, cx_s.at[s], cx_r.at[s], to_core),)

    def cot_copy(q):
        s = q % SLOTS
        return pltpu.make_async_copy(cot_hbm.at[:, q // per_chunk, :, lanes(q)], cbuf.at[s], c_sem.at[s])

    def st_copy(q):
        s = q % SLOTS
        return pltpu.make_async_copy(stbuf.at[s], st_hbm.at[:, q // per_chunk, :, lanes(q)], st_sem.at[s])

    def g_copy(k):
        return pltpu.make_async_copy(gfull.at[k % 2], g_hbm.at[:, :, :, :, k], g_sem.at[k % 2])

    def gw_copy(k):
        return pltpu.make_async_copy(zfin, gw_hbm.at[:, :, k], zf_sem)

    def z_copy(k, j, way):
        there = (z + 1, row) if way == 0 else (z - 1, row)
        return remote(zsend.at[way, j], zrecv.at[way, j], z_s.at[way, j], z_r.at[way, j], there)

    def wg_load(g):
        p, t = g // tiles, (g % tiles) // per_chunk
        return [
            pltpu.make_async_copy(w_hbm.at[t, :, w_lanes(r, p)], wgx.at[:, pl.ds(r * 128, 128)], wg_sem.at[r])
            for r in range(8)
        ]

    def g_load(g):
        p, t, i = g // tiles, (g % tiles) // per_chunk, g % per_chunk
        return pltpu.make_async_copy(
            g_hbm.at[t, :, :, :, pl.ds(p * 2, 2), :, lanes(i)], gtile.at[g % HELD], gt_sem.at[g % HELD]
        )

    def acc_in(g):
        return pltpu.make_async_copy(acc_hbm.at[g % tiles], acc.at[g % HELD], ai_sem.at[g % HELD])

    def acc_out(g):
        return pltpu.make_async_copy(acc.at[g % HELD], acc_hbm.at[g % tiles], ao_sem.at[g % HELD])

    def gx_out(g):
        t = (g % tiles) // per_chunk
        return pltpu.make_async_copy(gout.at[g % 2], gx_hbm.at[t, lanes(g)], go_sem.at[g % 2])

    def in_plane(n):
        there = (to_x, to_y, to_core)[n]
        return remote(scur.at[n], srecv.at[n], sc_s.at[n], sc_r.at[n], there)

    def to_plane(off):
        there = ((z + off) % planes, row)
        return remote(stats.at[z], stats.at[z], zs_s.at[off - 1], zs_r.at[off - 1], there)

    def from_plane(off):
        there = ((z + off) % planes, row)
        held = stats.at[(z + planes - off) % planes]
        return remote(held, held, zs_s.at[off - 1], zs_r.at[off - 1], there)

    def start(copies):
        for c in copies:
            c.start()

    def wait_send(copies):
        for c in copies:
            c.wait_send()

    def wait_recv(copies):
        for c in copies:
            c.wait_recv()

    def stage(q, work, sends, *sent):
        @pl.when((q >= SLOTS) & (q < total + SLOTS))
        def _():
            for copies in sent:
                wait_send(copies(q - SLOTS))

        @pl.when((q >= 0) & (q < total))
        def _():
            work(q)
            start(sends(q))

    def turn(p):
        for side, copies in enumerate((w_local(p), w_remote(p))):
            for c, copy in enumerate(copies):
                if side == 0:
                    copy.wait()
                else:
                    copy.wait_recv()

                def one(t, carry):
                    turned = jnp.transpose(raw[side, t, c])
                    wt[side, t, 0, c] = turned[:STEP]
                    wt[side, t, 1, c] = turned[STEP:]
                    return carry

                lax.fori_loop(0, towers, one, 0)

        @pl.when(p + 1 < pairs)
        def _():
            start(w_local(p + 1))

    def forward(q):
        k, i, s = q // per_chunk, q % per_chunk, q % SLOTS
        p, h = k // 2, k % 2

        cot_copy(q).start()

        cut = pl.ds(pl.multiple_of(i * IMAGES, IMAGES), IMAGES)

        @pl.when(k == 0)
        def _():
            x_local(i).wait()
            x_remote(i).wait_recv()
            keep = (1.0 - image_ref[cut, 0:1] * pad_row_ref[...]).astype(BF16)
            valid = image_ref[cut, 64:65]
            for t in range(towers):
                used = xb[0, t, cut] * keep
                xb[0, t, cut] = used
                used = used.astype(F32)
                usq_ref[...] = usq_ref[...] + jnp.sum(used * used * valid, axis=0, keepdims=True)
                xb[1, t, cut] = xb[1, t, cut] * keep

        @pl.when((i == 0) & (h == 0))
        def _():
            turn(p)

        @pl.when((i == 0) & (h == 1))
        def _():
            wait_send(w_remote(p))

            @pl.when(p + 1 < pairs)
            def _():
                start(w_remote(p + 1))

        for t in range(towers):
            out = lax.dot_general(
                wt[0, t, h].reshape(4 * STEP, width),
                xb[0, t, cut],
                (((1,), (1,)), ((), ())),
                preferred_element_type=F32,
            ) + lax.dot_general(
                wt[1, t, h].reshape(4 * STEP, width),
                xb[1, t, cut],
                (((1,), (1,)), ((), ())),
                preferred_element_type=F32,
            )
            out = out.reshape(2, 2, STEP, IMAGES)
            for a in range(2):
                for b in range(2):
                    part[s, a, b, t] = out[a, b]
        for a in range(2):
            p1[s, 0, a] = pack(part[s, a, ox, 0])
            p1[s, 1, a] = pack(part[s, oy, a, 1])

    def reduce(q):
        s = q % SLOTS
        wait_recv(rs1(q))
        p2[s, 0] = pack(part[s, oy, x, 0] + unpack(r1[s, 0, oy]))
        p2[s, 1] = pack(part[s, y, ox, 1] + unpack(r1[s, 1, ox]))
        part[s, y, x, 0] = part[s, y, x, 0] + unpack(r1[s, 0, y])
        part[s, y, x, 1] = part[s, y, x, 1] + unpack(r1[s, 1, x])

    def pointwise(q):
        k, i, s = q // per_chunk, q % per_chunk, q % SLOTS
        wait_recv(rs2(q))
        cot_copy(q).wait()

        @pl.when(q >= SLOTS)
        def _():
            st_copy(q - SLOTS).wait()

        valid = valid_ref[i]
        mix = mix_ref[k]
        bias = [mix[:, t : t + 1] for t in range(2)]
        stitch = [[mix[:, 2 + 2 * a + b : 3 + 2 * a + b] for b in range(2)] for a in range(2)]
        pre = [part[s, y, x, t] + unpack(r2[s, t]) + bias[t] for t in range(2)]
        act = [jnp.maximum(p, 0.0) for p in pre]
        up = [cbuf[s, t].astype(F32) * valid for t in range(2)]
        cut = lanes(q)
        for a in range(2):
            out = stitch[a][0] * act[0] + stitch[a][1] * act[1]
            stbuf[s, a] = out.astype(BF16)
            sq_ref[1] = sq_ref[1] + fold(out * out * valid)
            for b in range(2):
                gs_ref[k, a, b] = gs_ref[k, a, b] + fold(up[a] * act[b])
        for t in range(2):
            sq_ref[0] = sq_ref[0] + fold(pre[t] * pre[t] * valid)
            grad = stitch[0][t] * up[0] + stitch[1][t] * up[1]
            grad = jnp.where(pre[t] > 0, grad, 0.0).astype(BF16)
            gfull[k % 2, t, y, x, core, :, cut] = grad
            gb_ref[k, t] = gb_ref[k, t] + fold(grad.astype(F32))
        st_copy(q).start()

    def spread(q):
        wait_recv(ag1(q))

    def across(q):
        wait_recv(ag2(q))

    def terms(k, n):
        unit = width // 3
        for t, at, wide in (((0, 0, 2 * unit),), ((0, 2 * unit, unit), (1, 0, unit)), ((1, unit, 2 * unit),))[n]:
            value = jnp.dot(
                gfull[k % 2, t].reshape(8 * STEP, images),
                xb[0, t, :, at : at + wide],
                preferred_element_type=F32,
            )
            value = value.astype(BF16).reshape(planes, halves, STEP, wide)
            for d in range(planes):
                for e in range(halves):
                    zo[t, d, e, :, at : at + wide] = value[d, e]

    def chain(k, j):
        if j == planes - 2:

            @pl.when(k > 0)
            def _():
                gw_copy(k - 1).wait()

            def begin(i, carry):
                t, e = i // halves, i % halves
                zfin[t, e] = zo[t, z, e].astype(F32)
                return carry

            lax.fori_loop(0, towers * halves, begin, 0)
        for way in range(2):
            near = z if way == 0 else last - z
            source = (z - 1, row) if way == 0 else (z + 1, row)

            def freed():
                @pl.when(k + 1 < chunks)
                def _():
                    pl.semaphore_signal(
                        z_free.at[way, j - 1], inc=1, device_id=source, device_id_type=MESH
                    )

            if j <= planes - 2:

                @pl.when(near <= j)
                def _():
                    dest = last - j + z if way == 0 else j - last + z

                    @pl.when(k > 0)
                    def _():
                        z_copy(k - 1, j, way).wait_send()

                    if j > 0:

                        @pl.when(near >= 1)
                        def _():
                            z_copy(k, j - 1, way).wait_recv()

                            def add(i, carry):
                                t, e = i // halves, i % halves
                                value = zo[t, dest, e].astype(F32) + zrecv[way, j - 1, t, e].astype(F32)
                                zsend[way, j, t, e] = value.astype(BF16)
                                return carry

                            lax.fori_loop(0, towers * halves, add, 0)
                            freed()

                        @pl.when(near == 0)
                        def _():
                            zsend[way, j] = zo[:, dest]

                    else:
                        zsend[way, j] = zo[:, dest]

                    @pl.when(k > 0)
                    def _():
                        pl.semaphore_wait(z_free.at[way, j], 1)

                    z_copy(k, j, way).start()

            else:

                @pl.when(near >= 1)
                def _():
                    z_copy(k, j - 1, way).wait_recv()

                    def more(i, carry):
                        t, e = i // halves, i % halves
                        zfin[t, e] = zfin[t, e] + zrecv[way, j - 1, t, e].astype(F32)
                        return carry

                    lax.fori_loop(0, towers * halves, more, 0)
                    freed()

        if j == planes - 1:
            gw_copy(k).start()

    def prepare(g):
        g_load(g).start()

        @pl.when((g >= HELD) & (g - HELD < (pairs - 1) * tiles))
        def _():
            acc_out(g - HELD).wait()

        @pl.when(g >= tiles)
        def _():
            acc_in(g).start()

    def tile(g):
        g_load(g).wait()

        @pl.when(g % per_chunk == 0)
        def _():
            for c in wg_load(g):
                c.wait()

        value = jnp.dot(
            wgx[...], gtile[g % HELD].reshape(16 * STEP, IMAGES), preferred_element_type=F32
        )
        final = g >= (pairs - 1) * tiles

        @pl.when(g < tiles)
        def _():
            acc[g % HELD] = value

        @pl.when(g >= tiles)
        def _():
            acc_in(g).wait()
            acc[g % HELD] = acc[g % HELD] + value

        @pl.when(jnp.logical_not(final))
        def _():
            acc_out(g).start()

        @pl.when(final)
        def _():
            @pl.when(g >= (pairs - 1) * tiles + 2)
            def _():
                gx_out(g - 2).wait()

            keep = (1.0 - image_ref[lanes(g), 0:1] * pad_row_ref[...]).astype(BF16)
            gout[g % 2] = jnp.transpose(acc[g % HELD].astype(BF16)) * keep
            gx_out(g).start()

        @pl.when(((g + 1) % per_chunk == 0) & (g + 1 < pairs * tiles))
        def _():
            start(wg_load(g + 1))

        @pl.when(g + 2 < pairs * tiles)
        def _():
            prepare(g + 2)

    def sums(n):
        if n == 0:
            scur[0] = jnp.zeros_like(scur[0])
            scur[0, 0:1] = fold(usq_ref[...])
            scur[0, 1:2] = jnp.sum(sq_ref[0], axis=0, keepdims=True)
            scur[0, 2:3] = jnp.sum(sq_ref[1], axis=0, keepdims=True)
            scur[0, 3:4] = fold(sum(valid_ref[i] for i in range(per_chunk)))
            for k in range(chunks):
                at = k * 6 * STEP
                stats[z, :, at : at + 2 * STEP] = lane_sums(gb_ref[k].reshape(2 * STEP, 128))
                stats[z, :, at + 2 * STEP : at + 6 * STEP] = lane_sums(gs_ref[k].reshape(4 * STEP, 128))
        else:
            in_plane(n - 1).wait()
            value = scur[n - 1] + srecv[n - 1]
            if n < 3:
                scur[n] = value
            else:
                stats[z, :, chunks * 6 * STEP :] = value
        if n < 3:
            in_plane(n).start()
        else:
            for off in range(1, planes):
                to_plane(off).start()

    start(w_local(0))
    for i in range(per_chunk):
        x_local(i).start()
    for i in range(per_chunk):
        cut = slice(i * IMAGES, (i + 1) * IMAGES)
        valid = valid_in[:, cut].astype(F32)
        small = jnp.where(class_in[:, cut] == 195, 1.0, 0.0)
        valid_ref[i] = valid
        both = jnp.concatenate(
            [jnp.broadcast_to(small, (64, IMAGES)), jnp.broadcast_to(valid, (64, IMAGES))], axis=0
        )
        image_ref[cut] = jnp.transpose(both)
    mix = jnp.concatenate(
        [bias_in[...], stitch_in[0], stitch_in[1], jnp.zeros((122, mine), F32)], axis=0
    )
    mix_ref[...] = jnp.transpose(mix).reshape(chunks, STEP, 128)
    pl.semaphore_wait(barrier, 2 + planes)
    x_remote(0).start()
    start(w_remote(0))

    def send_x(i, carry):
        x_remote(i).start()
        return carry

    lax.fori_loop(1, per_chunk, send_x, 0)
    gb_ref[...] = jnp.zeros_like(gb_ref)
    gs_ref[...] = jnp.zeros_like(gs_ref)
    sq_ref[...] = jnp.zeros_like(sq_ref)
    usq_ref[...] = jnp.zeros_like(usq_ref)

    ready = per_chunk - 1 + 5
    offsets = [2 + 3 * j for j in range(planes)]
    ends = [2 + 10 * j for j in range(planes)]
    first = per_chunk + 3
    late = (chunks - 1) * per_chunk + 3

    def body(s, carry):
        stage(s, forward, rs1, rs1)
        stage(s - 1, reduce, rs2, rs2)
        stage(s - 2, pointwise, ag1, ag1)
        stage(s - 3, spread, ag2, ag2)
        stage(s - 4, across, cx, cx)

        @pl.when((s >= 5) & (s < total + 5))
        def _():
            wait_recv(cx(s - 5))

        for n in range(4):

            @pl.when(s == total + 2 + n)
            def _():
                sums(n)

        @pl.when(s >= ready)
        def _():
            done = s - ready
            k = done // per_chunk
            at = done % per_chunk

            def step(j):
                since = done - offsets[j]
                usual = (since >= 0) & (since % per_chunk == 0) & (since // per_chunk < chunks - 1)
                final = done == (chunks - 1) * per_chunk + ends[j]

                @pl.when(usual | final)
                def _():
                    chain(jnp.where(final, chunks - 1, since // per_chunk), j)

            for j in range(1, planes):
                step(j)
            for n in range(3):

                @pl.when((at == n) & (k < chunks))
                def _():
                    if n == 0:
                        g_copy(k).start()
                    terms(k, n)
                    if n == 2:
                        g_copy(k).wait()

            step(0)
            @pl.when(done == first - 1)
            def _():
                start(wg_load(0))
                prepare(0)
                prepare(1)

            since = done - first
            usual = (since >= 0) & (since % per_chunk < 5) & (since // per_chunk < chunks - 2)
            g = jnp.where(
                done >= late,
                done - late + EACH * (chunks - 2),
                EACH * (since // per_chunk) + since % per_chunk,
            )

            @pl.when(usual | ((done >= late) & (g < pairs * tiles)))
            def _():
                tile(g)

            @pl.when(usual & (since % per_chunk == 4))
            def _():
                tile(g + 1)

        return carry

    left = pairs * tiles - EACH * (chunks - 2)
    lax.fori_loop(0, ready + max((chunks - 1) * per_chunk + ends[-1], late + left - 1) + 1, body, 0)

    def drain(q, carry):
        st_copy(q).wait()
        return carry

    lax.fori_loop(total - SLOTS, total, drain, 0)

    def drain_x(i, carry):
        x_remote(i).wait_send()
        return carry

    lax.fori_loop(0, per_chunk, drain_x, 0)
    for g in (pairs * tiles - 2, pairs * tiles - 1):
        gx_out(g).wait()
    gw_copy(chunks - 1).wait()
    for way in range(2):
        near = z if way == 0 else last - z
        for j in range(planes - 1):

            @pl.when(near <= j)
            def _():
                z_copy(chunks - 1, j, way).wait_send()

    for off in range(1, planes):
        to_plane(off).wait_send()
        from_plane(off).wait_recv()
    every = sum(stats[d] for d in range(planes))
    for k in range(chunks):
        for n in range(6):
            at = (k * 6 + n) * STEP
            value = every[0:1, at : at + STEP]
            if n < 2:
                bias_out[n : n + 1, k * STEP : (k + 1) * STEP] = value
            else:
                stitch_out[(n - 2) // 2, n % 2 : n % 2 + 1, k * STEP : (k + 1) * STEP] = value
    ends = jnp.sum(every[:, chunks * 6 * STEP :], axis=1, keepdims=True)
    images_in = ends[3:4] / lax.axis_size("rows")
    for n, size in enumerate((F, C, C)):
        rms_out[n : n + 1] = jnp.broadcast_to(jnp.sqrt(ends[n : n + 1] / (images_in * 2 * size)), (1, 128))


def put_out(st_ref, gx_ref, gw_ref, st_out, gx_out, gw_out):
    st_out[...] = st_ref[...]
    gx_out[...] = gx_ref[...]
    gw_out[0] = jnp.transpose(gw_ref[0])


def results(stitched, grad_inputs, grad_weights):
    towers, width = grad_weights.shape[0], grad_weights.shape[2]
    mine = grad_weights.shape[1]
    block = min(mine, 512)
    each = mine // block
    steps = towers * each
    flat = [v.reshape(-1, v.shape[-1]) for v in (stitched, grad_inputs)]
    plain = [pl.BlockSpec((v.shape[0] // steps, v.shape[1]), lambda i: (i, 0)) for v in flat]
    out = pl.pallas_call(
        put_out,
        grid=(steps,),
        out_shape=(
            *(jax.ShapeDtypeStruct(v.shape, v.dtype) for v in flat),
            jax.ShapeDtypeStruct((towers, width, mine), F32),
        ),
        in_specs=[*plain, pl.BlockSpec((1, block, width), lambda i: (i // each, i % each, 0))],
        out_specs=[*plain, pl.BlockSpec((1, width, block), lambda i: (i // each, 0, i % each))],
        name="results",
    )(*flat, grad_weights)
    return out[0].reshape(stitched.shape), out[1].reshape(grad_inputs.shape), out[2]


def fused(inputs, weights, bias, stitch, cotangent, valid, size_class):
    planes = lax.axis_size("dp")
    towers, images, width = inputs.shape
    mine = bias.shape[1]
    chunks = mine // STEP
    per_chunk = images // IMAGES
    halves = 8 // planes
    tiles = towers * per_chunk
    place = np.arange(width) % 36
    padded = ((place // 6 == 5) | (place % 6 == 5)).astype(np.float32)
    many = chunks * 6 * STEP + 128
    vmem = pl.BlockSpec(memory_space=pltpu.VMEM)
    hbm = pl.BlockSpec(memory_space=pl.ANY)
    dma = pltpu.SemaphoreType.DMA
    stitched, grad_inputs, grad_weights, grad_bias, grad_stitch, means, _, _ = pl.pallas_call(
        functools.partial(kernel, planes),
        out_shape=(
            jax.ShapeDtypeStruct((2, chunks, STEP, images), BF16),
            jax.ShapeDtypeStruct((towers, images, width), BF16),
            jax.ShapeDtypeStruct((2, halves, chunks, STEP, width), F32),
            jax.ShapeDtypeStruct((2, mine), F32),
            jax.ShapeDtypeStruct((2, 2, mine), F32),
            jax.ShapeDtypeStruct((8, 128), F32),
            jax.ShapeDtypeStruct((2, 2, 2, 2, chunks, STEP, images), BF16),
            jax.ShapeDtypeStruct((tiles, width, IMAGES), F32),
        ),
        in_specs=[hbm] * 3 + [vmem] * 5,
        out_specs=(hbm, hbm, hbm, vmem, vmem, vmem, hbm, hbm),
        scratch_shapes=[
            pltpu.VMEM((images, 128), F32),
            pltpu.VMEM((per_chunk, 1, IMAGES), F32),
            pltpu.VMEM((chunks, STEP, 128), F32),
            pltpu.VMEM((2, towers, images, width), BF16),
            pltpu.VMEM((2, towers, 4, width, 2 * STEP), BF16),
            pltpu.VMEM((2, towers, 2, 4, STEP, width), BF16),
            pltpu.VMEM((SLOTS, 2, 2, towers, STEP, IMAGES), F32),
            pltpu.VMEM((SLOTS, 2, 2, WORDS, IMAGES), jnp.int32),
            pltpu.VMEM((SLOTS, 2, WORDS, IMAGES), jnp.int32),
            pltpu.VMEM((SLOTS, 2, 2, WORDS, IMAGES), jnp.int32),
            pltpu.VMEM((SLOTS, 2, WORDS, IMAGES), jnp.int32),
            pltpu.VMEM((2, towers, 2, 2, 2, STEP, images), BF16),
            pltpu.VMEM((SLOTS, 2, STEP, IMAGES), BF16),
            pltpu.VMEM((SLOTS, 2, STEP, IMAGES), BF16),
            pltpu.VMEM((towers, planes, halves, STEP, width), BF16),
            pltpu.VMEM((2, planes - 1, towers, halves, STEP, width), BF16),
            pltpu.VMEM((2, planes - 1, towers, halves, STEP, width), BF16),
            pltpu.VMEM((towers, halves, STEP, width), F32),
            pltpu.VMEM((chunks, 2, STEP, 128), F32),
            pltpu.VMEM((chunks, 2, 2, STEP, 128), F32),
            pltpu.VMEM((2, STEP, 128), F32),
            pltpu.VMEM((1, width), F32),
            pltpu.VMEM((width, 16 * STEP), BF16),
            pltpu.VMEM((HELD, 2, 2, 2, 2, STEP, IMAGES), BF16),
            pltpu.VMEM((HELD, width, IMAGES), F32),
            pltpu.VMEM((2, IMAGES, width), BF16),
            pltpu.VMEM((3, 8, 128), F32),
            pltpu.VMEM((3, 8, 128), F32),
            pltpu.VMEM((planes, 8, many), F32),
            dma((per_chunk,)),
            dma((per_chunk,)),
            dma((per_chunk,)),
            dma((4,)),
            dma((4,)),
            dma((4,)),
            dma((SLOTS, 2)),
            dma((SLOTS, 2)),
            dma((SLOTS, 2)),
            dma((SLOTS, 2)),
            dma((SLOTS, 2)),
            dma((SLOTS, 2)),
            dma((SLOTS, 2)),
            dma((SLOTS, 2)),
            dma((SLOTS,)),
            dma((SLOTS,)),
            dma((SLOTS,)),
            dma((SLOTS,)),
            dma((2,)),
            dma((2, planes - 1)),
            dma((2, planes - 1)),
            dma,
            pltpu.SemaphoreType.REGULAR((2, planes - 1)),
            dma((8,)),
            dma((HELD,)),
            dma((HELD,)),
            dma((HELD,)),
            dma((2,)),
            dma((3,)),
            dma((3,)),
            dma((planes - 1,)),
            dma((planes - 1,)),
        ],
        compiler_params=pltpu.CompilerParams(
            collective_id=0, has_side_effects=True, vmem_limit_bytes=67043328
        ),
        name="towers",
    )(
        inputs,
        weights,
        cotangent.reshape(2, chunks, STEP, images),
        valid[None, :],
        size_class[None, :],
        padded[None, :],
        bias,
        stitch,
    )
    stitched, grad_inputs, grad_weights = results(
        stitched.reshape(2, mine, images), grad_inputs, grad_weights.reshape(towers, -1, width)
    )
    return (stitched, grad_inputs, grad_weights, grad_bias, grad_stitch, means[:3, 0])


def rms(totals):
    count = totals[3] / lax.axis_size("rows")
    return jnp.sqrt(
        jnp.stack(
            [totals[0] / (count * 2 * F), totals[1] / (count * 2 * C), totals[2] / (count * 2 * C)]
        )
    )


def line_sum(own, up):
    size = lax.axis_size("dp")
    here = lax.axis_index("dp")
    got = None
    for step in range(size - 1):
        dest = size - 1 - step + here if up else step - (size - 1) + here
        dest = jnp.clip(dest, 0, size - 1)
        term = lax.dynamic_index_in_dim(own, dest, 0, keepdims=False)
        if got is not None:
            term = (term.astype(jnp.float32) + got.astype(jnp.float32)).astype(jnp.bfloat16)
        pairs = [(z, z + 1) for z in range(step + 1)]
        if not up:
            pairs = [(size - 1 - a, size - 1 - b) for a, b in pairs]
        got = lax.ppermute(term, "dp", pairs)
    return got


def plain(inputs, weights, bias, stitch, cotangent, valid, size_class):
    rows = lax.axis_size("rows")
    size = lax.axis_size("dp")
    here = lax.axis_index("dp")
    width = inputs.shape[2]
    mine = bias.shape[1]
    step = min(BLOCK, mine)
    blocks = mine // step
    place = lax.iota(jnp.int32, width) % 36
    padded = (place // 6 == 5) | (place % 6 == 5)
    dropped = (size_class == 195)[:, None] & padded[None, :]
    used = jnp.where(dropped[None], jnp.zeros((), jnp.bfloat16), inputs)
    split = weights.reshape(2, width, rows, mine)
    weight_valid = valid.astype(jnp.float32)
    pieces, stitched, grad_bias, grad_stitch, square_pre, square_out = [], [], [], [], [], []
    grad_weights = []
    mats = [split[:, :, :, k * step : (k + 1) * step] for k in range(blocks)]
    sums = []
    for k in range(blocks):
        part = jnp.einsum("tfrc,tbf->rctb", mats[k], used, preferred_element_type=jnp.float32)
        sums.append(
            lax.psum_scatter(part.reshape(rows * step, 2, -1), "rows", scatter_dimension=0, tiled=True)
        )
    for k in range(blocks):
        cut = slice(k * step, (k + 1) * step)
        pre = jnp.transpose(sums[k], (1, 0, 2)) + bias[:, cut, None]
        act = jax.nn.relu(pre)
        mix = stitch[:, :, cut, None]
        out = jnp.sum(mix * act[None], axis=1)
        stitched.append(out.astype(jnp.bfloat16))
        upstream = cotangent[:, cut].astype(jnp.float32) * weight_valid[None, None, :]
        grad_act = jnp.sum(mix * upstream[:, None], axis=0)
        grad_pre = jnp.where(pre > 0, grad_act, 0.0).astype(jnp.bfloat16)
        grad_bias.append(jnp.sum(grad_pre.astype(jnp.float32), axis=2))
        grad_stitch.append(jnp.sum(upstream[:, None] * act[None], axis=3))
        square_pre.append(jnp.sum(weight_valid[None, None, :] * pre * pre))
        square_out.append(jnp.sum(weight_valid[None, None, :] * out * out))
        piece = lax.all_gather(grad_pre, "rows", axis=0)
        pieces.append(piece)
        block = jnp.einsum("tbf,rtcb->rtfc", used, piece, preferred_element_type=jnp.float32)
        block = block.reshape(size, rows // size, 2, width, step)
        own = block.astype(jnp.bfloat16)
        total = lax.dynamic_index_in_dim(block, here, 0, keepdims=False)
        total = total + line_sum(own, True).astype(jnp.float32) + line_sum(own, False).astype(jnp.float32)
        grad_weights.append(total)
    total_x = sum(
        jnp.einsum("rtcb,tfrc->tbf", pieces[k], mats[k], preferred_element_type=jnp.float32)
        for k in range(blocks)
    )
    grad_inputs = jnp.where(dropped[None], 0.0, total_x).astype(jnp.bfloat16)
    grad_weights = jnp.stack(grad_weights, axis=0)
    grad_weights = jnp.transpose(grad_weights, (2, 3, 1, 0, 4)).reshape(2, width, -1)
    stitched = jnp.concatenate(stitched, axis=1)
    grad_bias = jnp.concatenate(grad_bias, axis=1)
    grad_stitch = jnp.concatenate(grad_stitch, axis=2)
    used_wide = used.astype(jnp.float32)
    partial_value = jnp.stack(
        [
            jnp.sum(weight_valid[None, :, None] * used_wide * used_wide),
            sum(square_pre),
            sum(square_out),
            jnp.sum(weight_valid),
        ]
    )
    grad_bias, grad_stitch = lax.psum((grad_bias, grad_stitch), "dp")
    totals = lax.psum(partial_value, ("dp", "rows"))
    return (stitched, grad_inputs, grad_weights, grad_bias, grad_stitch, rms(totals))


def small_plane(mesh):
    return mesh.shape["rows"] == 8 and mesh.shape["dp"] in (2, 4, 8)


def solution(mesh):
    in_specs = (
        P(None, "dp", "rows"),
        P(None, "rows", None),
        P(None, "rows"),
        P(None, None, "rows"),
        P(None, "rows", "dp"),
        P("dp"),
        P("dp"),
    )
    out_specs = (
        P(None, "rows", "dp"),
        P(None, "dp", "rows"),
        P(None, "rows", "dp"),
        P(None, "rows"),
        P(None, None, "rows"),
        P(),
    )
    return jax.shard_map(
        fused if small_plane(mesh) else plain, mesh=mesh, in_specs=in_specs, out_specs=out_specs, check_vma=False
    )
```

```python
import functools

import jax
import jax.numpy as jnp
import numpy as np
from jax import lax
from jax.experimental import pallas as pl
from jax.experimental.pallas import tpu as pltpu
from jax.sharding import PartitionSpec as P

F = 9216
C = 4096
BLOCK = 128
STEP = 64
IMAGES = 256
SLOTS = 4
HELD = 3
EACH = 6
WORDS = 40
TOP = 2.0**18 - 2.0
F32 = jnp.float32
BF16 = jnp.bfloat16
MESH = pl.DeviceIdType.MESH


def fold(value):
    return sum(value[:, i : i + 128] for i in range(0, value.shape[1], 128))


def lane_sums(value):
    ones = jnp.ones((8, 128), F32)
    return lax.dot_general(
        ones, value, (((1,), (1,)), ((), ())), precision=lax.Precision.HIGHEST, preferred_element_type=F32
    )


def pack(value):
    tiles = [value[8 * i : 8 * i + 8] for i in range(8)]
    top = jnp.abs(tiles[0])
    for v in tiles[1:]:
        top = jnp.maximum(top, jnp.abs(v))
    exponent = jnp.floor(jnp.log2(jnp.maximum(top, 2.0**-60))) + 1.0
    scale = jnp.exp2(-exponent) * TOP
    q = [jnp.round(v * scale).astype(jnp.int32) for v in tiles]
    low = [v & 0x1FFF for v in q[5:]]
    high = [(v >> 13) & 0x3F for v in q[5:]]
    words = [
        (q[0] << 13) | low[0],
        (q[1] << 13) | low[1],
        (q[2] << 13) | low[2],
        (q[3] << 13) | high[0] | (high[1] << 6),
        (q[4] << 13) | high[2] | ((exponent.astype(jnp.int32) & 0x7F) << 6),
    ]
    return jnp.concatenate(words, axis=0)


def unpack(words):
    w = [words[8 * i : 8 * i + 8] for i in range(5)]
    exponent = (w[4] << 19) >> 25
    scale = jnp.exp2(exponent.astype(F32)) * (1.0 / TOP)
    q = [v >> 13 for v in w]
    q.append(((w[3] << 26) >> 26 << 13) | (w[0] & 0x1FFF))
    q.append(((w[3] << 20) >> 26 << 13) | (w[1] & 0x1FFF))
    q.append(((w[4] << 26) >> 26 << 13) | (w[2] & 0x1FFF))
    return jnp.concatenate([v.astype(F32) * scale for v in q], axis=0)


def kernel(
    planes,
    x_hbm,
    w_hbm,
    cot_hbm,
    valid_in,
    class_in,
    pad_row_ref,
    bias_in,
    stitch_in,
    st_hbm,
    gx_hbm,
    gw_hbm,
    bias_out,
    stitch_out,
    rms_out,
    g_hbm,
    acc_hbm,
    image_ref,
    valid_ref,
    mix_ref,
    xb,
    raw,
    wt,
    part,
    p1,
    p2,
    r1,
    r2,
    gfull,
    cbuf,
    stbuf,
    zo,
    zsend,
    zrecv,
    zfin,
    gb_ref,
    gs_ref,
    sq_ref,
    usq_ref,
    wgx,
    gtile,
    acc,
    gout,
    scur,
    srecv,
    stats,
    x_sem,
    xs_sem,
    xr_sem,
    wo_sem,
    ws_sem,
    wr_sem,
    rs1_s,
    rs1_r,
    rs2_s,
    rs2_r,
    ag1_s,
    ag1_r,
    ag2_s,
    ag2_r,
    cx_s,
    cx_r,
    c_sem,
    st_sem,
    g_sem,
    z_s,
    z_r,
    zf_sem,
    z_free,
    wg_sem,
    gt_sem,
    ai_sem,
    ao_sem,
    go_sem,
    sc_s,
    sc_r,
    zs_s,
    zs_r,
):
    towers, images, width = x_hbm.shape
    chunks = cot_hbm.shape[1]
    pairs = chunks // 2
    mine = chunks * STEP
    per_chunk = images // IMAGES
    total = chunks * per_chunk
    tiles = towers * per_chunk
    last = planes - 1
    halves = 8 // planes

    z = lax.axis_index("dp")
    row = lax.axis_index("rows")
    y = row // 4
    x = (row // 2) % 2
    core = row % 2
    oy, ox, oc = 1 - y, 1 - x, 1 - core
    to_x = (z, y * 4 + ox * 2 + core)
    to_y = (z, oy * 4 + x * 2 + core)
    to_core = (z, y * 4 + x * 2 + oc)

    barrier = pltpu.get_barrier_semaphore()
    for there in (to_x, to_y, to_core):
        pl.semaphore_signal(barrier, inc=1, device_id=there, device_id_type=MESH)
    for off in range(1, planes):
        pl.semaphore_signal(barrier, inc=1, device_id=((z + off) % planes, row), device_id_type=MESH)

    def remote(src, dst, send, recv, there):
        return pltpu.make_async_remote_copy(
            src_ref=src, dst_ref=dst, send_sem=send, recv_sem=recv, device_id=there, device_id_type=MESH
        )

    def lanes(q):
        return pl.ds(pl.multiple_of((q % per_chunk) * IMAGES, IMAGES), IMAGES)

    def x_local(i):
        cut = pl.ds(i * IMAGES, IMAGES)
        return pltpu.make_async_copy(x_hbm.at[:, cut], xb.at[0, :, cut], x_sem.at[i])

    def x_remote(i):
        cut = pl.ds(i * IMAGES, IMAGES)
        return remote(x_hbm.at[:, cut], xb.at[1, :, cut], xs_sem.at[i], xr_sem.at[i], to_core)

    def w_lanes(owner, p):
        return pl.ds(pl.multiple_of(owner * mine + p * 2 * STEP, 2 * STEP), 2 * STEP)

    def w_local(p):
        return [
            pltpu.make_async_copy(w_hbm.at[:, :, w_lanes(c * 2 + core, p)], raw.at[0, :, c], wo_sem.at[c])
            for c in range(4)
        ]

    def w_remote(p):
        return [
            remote(
                w_hbm.at[:, :, w_lanes(c * 2 + oc, p)], raw.at[1, :, c], ws_sem.at[c], wr_sem.at[c], to_core
            )
            for c in range(4)
        ]

    def rs1(q):
        s = q % SLOTS
        return (
            remote(p1.at[s, 0], r1.at[s, 0], rs1_s.at[s, 0], rs1_r.at[s, 0], to_x),
            remote(p1.at[s, 1], r1.at[s, 1], rs1_s.at[s, 1], rs1_r.at[s, 1], to_y),
        )

    def rs2(q):
        s = q % SLOTS
        return (
            remote(p2.at[s, 0], r2.at[s, 0], rs2_s.at[s, 0], rs2_r.at[s, 0], to_y),
            remote(p2.at[s, 1], r2.at[s, 1], rs2_s.at[s, 1], rs2_r.at[s, 1], to_x),
        )

    def ag1(q):
        s, c, cut = q % SLOTS, (q // per_chunk) % 2, lanes(q)
        a = gfull.at[c, 0, y, x, core, :, cut]
        b = gfull.at[c, 1, y, x, core, :, cut]
        return (
            remote(a, a, ag1_s.at[s, 0], ag1_r.at[s, 0], to_x),
            remote(b, b, ag1_s.at[s, 1], ag1_r.at[s, 1], to_y),
        )

    def ag2(q):
        s, c, cut = q % SLOTS, (q // per_chunk) % 2, lanes(q)
        a = gfull.at[c, 0, y, :, core, :, cut]
        b = gfull.at[c, 1, :, x, core, :, cut]
        return (
            remote(a, a, ag2_s.at[s, 0], ag2_r.at[s, 0], to_y),
            remote(b, b, ag2_s.at[s, 1], ag2_r.at[s, 1], to_x),
        )

    def cx(q):
        s, c, cut = q % SLOTS, (q // per_chunk) % 2, lanes(q)
        a = gfull.at[c, :, :, :, core, :, cut]
        return (remote(a, a, cx_s.at[s], cx_r.at[s], to_core),)

    def cot_copy(q):
        s = q % SLOTS
        return pltpu.make_async_copy(cot_hbm.at[:, q // per_chunk, :, lanes(q)], cbuf.at[s], c_sem.at[s])

    def st_copy(q):
        s = q % SLOTS
        return pltpu.make_async_copy(stbuf.at[s], st_hbm.at[:, q // per_chunk, :, lanes(q)], st_sem.at[s])

    def g_copy(k):
        return pltpu.make_async_copy(gfull.at[k % 2], g_hbm.at[:, :, :, :, k], g_sem.at[k % 2])

    def gw_copy(k):
        return pltpu.make_async_copy(zfin, gw_hbm.at[:, :, k], zf_sem)

    def z_copy(k, j, way):
        there = (z + 1, row) if way == 0 else (z - 1, row)
        return remote(zsend.at[way, j], zrecv.at[way, j], z_s.at[way, j], z_r.at[way, j], there)

    def wg_load(g):
        p, t = g // tiles, (g % tiles) // per_chunk
        return [
            pltpu.make_async_copy(w_hbm.at[t, :, w_lanes(r, p)], wgx.at[:, pl.ds(r * 128, 128)], wg_sem.at[r])
            for r in range(8)
        ]

    def g_load(g):
        p, t, i = g // tiles, (g % tiles) // per_chunk, g % per_chunk
        return pltpu.make_async_copy(
            g_hbm.at[t, :, :, :, pl.ds(p * 2, 2), :, lanes(i)], gtile.at[g % HELD], gt_sem.at[g % HELD]
        )

    def acc_in(g):
        return pltpu.make_async_copy(acc_hbm.at[g % tiles], acc.at[g % HELD], ai_sem.at[g % HELD])

    def acc_out(g):
        return pltpu.make_async_copy(acc.at[g % HELD], acc_hbm.at[g % tiles], ao_sem.at[g % HELD])

    def gx_out(g):
        t = (g % tiles) // per_chunk
        return pltpu.make_async_copy(gout.at[g % 2], gx_hbm.at[t, lanes(g)], go_sem.at[g % 2])

    def in_plane(n):
        there = (to_x, to_y, to_core)[n]
        return remote(scur.at[n], srecv.at[n], sc_s.at[n], sc_r.at[n], there)

    def to_plane(off):
        there = ((z + off) % planes, row)
        return remote(stats.at[z], stats.at[z], zs_s.at[off - 1], zs_r.at[off - 1], there)

    def from_plane(off):
        there = ((z + off) % planes, row)
        held = stats.at[(z + planes - off) % planes]
        return remote(held, held, zs_s.at[off - 1], zs_r.at[off - 1], there)

    def start(copies):
        for c in copies:
            c.start()

    def wait_send(copies):
        for c in copies:
            c.wait_send()

    def wait_recv(copies):
        for c in copies:
            c.wait_recv()

    def stage(q, work, sends, *sent):
        @pl.when((q >= SLOTS) & (q < total + SLOTS))
        def _():
            for copies in sent:
                wait_send(copies(q - SLOTS))

        @pl.when((q >= 0) & (q < total))
        def _():
            work(q)
            start(sends(q))

    def turn(p):
        for side, copies in enumerate((w_local(p), w_remote(p))):
            for c, copy in enumerate(copies):
                if side == 0:
                    copy.wait()
                else:
                    copy.wait_recv()

                def one(t, carry):
                    turned = jnp.transpose(raw[side, t, c])
                    wt[side, t, 0, c] = turned[:STEP]
                    wt[side, t, 1, c] = turned[STEP:]
                    return carry

                lax.fori_loop(0, towers, one, 0)

        @pl.when(p + 1 < pairs)
        def _():
            start(w_local(p + 1))

    def forward(q):
        k, i, s = q // per_chunk, q % per_chunk, q % SLOTS
        p, h = k // 2, k % 2

        cot_copy(q).start()

        cut = pl.ds(pl.multiple_of(i * IMAGES, IMAGES), IMAGES)

        @pl.when(k == 0)
        def _():
            x_local(i).wait()
            x_remote(i).wait_recv()
            keep = (1.0 - image_ref[cut, 0:1] * pad_row_ref[...]).astype(BF16)
            valid = image_ref[cut, 64:65]
            for t in range(towers):
                used = xb[0, t, cut] * keep
                xb[0, t, cut] = used
                used = used.astype(F32)
                usq_ref[...] = usq_ref[...] + jnp.sum(used * used * valid, axis=0, keepdims=True)
                xb[1, t, cut] = xb[1, t, cut] * keep

        @pl.when((i == 0) & (h == 0))
        def _():
            turn(p)

        @pl.when((i == 0) & (h == 1))
        def _():
            wait_send(w_remote(p))

            @pl.when(p + 1 < pairs)
            def _():
                start(w_remote(p + 1))

        for t in range(towers):
            out = lax.dot_general(
                wt[0, t, h].reshape(4 * STEP, width),
                xb[0, t, cut],
                (((1,), (1,)), ((), ())),
                preferred_element_type=F32,
            ) + lax.dot_general(
                wt[1, t, h].reshape(4 * STEP, width),
                xb[1, t, cut],
                (((1,), (1,)), ((), ())),
                preferred_element_type=F32,
            )
            out = out.reshape(2, 2, STEP, IMAGES)
            for a in range(2):
                for b in range(2):
                    part[s, a, b, t] = out[a, b]
        for a in range(2):
            p1[s, 0, a] = pack(part[s, a, ox, 0])
            p1[s, 1, a] = pack(part[s, oy, a, 1])

    def reduce(q):
        s = q % SLOTS
        wait_recv(rs1(q))
        p2[s, 0] = pack(part[s, oy, x, 0] + unpack(r1[s, 0, oy]))
        p2[s, 1] = pack(part[s, y, ox, 1] + unpack(r1[s, 1, ox]))
        part[s, y, x, 0] = part[s, y, x, 0] + unpack(r1[s, 0, y])
        part[s, y, x, 1] = part[s, y, x, 1] + unpack(r1[s, 1, x])

    def pointwise(q):
        k, i, s = q // per_chunk, q % per_chunk, q % SLOTS
        wait_recv(rs2(q))
        cot_copy(q).wait()

        @pl.when(q >= SLOTS)
        def _():
            st_copy(q - SLOTS).wait()

        valid = valid_ref[i]
        mix = mix_ref[k]
        bias = [mix[:, t : t + 1] for t in range(2)]
        stitch = [[mix[:, 2 + 2 * a + b : 3 + 2 * a + b] for b in range(2)] for a in range(2)]
        pre = [part[s, y, x, t] + unpack(r2[s, t]) + bias[t] for t in range(2)]
        act = [jnp.maximum(p, 0.0) for p in pre]
        up = [cbuf[s, t].astype(F32) * valid for t in range(2)]
        cut = lanes(q)
        for a in range(2):
            out = stitch[a][0] * act[0] + stitch[a][1] * act[1]
            stbuf[s, a] = out.astype(BF16)
            sq_ref[1] = sq_ref[1] + fold(out * out * valid)
            for b in range(2):
                gs_ref[k, a, b] = gs_ref[k, a, b] + fold(up[a] * act[b])
        for t in range(2):
            sq_ref[0] = sq_ref[0] + fold(pre[t] * pre[t] * valid)
            grad = stitch[0][t] * up[0] + stitch[1][t] * up[1]
            grad = jnp.where(pre[t] > 0, grad, 0.0).astype(BF16)
            gfull[k % 2, t, y, x, core, :, cut] = grad
            gb_ref[k, t] = gb_ref[k, t] + fold(grad.astype(F32))
        st_copy(q).start()

    def spread(q):
        wait_recv(ag1(q))

    def across(q):
        wait_recv(ag2(q))

    def terms(k, n):
        unit = width // 3
        for t, at, wide in (((0, 0, 2 * unit),), ((0, 2 * unit, unit), (1, 0, unit)), ((1, unit, 2 * unit),))[n]:
            value = jnp.dot(
                gfull[k % 2, t].reshape(8 * STEP, images),
                xb[0, t, :, at : at + wide],
                preferred_element_type=F32,
            )
            value = value.astype(BF16).reshape(planes, halves, STEP, wide)
            for d in range(planes):
                for e in range(halves):
                    zo[t, d, e, :, at : at + wide] = value[d, e]

    def chain(k, j):
        if j == planes - 2:

            @pl.when(k > 0)
            def _():
                gw_copy(k - 1).wait()

            def begin(i, carry):
                t, e = i // halves, i % halves
                zfin[t, e] = zo[t, z, e].astype(F32)
                return carry

            lax.fori_loop(0, towers * halves, begin, 0)
        for way in range(2):
            near = z if way == 0 else last - z
            source = (z - 1, row) if way == 0 else (z + 1, row)

            def freed():
                @pl.when(k + 1 < chunks)
                def _():
                    pl.semaphore_signal(
                        z_free.at[way, j - 1], inc=1, device_id=source, device_id_type=MESH
                    )

            def put(n, fill):
                @pl.when(k > 0)
                def _():
                    z_copy(k - 1, n, way).wait_send()

                fill(last - n + z if way == 0 else n - last + z)

                @pl.when(k > 0)
                def _():
                    pl.semaphore_wait(z_free.at[way, n], 1)

                z_copy(k, n, way).start()

            if j < 2:

                @pl.when(near == 0)
                def _():
                    for n in range(2) if j == 0 else range(2, planes - 1):

                        def fill(dest):
                            zsend[way, n] = zo[:, dest]

                        if n <= planes - 2:
                            put(n, fill)

            if 1 <= j <= planes - 2:

                @pl.when((near >= 1) & (near <= j))
                def _():
                    def fill(dest):
                        z_copy(k, j - 1, way).wait_recv()

                        def add(i, carry):
                            t, e = i // halves, i % halves
                            value = zo[t, dest, e].astype(F32) + zrecv[way, j - 1, t, e].astype(F32)
                            zsend[way, j, t, e] = value.astype(BF16)
                            return carry

                        lax.fori_loop(0, towers * halves, add, 0)
                        freed()

                    put(j, fill)

            if j == planes - 1:

                @pl.when(near >= 1)
                def _():
                    z_copy(k, j - 1, way).wait_recv()

                    def more(i, carry):
                        t, e = i // halves, i % halves
                        zfin[t, e] = zfin[t, e] + zrecv[way, j - 1, t, e].astype(F32)
                        return carry

                    lax.fori_loop(0, towers * halves, more, 0)
                    freed()

        if j == planes - 1:
            gw_copy(k).start()

    def prepare(g):
        g_load(g).start()

        @pl.when((g >= HELD) & (g - HELD < (pairs - 1) * tiles))
        def _():
            acc_out(g - HELD).wait()

        @pl.when(g >= tiles)
        def _():
            acc_in(g).start()

    def tile(g):
        g_load(g).wait()

        @pl.when(g % per_chunk == 0)
        def _():
            for c in wg_load(g):
                c.wait()

        value = jnp.dot(
            wgx[...], gtile[g % HELD].reshape(16 * STEP, IMAGES), preferred_element_type=F32
        )
        final = g >= (pairs - 1) * tiles

        @pl.when(g < tiles)
        def _():
            acc[g % HELD] = value

        @pl.when(g >= tiles)
        def _():
            acc_in(g).wait()
            acc[g % HELD] = acc[g % HELD] + value

        @pl.when(jnp.logical_not(final))
        def _():
            acc_out(g).start()

        @pl.when(final)
        def _():
            @pl.when(g >= (pairs - 1) * tiles + 2)
            def _():
                gx_out(g - 2).wait()

            keep = (1.0 - image_ref[lanes(g), 0:1] * pad_row_ref[...]).astype(BF16)
            gout[g % 2] = jnp.transpose(acc[g % HELD].astype(BF16)) * keep
            gx_out(g).start()

        @pl.when(((g + 1) % per_chunk == 0) & (g + 1 < pairs * tiles))
        def _():
            start(wg_load(g + 1))

        @pl.when(g + 2 < pairs * tiles)
        def _():
            prepare(g + 2)

    def sums(n):
        if n == 0:
            scur[0] = jnp.zeros_like(scur[0])
            scur[0, 0:1] = fold(usq_ref[...])
            scur[0, 1:2] = jnp.sum(sq_ref[0], axis=0, keepdims=True)
            scur[0, 2:3] = jnp.sum(sq_ref[1], axis=0, keepdims=True)
            scur[0, 3:4] = fold(sum(valid_ref[i] for i in range(per_chunk)))
            for k in range(chunks):
                at = k * 6 * STEP
                stats[z, :, at : at + 2 * STEP] = lane_sums(gb_ref[k].reshape(2 * STEP, 128))
                stats[z, :, at + 2 * STEP : at + 6 * STEP] = lane_sums(gs_ref[k].reshape(4 * STEP, 128))
        else:
            in_plane(n - 1).wait()
            value = scur[n - 1] + srecv[n - 1]
            if n < 3:
                scur[n] = value
            else:
                stats[z, :, chunks * 6 * STEP :] = value
        if n < 3:
            in_plane(n).start()
        else:
            for off in range(1, planes):
                to_plane(off).start()

    start(w_local(0))
    for i in range(per_chunk):
        x_local(i).start()
    for i in range(per_chunk):
        cut = slice(i * IMAGES, (i + 1) * IMAGES)
        valid = valid_in[:, cut].astype(F32)
        small = jnp.where(class_in[:, cut] == 195, 1.0, 0.0)
        valid_ref[i] = valid
        both = jnp.concatenate(
            [jnp.broadcast_to(small, (64, IMAGES)), jnp.broadcast_to(valid, (64, IMAGES))], axis=0
        )
        image_ref[cut] = jnp.transpose(both)
    mix = jnp.concatenate(
        [bias_in[...], stitch_in[0], stitch_in[1], jnp.zeros((122, mine), F32)], axis=0
    )
    mix_ref[...] = jnp.transpose(mix).reshape(chunks, STEP, 128)
    pl.semaphore_wait(barrier, 2 + planes)
    x_remote(0).start()
    start(w_remote(0))

    def send_x(i, carry):
        x_remote(i).start()
        return carry

    lax.fori_loop(1, per_chunk, send_x, 0)
    gb_ref[...] = jnp.zeros_like(gb_ref)
    gs_ref[...] = jnp.zeros_like(gs_ref)
    sq_ref[...] = jnp.zeros_like(sq_ref)
    usq_ref[...] = jnp.zeros_like(usq_ref)

    ready = per_chunk - 1 + 5
    offsets = [2 + 3 * j for j in range(planes)]
    ends = [2 + 11 * j - j // 3 for j in range(planes)]
    first = per_chunk + 3
    late = (chunks - 1) * per_chunk + 3

    def body(s, carry):
        stage(s, forward, rs1, rs1)
        stage(s - 1, reduce, rs2, rs2)
        stage(s - 2, pointwise, ag1, ag1)
        stage(s - 3, spread, ag2, ag2)
        stage(s - 4, across, cx, cx)

        @pl.when((s >= 5) & (s < total + 5))
        def _():
            wait_recv(cx(s - 5))

        for n in range(4):

            @pl.when(s == total + 2 + n)
            def _():
                sums(n)

        @pl.when(s >= ready)
        def _():
            done = s - ready
            k = done // per_chunk
            at = done % per_chunk

            def step(j):
                since = done - offsets[j]
                usual = (since >= 0) & (since % per_chunk == 0) & (since // per_chunk < chunks - 1)
                final = done == (chunks - 1) * per_chunk + ends[j]

                @pl.when(usual | final)
                def _():
                    chain(jnp.where(final, chunks - 1, since // per_chunk), j)

            for j in range(1, planes):
                step(j)
            for n in range(3):

                @pl.when((at == n) & (k < chunks))
                def _():
                    if n == 0:
                        g_copy(k).start()
                    terms(k, n)
                    if n == 2:
                        g_copy(k).wait()

            step(0)
            @pl.when(done == first - 1)
            def _():
                start(wg_load(0))
                prepare(0)
                prepare(1)

            since = done - first
            usual = (since >= 0) & (since % per_chunk < 5) & (since // per_chunk < chunks - 2)
            g = jnp.where(
                done >= late,
                done - late + EACH * (chunks - 2),
                EACH * (since // per_chunk) + since % per_chunk,
            )

            @pl.when(usual | ((done >= late) & (g < pairs * tiles)))
            def _():
                tile(g)

            @pl.when(usual & (since % per_chunk == 4))
            def _():
                tile(g + 1)

        return carry

    left = pairs * tiles - EACH * (chunks - 2)
    lax.fori_loop(0, ready + max((chunks - 1) * per_chunk + ends[-1], late + left - 1) + 1, body, 0)

    def drain(q, carry):
        st_copy(q).wait()
        return carry

    lax.fori_loop(total - SLOTS, total, drain, 0)

    def drain_x(i, carry):
        x_remote(i).wait_send()
        return carry

    lax.fori_loop(0, per_chunk, drain_x, 0)
    for g in (pairs * tiles - 2, pairs * tiles - 1):
        gx_out(g).wait()
    gw_copy(chunks - 1).wait()
    for way in range(2):
        near = z if way == 0 else last - z
        for j in range(planes - 1):

            @pl.when(near <= j)
            def _():
                z_copy(chunks - 1, j, way).wait_send()

    for off in range(1, planes):
        to_plane(off).wait_send()
        from_plane(off).wait_recv()
    every = sum(stats[d] for d in range(planes))
    for k in range(chunks):
        for n in range(6):
            at = (k * 6 + n) * STEP
            value = every[0:1, at : at + STEP]
            if n < 2:
                bias_out[n : n + 1, k * STEP : (k + 1) * STEP] = value
            else:
                stitch_out[(n - 2) // 2, n % 2 : n % 2 + 1, k * STEP : (k + 1) * STEP] = value
    ends = jnp.sum(every[:, chunks * 6 * STEP :], axis=1, keepdims=True)
    images_in = ends[3:4] / lax.axis_size("rows")
    for n, size in enumerate((F, C, C)):
        rms_out[n : n + 1] = jnp.broadcast_to(jnp.sqrt(ends[n : n + 1] / (images_in * 2 * size)), (1, 128))


def put_out(st_ref, gx_ref, gw_ref, st_out, gx_out, gw_out):
    st_out[...] = st_ref[...]
    gx_out[...] = gx_ref[...]
    gw_out[0] = jnp.transpose(gw_ref[0])


def results(stitched, grad_inputs, grad_weights):
    towers, width = grad_weights.shape[0], grad_weights.shape[2]
    mine = grad_weights.shape[1]
    block = min(mine, 512)
    each = mine // block
    steps = towers * each
    flat = [v.reshape(-1, v.shape[-1]) for v in (stitched, grad_inputs)]
    plain = [pl.BlockSpec((v.shape[0] // steps, v.shape[1]), lambda i: (i, 0)) for v in flat]
    out = pl.pallas_call(
        put_out,
        grid=(steps,),
        out_shape=(
            *(jax.ShapeDtypeStruct(v.shape, v.dtype) for v in flat),
            jax.ShapeDtypeStruct((towers, width, mine), F32),
        ),
        in_specs=[*plain, pl.BlockSpec((1, block, width), lambda i: (i // each, i % each, 0))],
        out_specs=[*plain, pl.BlockSpec((1, width, block), lambda i: (i // each, 0, i % each))],
        name="results",
    )(*flat, grad_weights)
    return out[0].reshape(stitched.shape), out[1].reshape(grad_inputs.shape), out[2]


def fused(inputs, weights, bias, stitch, cotangent, valid, size_class):
    planes = lax.axis_size("dp")
    towers, images, width = inputs.shape
    mine = bias.shape[1]
    chunks = mine // STEP
    per_chunk = images // IMAGES
    halves = 8 // planes
    tiles = towers * per_chunk
    place = np.arange(width) % 36
    padded = ((place // 6 == 5) | (place % 6 == 5)).astype(np.float32)
    many = chunks * 6 * STEP + 128
    vmem = pl.BlockSpec(memory_space=pltpu.VMEM)
    hbm = pl.BlockSpec(memory_space=pl.ANY)
    dma = pltpu.SemaphoreType.DMA
    stitched, grad_inputs, grad_weights, grad_bias, grad_stitch, means, _, _ = pl.pallas_call(
        functools.partial(kernel, planes),
        out_shape=(
            jax.ShapeDtypeStruct((2, chunks, STEP, images), BF16),
            jax.ShapeDtypeStruct((towers, images, width), BF16),
            jax.ShapeDtypeStruct((2, halves, chunks, STEP, width), F32),
            jax.ShapeDtypeStruct((2, mine), F32),
            jax.ShapeDtypeStruct((2, 2, mine), F32),
            jax.ShapeDtypeStruct((8, 128), F32),
            jax.ShapeDtypeStruct((2, 2, 2, 2, chunks, STEP, images), BF16),
            jax.ShapeDtypeStruct((tiles, width, IMAGES), F32),
        ),
        in_specs=[hbm] * 3 + [vmem] * 5,
        out_specs=(hbm, hbm, hbm, vmem, vmem, vmem, hbm, hbm),
        scratch_shapes=[
            pltpu.VMEM((images, 128), F32),
            pltpu.VMEM((per_chunk, 1, IMAGES), F32),
            pltpu.VMEM((chunks, STEP, 128), F32),
            pltpu.VMEM((2, towers, images, width), BF16),
            pltpu.VMEM((2, towers, 4, width, 2 * STEP), BF16),
            pltpu.VMEM((2, towers, 2, 4, STEP, width), BF16),
            pltpu.VMEM((SLOTS, 2, 2, towers, STEP, IMAGES), F32),
            pltpu.VMEM((SLOTS, 2, 2, WORDS, IMAGES), jnp.int32),
            pltpu.VMEM((SLOTS, 2, WORDS, IMAGES), jnp.int32),
            pltpu.VMEM((SLOTS, 2, 2, WORDS, IMAGES), jnp.int32),
            pltpu.VMEM((SLOTS, 2, WORDS, IMAGES), jnp.int32),
            pltpu.VMEM((2, towers, 2, 2, 2, STEP, images), BF16),
            pltpu.VMEM((SLOTS, 2, STEP, IMAGES), BF16),
            pltpu.VMEM((SLOTS, 2, STEP, IMAGES), BF16),
            pltpu.VMEM((towers, planes, halves, STEP, width), BF16),
            pltpu.VMEM((2, planes - 1, towers, halves, STEP, width), BF16),
            pltpu.VMEM((2, planes - 1, towers, halves, STEP, width), BF16),
            pltpu.VMEM((towers, halves, STEP, width), F32),
            pltpu.VMEM((chunks, 2, STEP, 128), F32),
            pltpu.VMEM((chunks, 2, 2, STEP, 128), F32),
            pltpu.VMEM((2, STEP, 128), F32),
            pltpu.VMEM((1, width), F32),
            pltpu.VMEM((width, 16 * STEP), BF16),
            pltpu.VMEM((HELD, 2, 2, 2, 2, STEP, IMAGES), BF16),
            pltpu.VMEM((HELD, width, IMAGES), F32),
            pltpu.VMEM((2, IMAGES, width), BF16),
            pltpu.VMEM((3, 8, 128), F32),
            pltpu.VMEM((3, 8, 128), F32),
            pltpu.VMEM((planes, 8, many), F32),
            dma((per_chunk,)),
            dma((per_chunk,)),
            dma((per_chunk,)),
            dma((4,)),
            dma((4,)),
            dma((4,)),
            dma((SLOTS, 2)),
            dma((SLOTS, 2)),
            dma((SLOTS, 2)),
            dma((SLOTS, 2)),
            dma((SLOTS, 2)),
            dma((SLOTS, 2)),
            dma((SLOTS, 2)),
            dma((SLOTS, 2)),
            dma((SLOTS,)),
            dma((SLOTS,)),
            dma((SLOTS,)),
            dma((SLOTS,)),
            dma((2,)),
            dma((2, planes - 1)),
            dma((2, planes - 1)),
            dma,
            pltpu.SemaphoreType.REGULAR((2, planes - 1)),
            dma((8,)),
            dma((HELD,)),
            dma((HELD,)),
            dma((HELD,)),
            dma((2,)),
            dma((3,)),
            dma((3,)),
            dma((planes - 1,)),
            dma((planes - 1,)),
        ],
        compiler_params=pltpu.CompilerParams(
            collective_id=0, has_side_effects=True, vmem_limit_bytes=67043328
        ),
        name="towers",
    )(
        inputs,
        weights,
        cotangent.reshape(2, chunks, STEP, images),
        valid[None, :],
        size_class[None, :],
        padded[None, :],
        bias,
        stitch,
    )
    stitched, grad_inputs, grad_weights = results(
        stitched.reshape(2, mine, images), grad_inputs, grad_weights.reshape(towers, -1, width)
    )
    return (stitched, grad_inputs, grad_weights, grad_bias, grad_stitch, means[:3, 0])


def rms(totals):
    count = totals[3] / lax.axis_size("rows")
    return jnp.sqrt(
        jnp.stack(
            [totals[0] / (count * 2 * F), totals[1] / (count * 2 * C), totals[2] / (count * 2 * C)]
        )
    )


def line_sum(own, up):
    size = lax.axis_size("dp")
    here = lax.axis_index("dp")
    got = None
    for step in range(size - 1):
        dest = size - 1 - step + here if up else step - (size - 1) + here
        dest = jnp.clip(dest, 0, size - 1)
        term = lax.dynamic_index_in_dim(own, dest, 0, keepdims=False)
        if got is not None:
            term = (term.astype(jnp.float32) + got.astype(jnp.float32)).astype(jnp.bfloat16)
        pairs = [(z, z + 1) for z in range(step + 1)]
        if not up:
            pairs = [(size - 1 - a, size - 1 - b) for a, b in pairs]
        got = lax.ppermute(term, "dp", pairs)
    return got


def plain(inputs, weights, bias, stitch, cotangent, valid, size_class):
    rows = lax.axis_size("rows")
    size = lax.axis_size("dp")
    here = lax.axis_index("dp")
    width = inputs.shape[2]
    mine = bias.shape[1]
    step = min(BLOCK, mine)
    blocks = mine // step
    place = lax.iota(jnp.int32, width) % 36
    padded = (place // 6 == 5) | (place % 6 == 5)
    dropped = (size_class == 195)[:, None] & padded[None, :]
    used = jnp.where(dropped[None], jnp.zeros((), jnp.bfloat16), inputs)
    split = weights.reshape(2, width, rows, mine)
    weight_valid = valid.astype(jnp.float32)
    pieces, stitched, grad_bias, grad_stitch, square_pre, square_out = [], [], [], [], [], []
    grad_weights = []
    mats = [split[:, :, :, k * step : (k + 1) * step] for k in range(blocks)]
    sums = []
    for k in range(blocks):
        part = jnp.einsum("tfrc,tbf->rctb", mats[k], used, preferred_element_type=jnp.float32)
        sums.append(
            lax.psum_scatter(part.reshape(rows * step, 2, -1), "rows", scatter_dimension=0, tiled=True)
        )
    for k in range(blocks):
        cut = slice(k * step, (k + 1) * step)
        pre = jnp.transpose(sums[k], (1, 0, 2)) + bias[:, cut, None]
        act = jax.nn.relu(pre)
        mix = stitch[:, :, cut, None]
        out = jnp.sum(mix * act[None], axis=1)
        stitched.append(out.astype(jnp.bfloat16))
        upstream = cotangent[:, cut].astype(jnp.float32) * weight_valid[None, None, :]
        grad_act = jnp.sum(mix * upstream[:, None], axis=0)
        grad_pre = jnp.where(pre > 0, grad_act, 0.0).astype(jnp.bfloat16)
        grad_bias.append(jnp.sum(grad_pre.astype(jnp.float32), axis=2))
        grad_stitch.append(jnp.sum(upstream[:, None] * act[None], axis=3))
        square_pre.append(jnp.sum(weight_valid[None, None, :] * pre * pre))
        square_out.append(jnp.sum(weight_valid[None, None, :] * out * out))
        piece = lax.all_gather(grad_pre, "rows", axis=0)
        pieces.append(piece)
        block = jnp.einsum("tbf,rtcb->rtfc", used, piece, preferred_element_type=jnp.float32)
        block = block.reshape(size, rows // size, 2, width, step)
        own = block.astype(jnp.bfloat16)
        total = lax.dynamic_index_in_dim(block, here, 0, keepdims=False)
        total = total + line_sum(own, True).astype(jnp.float32) + line_sum(own, False).astype(jnp.float32)
        grad_weights.append(total)
    total_x = sum(
        jnp.einsum("rtcb,tfrc->tbf", pieces[k], mats[k], preferred_element_type=jnp.float32)
        for k in range(blocks)
    )
    grad_inputs = jnp.where(dropped[None], 0.0, total_x).astype(jnp.bfloat16)
    grad_weights = jnp.stack(grad_weights, axis=0)
    grad_weights = jnp.transpose(grad_weights, (2, 3, 1, 0, 4)).reshape(2, width, -1)
    stitched = jnp.concatenate(stitched, axis=1)
    grad_bias = jnp.concatenate(grad_bias, axis=1)
    grad_stitch = jnp.concatenate(grad_stitch, axis=2)
    used_wide = used.astype(jnp.float32)
    partial_value = jnp.stack(
        [
            jnp.sum(weight_valid[None, :, None] * used_wide * used_wide),
            sum(square_pre),
            sum(square_out),
            jnp.sum(weight_valid),
        ]
    )
    grad_bias, grad_stitch = lax.psum((grad_bias, grad_stitch), "dp")
    totals = lax.psum(partial_value, ("dp", "rows"))
    return (stitched, grad_inputs, grad_weights, grad_bias, grad_stitch, rms(totals))


def small_plane(mesh):
    return mesh.shape["rows"] == 8 and mesh.shape["dp"] in (2, 4, 8)


def solution(mesh):
    in_specs = (
        P(None, "dp", "rows"),
        P(None, "rows", None),
        P(None, "rows"),
        P(None, None, "rows"),
        P(None, "rows", "dp"),
        P("dp"),
        P("dp"),
    )
    out_specs = (
        P(None, "rows", "dp"),
        P(None, "dp", "rows"),
        P(None, "rows", "dp"),
        P(None, "rows"),
        P(None, None, "rows"),
        P(),
    )
    return jax.shard_map(
        fused if small_plane(mesh) else plain, mesh=mesh, in_specs=in_specs, out_specs=out_specs, check_vma=False
    )
```
